256 devices in a mesh: req: 16 (over z_hi, y, core), tp: 16 (over z_lo, x).
Axes of the slice: x: 4, y: 4, z: 8 (z_hi: 2, z_lo: 4; z = z_hi * 4 + z_lo), core: 2. Of those that a mesh axis runs over, the one named last changes fastest.
Arguments:
- queries: bfloat16 [64, 32, 4096], P('req'), may hold values from -128 to 128
- cache_keys: bfloat16 [64, 4096, 512], P('req', 'tp'), may hold values from -4 to 4
- cache_values: bfloat16 [64, 4096, 512], P('req', 'tp'), may hold values from -5 to 5
- tree_keys: bfloat16 [64, 32, 512], P('req', 'tp'), may hold values from -5 to 5
- tree_values: bfloat16 [64, 32, 512], P('req', 'tp'), may hold values from -5 to 5
- parents: int32 [64, 32], P('req'), may hold values from -1 to 30, as said below
- lengths: int32 [64], P('req'), may hold values from 2 to 4096
- accepted_leaf: int32 [64], P('req'), may hold values from 0 to 31
- residual: bfloat16 [64, 32, 8192], P('req', None, 'tp'), may hold values from -12 to 12
- norm_gain: float32 [8192], replicated, may hold values from 0.5 to 4
- out_weight: bfloat16 [4096, 8192], P('tp'), may hold values from -0.09375 to 0.09375
- prev_feature: bfloat16 [64, 8192], P('req'), may hold values from -5 to 5
- draft_weight: bfloat16 [8192, 8192], P('req', 'tp'), may hold values from -0.0625 to 0.0625
- first_moment: float32 [8192, 8192], P('req', 'tp'), may hold values from -5 to 5
- second_moment: float32 [8192, 8192], P('req', 'tp'), may hold values from 0.25 to 4
Outputs:
- features: bfloat16 [64, 32, 8192], P('req', None, 'tp')
- new_weight: bfloat16 [8192, 8192], P('req', 'tp')
- new_first: float32 [8192, 8192], P('req', 'tp')
- new_second: float32 [8192, 8192], P('req', 'tp')
- draft_loss: float32 [], replicated
The draws below stay inside these ranges and needn't reach their ends.
Inputs may be any that keep to these rules, and one draw needn't show every extreme that they name: parents[r, 0] = -1; for i of 1 or more, parents[r, i] lies in 0 to i - 1; node 31 is a child of node 30.
All inputs are finite; a program needn't handle non-finite values.
Results may differ from the reference program's by a relative error of at most 0.014.
Values may be sent and summed in bfloat16 or wider, within the bound.
No kernel may reach another device: no remote copies, remote signals or barrier semaphores. Data moves between devices by JAX's collectives and lax.ppermute only.
A program may use at most 128 MiB of HBM per device.

```python
import math
import jax
import jax.numpy as jnp
from jax import lax

D = 8192
HEADS = 32
KV_HEADS = 4
HEAD = 128
NODES = 32
CACHE = 4096
REQS = 64
N_TP = 16


def anchor_keys(key):
    return jnp.clip(jax.random.normal(jax.random.fold_in(key, 7001), (REQS, KV_HEADS * HEAD), jnp.float32), -4.0, 4.0)


def draw_queries(key, part):
    groups = HEADS // KV_HEADS
    normal_part = 2.5 * jnp.clip(jax.random.normal(jax.random.fold_in(key, 1), (REQS, NODES, KV_HEADS, groups, HEAD), jnp.float32), -4.0, 4.0)
    normal_part = jnp.clip(normal_part, -128.0, 128.0)
    return normal_part.reshape(REQS, NODES, HEADS * HEAD).astype(jnp.bfloat16)


def draw_cache_keys(key, part):
    normal_part = jnp.clip(jax.random.normal(jax.random.fold_in(key, 11), (REQS, CACHE, KV_HEADS * HEAD), jnp.float32), -4.0, 4.0)
    anchor = anchor_keys(key)
    second = normal_part[:, 1, :]
    normal_part = normal_part.at[:, 0, :].set(anchor).at[:, 1, :].set(second)
    return normal_part.astype(jnp.bfloat16)


def draw_residual(key, part):
    column = jnp.arange(D, dtype=jnp.float32) / D
    column_power = 0.5 * column + 0.5 * jax.random.uniform(jax.random.fold_in(key, 21), (D,), jnp.float32)
    row_power = jax.random.uniform(jax.random.fold_in(key, 22), (REQS, NODES, 1), jnp.float32)
    scales = 0.03 * jnp.exp(math.log(10.0) * (column_power[None, None, :] + row_power))
    jitter = jnp.clip(jax.random.normal(jax.random.fold_in(key, 23), (REQS, NODES, D), jnp.float32), -4.0, 4.0)
    return (scales * jitter).astype(jnp.bfloat16)


def draw_parents(key, part):
    node_ids = jnp.arange(NODES, dtype=jnp.int32)
    upper_bound = jnp.maximum(node_ids, 1)
    picked = jax.random.randint(jax.random.fold_in(key, 31), (REQS, NODES), 0, upper_bound[None, :], dtype=jnp.int32)
    picked = jnp.where(node_ids[None, :] == NODES - 1, NODES - 2, picked)
    return jnp.where(node_ids[None, :] == 0, -1, picked).astype(jnp.int32)


def draw_lengths(key, part):
    request_ids = jnp.arange(REQS, dtype=jnp.int32)
    low_end = 2 + (CACHE - 2) * request_ids // REQS
    high_end = 2 + (CACHE - 2) * (request_ids + 1) // REQS
    picked = jax.random.randint(jax.random.fold_in(key, 41), (REQS,), low_end, high_end + 1, dtype=jnp.int32)
    picked = jnp.where(request_ids == 0, 2, picked)
    picked = jnp.where(request_ids == REQS - 1, CACHE, picked)
    return picked.astype(jnp.int32)


def draw_norm_gain(key, part):
    column = jnp.arange(D, dtype=jnp.float32) / D
    base = jnp.exp(0.5 * math.log(3.0) * column)
    jitter = jax.random.uniform(jax.random.fold_in(key, 52), (D,), jnp.float32, minval=0.7, maxval=1.3)
    return base * jitter


def place_ends(values, stream_key, least, largest):
    place = [jax.random.randint(jax.random.fold_in(stream_key, axis), (), 0, length) for axis, length in enumerate(values.shape)]
    main_axis = values.shape.index(max(values.shape))
    next_to = place[:main_axis] + [(place[main_axis] + 1) % values.shape[main_axis]] + place[main_axis + 1:]
    return values.at[tuple(place)].set(least).at[tuple(next_to)].set(largest)


def shard_levels(stream_key, dims, cuts, low, high):
    def one(axis_at, blocks):
        steps = jax.random.uniform(jax.random.fold_in(jax.random.fold_in(stream_key, 6), axis_at), (blocks,), jnp.float32, low / len(cuts), high / len(cuts))
        return jnp.repeat(jnp.exp(steps), dims[axis_at] // blocks).reshape((-1,) + (1,) * (len(dims) - axis_at - 1))

    loudness = one(*cuts[0])
    for cut in cuts[1:]:
        loudness = loudness * one(*cut)
    return loudness


def centred(key, dims, spread, most, split=(), kind=jnp.bfloat16):
    drawn = spread * jax.random.normal(key, dims, jnp.float32)
    if split:
        drawn = drawn * shard_levels(key, dims, split, -0.22, 0.18)
    return jnp.clip(drawn, -most, most).astype(kind)


def setup_inputs(seed: int = 0) -> dict:
    streams_of = jax.random.split(jax.random.key(seed), 16)
    queries = draw_queries(jax.random.fold_in(streams_of[15], 71), 0)
    cache_keys = draw_cache_keys(jax.random.fold_in(streams_of[15], 71), 0)
    cache_values = centred(streams_of[2], (REQS, CACHE, KV_HEADS * HEAD), 1.0, 5.0, ((0, 16), (1, 16)))
    tree_keys = centred(streams_of[3], (REQS, NODES, KV_HEADS * HEAD), 1.0, 5.0, ((0, 16), (1, 16)))
    tree_values = centred(streams_of[4], (REQS, NODES, KV_HEADS * HEAD), 1.0, 5.0, ((0, 16), (1, 16)))
    parents = draw_parents(jax.random.fold_in(streams_of[15], 71), 0)
    lengths = draw_lengths(jax.random.fold_in(streams_of[15], 71), 0)
    accepted_leaf = place_ends(jax.random.randint(streams_of[7], (REQS,), 0, NODES), jax.random.fold_in(streams_of[7], 1), 0, NODES - 1).astype(jnp.int32)
    residual = draw_residual(jax.random.fold_in(streams_of[15], 71), 0)
    norm_gain = draw_norm_gain(jax.random.fold_in(streams_of[15], 71), 0)
    out_weight = centred(streams_of[10], (HEADS * HEAD, D), (HEADS * HEAD) ** -0.5, 0.09375, ((0, 16),))
    prev_feature = centred(streams_of[11], (REQS, D), 1.0, 5.0, ((0, 16),))
    draft_weight = centred(streams_of[12], (D, D), D ** -0.5, 0.0625, ((0, 16), (1, 16)))
    first_moment = centred(streams_of[13], (D, D), 1.0, 5.0, ((0, 16), (1, 16)), jnp.float32)
    second_moment = jnp.clip(jnp.exp(math.log(4.0) - 2.7725887 * jax.random.uniform(streams_of[14], (D, D), jnp.float32) ** shard_levels(streams_of[14], (D, D), ((0, 16), (1, 16)), -0.2, 0.2)), 0.25, 4.0)
    return {"queries": queries, "cache_keys": cache_keys, "cache_values": cache_values, "tree_keys": tree_keys, "tree_values": tree_values, "parents": parents, "lengths": lengths, "accepted_leaf": accepted_leaf, "residual": residual, "norm_gain": norm_gain, "out_weight": out_weight, "prev_feature": prev_feature, "draft_weight": draft_weight, "first_moment": first_moment, "second_moment": second_moment}


NEG_FILL = -1e+30
NORM_EPSILON = 1e-06
BETA_ONE = 0.9
BETA_TWO = 0.95
CORRECT_ONE = 1.0 - 0.9 ** 10
CORRECT_TWO = 1.0 - 0.95 ** 10
LEARN_RATE = 0.001

def ancestors(parents):
    node_count = parents.shape[-1]
    onehot = (parents[:, :, None] == jnp.arange(node_count, dtype=jnp.int32)[None, None, :]).astype(jnp.float32)
    reach_map = jnp.eye(node_count, dtype=jnp.float32)[None] + onehot
    for repeat in range(node_count.bit_length()):
        reach_map = jnp.minimum(jnp.einsum('rij,rjk->rik', reach_map, reach_map, precision=lax.Precision.HIGHEST), 1.0)
    return reach_map

def attend_one(operands):
    query_rows, cache_keys, cache_values, tree_keys, tree_values, length, visible = operands
    groups = HEADS // KV_HEADS
    score_scale = 1.0 / math.sqrt(HEAD)
    query_view = query_rows.astype(jnp.float32).reshape(NODES, KV_HEADS, groups, HEAD)
    cache_kview = cache_keys.astype(jnp.float32).reshape(CACHE, KV_HEADS, HEAD)
    cache_vview = cache_values.astype(jnp.float32).reshape(CACHE, KV_HEADS, HEAD)
    tree_kview = tree_keys.astype(jnp.float32).reshape(NODES, KV_HEADS, HEAD)
    tree_vview = tree_values.astype(jnp.float32).reshape(NODES, KV_HEADS, HEAD)
    cache_scores = jnp.einsum('nkgd,ckd->kgnc', query_view, cache_kview) * score_scale
    tree_scores = jnp.einsum('nkgd,jkd->kgnj', query_view, tree_kview) * score_scale
    cache_live = (jnp.arange(CACHE, dtype=jnp.int32) < length)[None, None, None, :]
    tree_live = (visible > 0.5)[None, None, :, :]
    cache_scores = jnp.where(cache_live, cache_scores, NEG_FILL)
    tree_scores = jnp.where(tree_live, tree_scores, NEG_FILL)
    row_top = jnp.maximum(lax.optimization_barrier(jnp.max(cache_scores, axis=-1)), lax.optimization_barrier(jnp.max(tree_scores, axis=-1)))
    cache_probs = jnp.where(cache_live, jnp.exp(cache_scores - row_top[..., None]), 0.0).astype(jnp.bfloat16)
    tree_probs = jnp.where(tree_live, jnp.exp(tree_scores - row_top[..., None]), 0.0).astype(jnp.bfloat16)
    totals = lax.optimization_barrier(jnp.sum(cache_probs.astype(jnp.float32), axis=-1)) + lax.optimization_barrier(jnp.sum(tree_probs.astype(jnp.float32), axis=-1))
    weighted = jnp.einsum('kgnc,ckd->nkgd', cache_probs.astype(jnp.float32), cache_vview)
    weighted = weighted + jnp.einsum('kgnj,jkd->nkgd', tree_probs.astype(jnp.float32), tree_vview)
    attended = (weighted / jnp.transpose(totals, (2, 0, 1))[..., None]).astype(jnp.bfloat16)
    return attended.reshape(NODES, HEADS * HEAD)

def reference(queries, cache_keys, cache_values, tree_keys, tree_values, parents, lengths, accepted_leaf, residual, norm_gain, out_weight, prev_feature, draft_weight, first_moment, second_moment):
    reach_map = ancestors(parents)
    attended = lax.map(attend_one, (queries, cache_keys, cache_values, tree_keys, tree_values, lengths, reach_map))
    row_count = REQS * NODES
    attended = attended.reshape(row_count, HEADS * HEAD)
    head_width = HEADS * HEAD // N_TP
    attn_parts = jnp.transpose(attended.reshape(row_count, N_TP, head_width), (1, 0, 2))
    weight_parts = out_weight.reshape(N_TP, head_width, D)

    def add_part(running, pair):
        piece_rows, piece_weight = pair
        term = jnp.dot(piece_rows, piece_weight, preferred_element_type=jnp.float32).astype(jnp.bfloat16)
        return (running + lax.optimization_barrier(term).astype(jnp.float32), None)
    projected, unused = lax.scan(add_part, jnp.zeros((row_count, D), jnp.float32), (attn_parts, weight_parts))
    mixed = residual.reshape(row_count, D).astype(jnp.float32) + projected
    mean_sq = lax.optimization_barrier(jnp.mean(mixed * mixed, axis=1, keepdims=True))
    features = (mixed * lax.rsqrt(mean_sq + NORM_EPSILON) * norm_gain[None, :]).astype(jnp.bfloat16)
    feature_table = jnp.concatenate([prev_feature[:, None, :], features.reshape(REQS, NODES, D)], axis=1)
    inputs = jnp.take_along_axis(feature_table, (parents + 1).astype(jnp.int32)[:, :, None], axis=1).reshape(row_count, D)
    leaf_hot = (accepted_leaf[:, None] == jnp.arange(NODES, dtype=jnp.int32)[None, :]).astype(jnp.float32)
    accepted = jnp.einsum('rn,rnj->rj', leaf_hot, reach_map, precision=lax.Precision.HIGHEST)
    fill_share = 0.5 + lengths.astype(jnp.float32) / CACHE
    weights = ((1.0 + 3.0 * accepted) * fill_share[:, None]).reshape(row_count, 1)
    predicted = jnp.dot(inputs, draft_weight, preferred_element_type=jnp.float32)
    pred_error = predicted - features.astype(jnp.float32)
    scaled_err = (weights * pred_error).astype(jnp.bfloat16)
    gradient = lax.dot_general(inputs, scaled_err, (((0,), (0,)), ((), ())), preferred_element_type=jnp.float32)
    draft_loss = 0.5 * jnp.sum(weights * pred_error * pred_error) / (row_count * D)
    grad_norm = jnp.sqrt(jnp.sum(gradient * gradient)) + 1e-06
    clip_factor = jnp.minimum(1.0, D / grad_norm)
    clipped = gradient * clip_factor
    new_first = BETA_ONE * first_moment + (1.0 - BETA_ONE) * clipped
    new_second = BETA_TWO * second_moment + (1.0 - BETA_TWO) * clipped * clipped
    direction = new_first / CORRECT_ONE / (jnp.sqrt(new_second / CORRECT_TWO) + 1e-08)
    new_weight = (draft_weight.astype(jnp.float32) - LEARN_RATE * direction).astype(jnp.bfloat16)
    return (features.reshape(REQS, NODES, D), new_weight, new_first, new_second, draft_loss)
```

```python
import math

import jax
import jax.numpy as jnp
from jax import lax
from jax.sharding import Mesh
from jax.sharding import PartitionSpec as P

HEADS = 32
KV_HEADS = 4
HEAD = 128
NODES = 32
CACHE = 4096
D = 8192
N_TP = 16
N_REQ = 16

NEG_FILL = -1e30
NORM_EPSILON = 1e-06
BETA_ONE = 0.9
BETA_TWO = 0.95
CORRECT_ONE = 1.0 - 0.9**10
CORRECT_TWO = 1.0 - 0.95**10
LEARN_RATE = 0.001

REQ = ("zh", "y", "c")
TP = ("zl", "x")
F32 = jnp.float32
BF16 = jnp.bfloat16


def exchange(value, axis):
    return lax.all_to_all(value, axis, 0, 0, tiled=True)


def spread(value, axis, count):
    wide = jnp.broadcast_to(value[None], (count, *value.shape))
    return exchange(wide.reshape(count * value.shape[0], *value.shape[1:]), axis)


def gather(value, axis):
    return lax.all_gather(value, axis, axis=0, tiled=True)


def closure(parents):
    onehot = (parents[:, :, None] == jnp.arange(NODES, dtype=jnp.int32)[None, None, :]).astype(BF16)
    reach_map = jnp.eye(NODES, dtype=BF16)[None] + onehot
    for repeat in range((NODES - 1).bit_length()):
        squared = jnp.einsum("rij,rjk->rik", reach_map, reach_map, preferred_element_type=F32)
        reach_map = jnp.minimum(squared, 1.0).astype(BF16)
    return reach_map


def pieces(value):
    high = value.astype(BF16)
    return high, (value - high.astype(F32)).astype(BF16)


def body(
    queries,
    cache_keys,
    cache_values,
    tree_keys,
    tree_values,
    parents,
    lengths,
    accepted_leaf,
    residual,
    norm_gain,
    out_weight,
    prev_feature,
    draft_weight,
    first_moment,
    second_moment,
):
    requests = queries.shape[0]
    rows = requests * NODES
    groups = HEADS // KV_HEADS
    score_scale = 1.0 / math.sqrt(HEAD)
    tp_rank = lax.axis_index(TP)
    cache_span = cache_keys.shape[1]
    tree_span = tree_keys.shape[1]
    block = residual.shape[2]

    all_weight = gather(gather(gather(draft_weight[None], "zh"), "y"), "c")
    all_weight = jnp.transpose(
        all_weight.reshape(2, 4, 2, *draft_weight.shape), (2, 1, 0, 3, 4)
    ).reshape(D, block)

    reach_map = closure(parents)
    query_view = queries.reshape(requests, NODES, KV_HEADS, groups, HEAD)
    cache_view = cache_keys.reshape(requests, cache_span, KV_HEADS, HEAD)
    tree_view = tree_keys.reshape(requests, tree_span, KV_HEADS, HEAD)
    cache_scores = (
        jnp.einsum("rnkgd,rckd->rkgnc", query_view, cache_view, preferred_element_type=F32)
        * score_scale
    )
    tree_scores = (
        jnp.einsum("rnkgd,rjkd->rkgnj", query_view, tree_view, preferred_element_type=F32)
        * score_scale
    )
    positions = tp_rank * cache_span + jnp.arange(cache_span, dtype=jnp.int32)
    cache_live = (positions[None, :] < lengths[:, None])[:, None, None, None, :]
    visible = lax.dynamic_slice_in_dim(reach_map, tp_rank * tree_span, tree_span, 2)
    tree_live = (visible > 0.5)[:, None, None, :, :]
    cache_scores = jnp.where(cache_live, cache_scores, NEG_FILL)
    tree_scores = jnp.where(tree_live, tree_scores, NEG_FILL)
    local_top = jnp.maximum(jnp.max(cache_scores, axis=-1), jnp.max(tree_scores, axis=-1)).astype(BF16)
    shift = local_top.astype(F32)[..., None]
    cache_probs = jnp.where(cache_live, jnp.exp(cache_scores - shift), 0.0).astype(BF16)
    tree_probs = jnp.where(tree_live, jnp.exp(tree_scores - shift), 0.0).astype(BF16)
    totals = jnp.sum(cache_probs, axis=-1, dtype=F32) + jnp.sum(tree_probs, axis=-1, dtype=F32)
    value_view = cache_values.reshape(requests, cache_span, KV_HEADS, HEAD)
    tree_value_view = tree_values.reshape(requests, tree_span, KV_HEADS, HEAD)
    weighted = jnp.einsum("rkgnc,rckd->rkgnd", cache_probs, value_view, preferred_element_type=F32)
    weighted = weighted + jnp.einsum(
        "rkgnj,rjkd->rkgnd", tree_probs, tree_value_view, preferred_element_type=F32
    )
    weighted = weighted.astype(BF16).reshape(requests, N_TP, 2, NODES, HEAD)
    weighted = jnp.transpose(weighted, (1, 0, 3, 2, 4)).reshape(N_TP, rows, 2 * HEAD)
    total_high, total_low = pieces(totals)
    stats = jnp.stack([local_top, total_high, total_low]).reshape(3, requests, N_TP, 2, NODES)
    stats = jnp.transpose(stats, (2, 0, 3, 1, 4)).reshape(N_TP, 3, 2 * rows)
    stats = jnp.pad(stats, ((0, 0), (0, 13), (0, 0)))
    parcel = jnp.concatenate([weighted, stats], axis=1).reshape(N_TP * (rows + 16), 2 * HEAD)
    parcel = exchange(parcel, TP).reshape(N_TP, rows + 16, 2 * HEAD)
    sums = parcel[:, :rows].reshape(N_TP, rows, 2, HEAD).astype(F32)
    stats = parcel[:, rows : rows + 3].astype(F32).reshape(N_TP, 3, 2, rows)
    tops = stats[:, 0]
    factor = jnp.exp(tops - jnp.max(tops, axis=0, keepdims=True))
    share = factor / jnp.sum(factor * (stats[:, 1] + stats[:, 2]), axis=0, keepdims=True)
    share = jnp.transpose(share, (0, 2, 1))[..., None]
    attended = jnp.sum(sums * share, axis=0).astype(BF16).reshape(rows, 2 * HEAD)

    partial_value = jnp.dot(attended, out_weight, preferred_element_type=F32).astype(BF16)
    partial_value = jnp.transpose(partial_value.reshape(rows, 4, 4, block), (2, 1, 0, 3))
    along_x = exchange(partial_value.reshape(16 * rows, block), "x").reshape(4, 4 * rows, block)
    along_x = jnp.sum(along_x.astype(F32), axis=0).astype(BF16)
    along_z = exchange(along_x, "zl").reshape(4, rows, block)
    projected = jnp.sum(along_z.astype(F32), axis=0)
    mixed = residual.reshape(rows, block).astype(F32) + projected

    near = gather(mixed.astype(BF16)[None], "zl")
    far = spread(near, "x", 4).reshape(4, 4, rows, block)
    table = jnp.transpose(far, (1, 0, 2, 3)).reshape(N_TP, rows, block).astype(F32)
    mean_sq = jnp.mean(table * table, axis=(0, 2))[:, None]
    scale = lax.rsqrt(mean_sq + NORM_EPSILON)
    own_gain = lax.dynamic_slice_in_dim(norm_gain, tp_rank * block, block, 0)
    own_features = (mixed * scale * own_gain[None, :]).astype(BF16)
    table = (table * scale[None] * norm_gain.reshape(N_TP, 1, block)).astype(BF16)
    prev = jnp.transpose(prev_feature.reshape(requests, N_TP, block), (1, 0, 2))[:, :, None, :]
    last = (jnp.arange(NODES) == NODES - 1)[None, None, :, None]
    table = jnp.where(last, prev, table.reshape(N_TP, requests, NODES, block))
    table = table.reshape(N_TP, rows, block)
    pick = jnp.where(parents < 0, NODES - 1, parents)
    pick = (pick[:, :, None] == jnp.arange(NODES, dtype=jnp.int32)[None, None, :]).astype(F32)

    columns = exchange(table.reshape(N_TP * rows, block), REQ)

    leaf_hot = (accepted_leaf[:, None] == jnp.arange(NODES, dtype=jnp.int32)[None, :]).astype(BF16)
    accepted = jnp.einsum("rn,rnj->rj", leaf_hot, reach_map, preferred_element_type=F32)
    fill_share = 0.5 + lengths.astype(F32) / CACHE
    weights = ((1.0 + 3.0 * accepted) * fill_share[:, None]).reshape(rows, 1)

    ahead = jnp.dot(
        jnp.transpose(table, (1, 0, 2)).reshape(rows, D), all_weight, preferred_element_type=F32
    )
    predicted = jnp.einsum(
        "rij,rjd->rid", pick, ahead.reshape(requests, NODES, block), precision=lax.Precision.HIGHEST
    ).reshape(rows, block)
    pred_error = predicted - own_features.astype(F32)
    weighted_err = weights * pred_error
    scaled_err = jnp.einsum(
        "rij,rid->rjd",
        pick,
        weighted_err.reshape(requests, NODES, block),
        precision=lax.Precision.HIGHEST,
    ).astype(BF16)
    all_err = gather(scaled_err.reshape(1, rows, block), "zh")
    all_err = spread(spread(all_err, "y", 4), "c", 2)
    all_err = jnp.transpose(all_err.reshape(2, 4, 2, rows, block), (2, 1, 0, 3, 4))
    gradient = lax.dot_general(
        columns,
        all_err.reshape(N_REQ * rows, block),
        (((0,), (0,)), ((), ())),
        preferred_element_type=F32,
    )
    square = jnp.sum(gradient * gradient)
    error = jnp.sum(weighted_err * pred_error)
    lane = jnp.arange(128)[None, :]
    pair = jnp.where(lane == 0, square, jnp.where(lane == 1, error, 0.0))
    pair = jnp.sum(spread(pair, REQ + TP, N_REQ * N_TP), axis=0)
    square_total, error_total = pair[0], pair[1]
    draft_loss = 0.5 * error_total / (rows * N_REQ * D)
    grad_norm = jnp.sqrt(square_total) + 1e-06
    clip_factor = jnp.minimum(1.0, D / grad_norm)
    clipped = gradient * clip_factor
    new_first = BETA_ONE * first_moment + (1.0 - BETA_ONE) * clipped
    new_second = BETA_TWO * second_moment + (1.0 - BETA_TWO) * clipped * clipped
    direction = new_first / CORRECT_ONE / (jnp.sqrt(new_second / CORRECT_TWO) + 1e-08)
    new_weight = (draft_weight.astype(F32) - LEARN_RATE * direction).astype(BF16)
    return (
        own_features.reshape(requests, NODES, block),
        new_weight,
        new_first,
        new_second,
        draft_loss,
    )


def solution(mesh):
    fine = Mesh(mesh.devices.reshape(2, 4, 2, 4, 4), REQ + TP)
    placed = (
        P(REQ, None, None),
        P(REQ, TP, None),
        P(REQ, TP, None),
        P(REQ, TP, None),
        P(REQ, TP, None),
        P(REQ, None),
        P(REQ),
        P(REQ),
        P(REQ, None, TP),
        P(),
        P(TP, None),
        P(REQ, None),
        P(REQ, TP),
        P(REQ, TP),
        P(REQ, TP),
    )
    return jax.shard_map(
        body,
        mesh=fine,
        in_specs=placed,
        out_specs=(P(REQ, None, TP), P(REQ, TP), P(REQ, TP), P(REQ, TP), P()),
        check_vma=False,
    )
```

```python
import math

import jax
import jax.numpy as jnp
from jax import lax
from jax.experimental import pallas as pl
from jax.experimental.pallas import tpu as pltpu
from jax.sharding import Mesh
from jax.sharding import PartitionSpec as P

KV_HEADS = 4
HEAD = 128
NODES = 32
CACHE = 4096
D = 8192
N_TP = 16
N_REQ = 16

NEG_FILL = -1e30
NORM_EPSILON = 1e-06
BETA_ONE = 0.9
BETA_TWO = 0.95
CORRECT_ONE = 1.0 - 0.9**10
CORRECT_TWO = 1.0 - 0.95**10
LEARN_RATE = 0.001

REQ = ("zh", "y", "c")
TP = ("zl", "x")
F32 = jnp.float32
BF16 = jnp.bfloat16


def exchange(value, axis):
    return lax.all_to_all(value, axis, 0, 0, tiled=True)


def spread(value, axis, count):
    wide = jnp.broadcast_to(value[None], (count, *value.shape))
    return exchange(wide.reshape(count * value.shape[0], *value.shape[1:]), axis)


def turn(count, step):
    return [(i, (i + step) % count) for i in range(count)]


def gather(value, axis):
    return lax.all_gather(value, axis, axis=0, tiled=True)


def dot(left, right, dims, **kwargs):
    return lax.dot_general(left, right, (dims, ((), ())), preferred_element_type=F32, **kwargs)


def same_request(width=128):
    row = lax.broadcasted_iota(jnp.int32, (128, width), 0)
    lane = lax.broadcasted_iota(jnp.int32, (128, width), 1)
    return row, lane


def attend_kernel(rank_ref, len_ref, par_ref, q_ref, ck_ref, cv_ref, tk_ref, tv_ref, out_ref, reach_ref, stat_ref):
    rank = rank_ref[0]
    row, lane = same_request()
    base = (row // NODES) * NODES
    up = jnp.where(par_ref[...] + base == lane, jnp.where(par_ref[...] >= 0, 1.0, 0.0), 0.0)
    reach = (jnp.where(row == lane, 1.0, 0.0) + up).astype(BF16)
    for _ in range((NODES - 1).bit_length()):
        reach = jnp.minimum(dot(reach, reach, ((1,), (0,))), 1.0).astype(BF16)
    reach_ref[...] = reach
    pick = jnp.where(row % NODES == 2 * rank + lane, jnp.where(lane < 2, 1.0, 0.0), 0.0)
    visible = dot(reach, pick.astype(BF16), ((1,), (0,)))
    scale = 1.0 / math.sqrt(HEAD)
    span = ck_ref.shape[1]
    slot = lax.broadcasted_iota(jnp.int32, (256, span), 1) + rank * span
    wide_lane = lax.broadcasted_iota(jnp.int32, (NODES, 128), 1)
    for r in range(q_ref.shape[0]):
        live = slot < len_ref[r]
        seen = visible[r * NODES : (r + 1) * NODES, :8]
        seen = jnp.concatenate([seen] * 8, axis=0) > 0.5
        stats = jnp.zeros((NODES, 128), F32)
        for k in range(KV_HEADS):
            head = slice(k * HEAD, (k + 1) * HEAD)
            query = jnp.concatenate(
                [q_ref[r, :, (k * 8 + g) * HEAD : (k * 8 + g + 1) * HEAD] for g in range(8)], axis=0
            )
            scores = dot(query, ck_ref[r, :, head], ((1,), (1,))) * scale
            tree = dot(query, tk_ref[r, :, head], ((1,), (1,))) * scale
            scores = jnp.where(live, scores, NEG_FILL)
            tree = jnp.where(seen, tree, NEG_FILL)
            top = jnp.maximum(
                jnp.max(scores, axis=1, keepdims=True), jnp.max(tree, axis=1, keepdims=True)
            )
            top = top.astype(BF16).astype(F32)
            probs = jnp.where(live, jnp.exp(scores - top), 0.0).astype(BF16)
            tree = jnp.where(seen, jnp.exp(tree - top), 0.0).astype(BF16)
            total = jnp.sum(probs.astype(F32), axis=1, keepdims=True) + jnp.sum(
                tree.astype(F32), axis=1, keepdims=True
            )
            high = total.astype(BF16).astype(F32)
            low = total - high
            value = dot(probs, cv_ref[r, :, head], ((1,), (0,))) + dot(
                tree, tv_ref[r, :, head], ((1,), (0,))
            )
            value = value.astype(BF16)
            for g in range(8):
                h = k * 8 + g
                part = slice(g * NODES, (g + 1) * NODES)
                out_ref[h // 2, r * NODES : (r + 1) * NODES, (h % 2) * HEAD : (h % 2 + 1) * HEAD] = value[part]
                for at, column in enumerate((top, high, low)):
                    stats = jnp.where(wide_lane == h * 4 + at, column[part], stats)
        stat_ref[r * NODES : (r + 1) * NODES, :] = stats
    turned = jnp.transpose(stat_ref[...])
    empty = jnp.zeros((8, 128), F32)
    blank = jnp.zeros((16, 128), BF16)
    for owner in range(N_TP):
        block = jnp.concatenate([turned[owner * 8 : (owner + 1) * 8], empty], axis=0)
        out_ref[owner, 128:144, 0:128] = block.astype(BF16)
        out_ref[owner, 128:144, 128:256] = blank


def project_kernel(parcel_ref, weight_ref, out_ref, att_ref):
    @pl.when(pl.program_id(0) == 0)
    def join():
        stats = jnp.concatenate(
            [parcel_ref[src, 128:144, 0:128].astype(F32)[0:8] for src in range(N_TP)], axis=0
        )
        total = pltpu.roll(stats, 127, 0) + pltpu.roll(stats, 126, 0)
        stats = stats.reshape(N_TP, 8, 128)
        factor = jnp.exp(stats - jnp.max(stats, axis=0, keepdims=True))
        share = factor / jnp.sum(factor * total.reshape(N_TP, 8, 128), axis=0, keepdims=True)
        share = jnp.transpose(share.reshape(128, 128))
        for side in range(2):
            cols = slice(side * HEAD, (side + 1) * HEAD)
            joined = jnp.zeros((128, HEAD), F32)
            for src in range(N_TP):
                at = src * 8 + side * 4
                joined = joined + parcel_ref[src, 0:128, cols].astype(F32) * share[:, at : at + 1]
            att_ref[:, cols] = joined.astype(BF16)

    out_ref[0, 0] = dot(att_ref[...], weight_ref[...], ((1,), (0,))).astype(BF16)


def predict_kernel(
    far_ref, mixed_ref, gain_ref, own_gain_ref, prev_ref, par_ref, scale_w_ref, weight_ref,
    table_ref, own_ref, err_ref, loss_ref, scale_ref, ahead_ref,
):
    p = pl.program_id(0)

    @pl.when(p == 0)
    def start():
        square = jnp.zeros((128, 1), F32)
        for zl in range(4):
            for x in range(4):
                part = far_ref[x, zl].astype(F32)
                square = square + jnp.sum(part * part, axis=1, keepdims=True)
        scale = lax.rsqrt(square / D + NORM_EPSILON)
        scale_ref[...] = jnp.broadcast_to(scale, (128, 128))
        own_ref[...] = (mixed_ref[...] * scale * own_gain_ref[...]).astype(BF16)
        ahead_ref[...] = jnp.zeros_like(ahead_ref)

    block = far_ref[lax.rem(p, 4), p // 4].astype(F32) * scale_ref[:, 0:1] * gain_ref[0]
    node = lax.broadcasted_iota(jnp.int32, (NODES, 1), 0)
    prev = prev_ref[...].astype(F32)
    block = jnp.concatenate(
        [
            jnp.where(node == NODES - 1, prev[r : r + 1], block[r * NODES : (r + 1) * NODES])
            for r in range(4)
        ],
        axis=0,
    ).astype(BF16)
    table_ref[0] = block
    ahead_ref[...] += dot(block, weight_ref[0], ((1,), (0,)))

    @pl.when(p == N_TP - 1)
    def finish():
        row, lane = same_request()
        parent = jnp.where(par_ref[...] < 0, NODES - 1, par_ref[...])
        pick = jnp.where(parent + (row // NODES) * NODES == lane, 1.0, 0.0)
        predicted = dot(pick, ahead_ref[...], ((1,), (0,)), precision=lax.Precision.HIGHEST)
        error = predicted - own_ref[...].astype(F32)
        weighted = scale_w_ref[...] * error
        err_ref[...] = dot(pick, weighted, ((0,), (0,)), precision=lax.Precision.HIGHEST).astype(BF16)
        loss = jnp.sum(jnp.sum(weighted * error, axis=0, keepdims=True), axis=1, keepdims=True)
        loss_ref[...] = jnp.broadcast_to(loss, (8, 128))


def differentiate_kernel(source_ref, column_ref, near_ref, other_ref, loss_ref, grad_ref, pair_ref):
    for part in range(4):
        left = jnp.concatenate([column_ref[source_ref[part * 4 + i]] for i in range(4)], axis=0)
        err_ref = near_ref if part < 2 else other_ref
        right = jnp.concatenate(
            [err_ref[(part % 2) * 2 + i // 2, i % 2] for i in range(4)], axis=0
        )
        term = dot(left, right, ((0,), (0,)))
        if part == 0:
            grad_ref[...] = term
        else:
            grad_ref[...] += term
    value = grad_ref[...]
    square = jnp.sum(jnp.sum(value * value, axis=0, keepdims=True), axis=1, keepdims=True)
    lane = lax.broadcasted_iota(jnp.int32, (8, 128), 1)
    pair = jnp.where(lane == 0, square, jnp.where(lane == 1, loss_ref[...], 0.0))
    for i in range(32):
        pair_ref[i * 8 : (i + 1) * 8] = pair


def in_vmem():
    return pl.BlockSpec(memory_space=pltpu.VMEM)


def in_smem():
    return pl.BlockSpec(memory_space=pltpu.SMEM)


def attend(rank, lengths, parent_column, queries, cache_keys, cache_values, tree_keys, tree_values):
    return pl.pallas_call(
        attend_kernel,
        out_shape=(
            jax.ShapeDtypeStruct((N_TP, 144, 2 * HEAD), BF16),
            jax.ShapeDtypeStruct((128, 128), BF16),
        ),
        in_specs=[in_smem(), in_smem()] + [in_vmem()] * 6,
        out_specs=(in_vmem(), in_vmem()),
        scratch_shapes=[pltpu.VMEM((128, 128), F32)],
        cost_estimate=pl.CostEstimate(
            flops=2 * 2 * 16 * 256 * 256 * 128, bytes_accessed=4 << 20, transcendentals=16 * 256 * 256
        ),
        name="attend",
    )(rank, lengths, parent_column, queries, cache_keys, cache_values, tree_keys, tree_values)


def project(parcel, out_weight):
    return pl.pallas_call(
        project_kernel,
        grid=(N_TP,),
        out_shape=jax.ShapeDtypeStruct((4, 4, 128, 512), BF16),
        in_specs=[
            pl.BlockSpec((N_TP, 144, 2 * HEAD), lambda p: (0, 0, 0)),
            pl.BlockSpec((2 * HEAD, 512), lambda p: (0, p)),
        ],
        out_specs=pl.BlockSpec((1, 1, 128, 512), lambda p: (lax.rem(p, 4), p // 4, 0, 0)),
        scratch_shapes=[pltpu.VMEM((128, 2 * HEAD), BF16)],
        cost_estimate=pl.CostEstimate(
            flops=2 * 128 * 256 * 8192, bytes_accessed=7 << 20, transcendentals=0
        ),
        name="project",
    )(parcel, out_weight)


def differentiate(source, columns, near_err, other_err, loss):
    return pl.pallas_call(
        differentiate_kernel,
        out_shape=(
            jax.ShapeDtypeStruct((512, 512), F32),
            jax.ShapeDtypeStruct((N_REQ * N_TP, 128), F32),
        ),
        in_specs=[in_smem()] + [in_vmem()] * 4,
        out_specs=(in_vmem(), in_vmem()),
        cost_estimate=pl.CostEstimate(
            flops=2 * 2048 * 512 * 512, bytes_accessed=5 << 20, transcendentals=0
        ),
        name="differentiate",
    )(source, columns, near_err, other_err, loss)


def predict(far, mixed, gain, own_gain, prev, parent_column, weights, all_weight):
    return pl.pallas_call(
        predict_kernel,
        grid=(N_TP,),
        out_shape=(
            jax.ShapeDtypeStruct((N_TP, 128, 512), BF16),
            jax.ShapeDtypeStruct((128, 512), BF16),
            jax.ShapeDtypeStruct((128, 512), BF16),
            jax.ShapeDtypeStruct((8, 128), F32),
        ),
        in_specs=[
            pl.BlockSpec((4, 4, 128, 512), lambda p: (0, 0, 0, 0)),
            pl.BlockSpec((128, 512), lambda p: (0, 0)),
            pl.BlockSpec((1, 1, 512), lambda p: (p, 0, 0)),
            pl.BlockSpec((1, 512), lambda p: (0, 0)),
            pl.BlockSpec((4, 512), lambda p: (0, p)),
            pl.BlockSpec((128, 1), lambda p: (0, 0)),
            pl.BlockSpec((128, 1), lambda p: (0, 0)),
            pl.BlockSpec(
                (1, 512, 512),
                lambda p: (lax.rem(p, 2) * 8 + lax.rem(p // 2, 4) * 2 + p // 8, 0, 0),
            ),
        ],
        out_specs=(
            pl.BlockSpec((1, 128, 512), lambda p: (p, 0, 0)),
            pl.BlockSpec((128, 512), lambda p: (0, 0)),
            pl.BlockSpec((128, 512), lambda p: (0, 0)),
            pl.BlockSpec((8, 128), lambda p: (0, 0)),
        ),
        scratch_shapes=[pltpu.VMEM((128, 128), F32), pltpu.VMEM((128, 512), F32)],
        cost_estimate=pl.CostEstimate(
            flops=2 * 128 * 8192 * 512, bytes_accessed=13 << 20, transcendentals=0
        ),
        name="predict",
    )(far, mixed, gain, own_gain, prev, parent_column, weights, all_weight)


def body(
    queries,
    cache_keys,
    cache_values,
    tree_keys,
    tree_values,
    parents,
    lengths,
    accepted_leaf,
    residual,
    norm_gain,
    out_weight,
    prev_feature,
    draft_weight,
    first_moment,
    second_moment,
):
    requests = queries.shape[0]
    rows = requests * NODES
    tp_rank = lax.axis_index(TP)
    block = residual.shape[2]
    parent_column = parents.reshape(rows, 1)

    wide_weight = gather(draft_weight[None], "zh")

    pad = ((0, 0), (0, 6), (0, 0))
    parcel, reach = attend(
        tp_rank.reshape(1),
        lengths,
        parent_column,
        queries,
        cache_keys,
        cache_values,
        jnp.pad(tree_keys, pad),
        jnp.pad(tree_values, pad),
    )
    parcel = exchange(parcel, TP)
    parcel, wide_weight = lax.optimization_barrier((parcel, wide_weight))
    wide_weight = gather(wide_weight, "y")

    leaf = jnp.arange(requests, dtype=jnp.int32) * NODES + accepted_leaf
    leaf_hot = (leaf[:, None] == jnp.arange(rows, dtype=jnp.int32)[None, :]).astype(BF16)
    accepted = jnp.dot(jnp.sum(leaf_hot, axis=0, keepdims=True), reach, preferred_element_type=F32)
    fill_share = jnp.repeat(0.5 + lengths.astype(F32) / CACHE, NODES)
    weights = ((1.0 + 3.0 * accepted.reshape(rows)) * fill_share).reshape(rows, 1)
    own_gain = lax.dynamic_slice_in_dim(norm_gain, tp_rank * block, block, 0).reshape(1, block)

    partial_value = project(parcel, out_weight)
    along_x = exchange(partial_value, "x")
    along_x = jnp.sum(along_x.astype(F32), axis=0).astype(BF16)
    along_x, wide_weight = lax.optimization_barrier((along_x, wide_weight))
    all_weight = gather(wide_weight, "c")
    along_z = exchange(along_x, "zl")
    projected = jnp.sum(along_z.astype(F32), axis=0)
    mixed = residual.reshape(rows, block).astype(F32) + projected

    near = gather(mixed.astype(BF16)[None], "zl")
    far = spread(near, "x", 4).reshape(4, 4, rows, block)
    table, own_features, scaled_err, loss = predict(
        far,
        mixed,
        norm_gain.reshape(N_TP, 1, block),
        own_gain,
        prev_feature,
        parent_column,
        weights,
        all_weight,
    )
    columns = exchange(table, REQ)
    near_err = jnp.stack([scaled_err, lax.ppermute(scaled_err, "zh", turn(2, 1))])
    near_err = jnp.stack(
        [near_err] + [lax.ppermute(near_err, "y", turn(4, step)) for step in (1, 2, 3)]
    )
    other_err = lax.ppermute(near_err, "c", turn(2, 1))
    zh, y, c = lax.axis_index("zh"), lax.axis_index("y"), lax.axis_index("c")
    piece = jnp.arange(N_REQ, dtype=jnp.int32)
    source = (
        ((zh + piece % 2) % 2) * 8 + ((y + 4 - (piece // 2) % 4) % 4) * 2 + (c + piece // 8) % 2
    )
    gradient, pair = differentiate(source, columns, near_err, other_err, loss)
    pair = jnp.sum(exchange(pair, REQ + TP), axis=0)
    square_total, error_total = pair[0], pair[1]
    draft_loss = 0.5 * error_total / (rows * N_REQ * D)
    grad_norm = jnp.sqrt(square_total) + 1e-06
    clip_factor = jnp.minimum(1.0, D / grad_norm)
    clipped = gradient * clip_factor
    new_first = BETA_ONE * first_moment + (1.0 - BETA_ONE) * clipped
    new_second = BETA_TWO * second_moment + (1.0 - BETA_TWO) * clipped * clipped
    direction = new_first / CORRECT_ONE / (jnp.sqrt(new_second / CORRECT_TWO) + 1e-08)
    new_weight = (draft_weight.astype(F32) - LEARN_RATE * direction).astype(BF16)
    return (
        own_features.reshape(requests, NODES, block),
        new_weight,
        new_first,
        new_second,
        draft_loss,
    )


def solution(mesh):
    fine = Mesh(mesh.devices.reshape(2, 4, 2, 4, 4), REQ + TP)
    placed = (
        P(REQ, None, None),
        P(REQ, TP, None),
        P(REQ, TP, None),
        P(REQ, TP, None),
        P(REQ, TP, None),
        P(REQ, None),
        P(REQ),
        P(REQ),
        P(REQ, None, TP),
        P(),
        P(TP, None),
        P(REQ, None),
        P(REQ, TP),
        P(REQ, TP),
        P(REQ, TP),
    )

    return jax.shard_map(
        body,
        mesh=fine,
        in_specs=placed,
        out_specs=(P(REQ, None, TP), P(REQ, TP), P(REQ, TP), P(REQ, TP), P()),
        check_vma=False,
    )
```

```python
import math

import jax
import jax.numpy as jnp
from jax import lax
from jax.experimental import pallas as pl
from jax.experimental.pallas import tpu as pltpu
from jax.sharding import Mesh
from jax.sharding import PartitionSpec as P

KV_HEADS = 4
HEAD = 128
NODES = 32
CACHE = 4096
D = 8192
N_TP = 16
N_REQ = 16

NEG_FILL = -1e30
NORM_EPSILON = 1e-06
BETA_ONE = 0.9
BETA_TWO = 0.95
CORRECT_ONE = 1.0 - 0.9**10
CORRECT_TWO = 1.0 - 0.95**10
LEARN_RATE = 0.001


REQ = ("zh", "y", "c")
TP = ("zl", "x")
F32 = jnp.float32
BF16 = jnp.bfloat16


def exchange(value, axis):
    return lax.all_to_all(value, axis, 0, 0, tiled=True)


def spread(value, axis, count):
    wide = jnp.broadcast_to(value[None], (count, *value.shape))
    return exchange(wide.reshape(count * value.shape[0], *value.shape[1:]), axis)


def turn(count, step):
    return [(i, (i + step) % count) for i in range(count)]


def turns(value, axis, count):
    return jnp.stack(
        [value] + [lax.ppermute(value, axis, turn(count, step)) for step in range(1, count)]
    )


def gather(value, axis):
    return lax.all_gather(value, axis, axis=0, tiled=True)


def dot(left, right, dims, **kwargs):
    return lax.dot_general(left, right, (dims, ((), ())), preferred_element_type=F32, **kwargs)


def same_request(width=128):
    row = lax.broadcasted_iota(jnp.int32, (128, width), 0)
    lane = lax.broadcasted_iota(jnp.int32, (128, width), 1)
    return row, lane


def attend_kernel(
    rank_ref, len_ref, par_ref, q_ref, ck_ref, cv_ref, tk_ref, tv_ref,
    out_ref, reach_ref, pick_ref, stat_ref,
):
    rank = rank_ref[0]
    row, lane = same_request()
    base = (lane // NODES) * NODES
    tile = jnp.where(
        lax.broadcasted_iota(jnp.int32, (NODES, 128), 0)
        == lax.broadcasted_iota(jnp.int32, (NODES, 128), 1) % NODES,
        1.0,
        0.0,
    )
    wide = dot(par_ref[...].astype(F32).astype(BF16), tile.astype(BF16), ((1,), (0,)))
    lane_request = lax.broadcasted_iota(jnp.int32, (1, 128), 1) // NODES
    parent = wide[0:1]
    for r in range(1, 4):
        parent = jnp.where(lane_request == r, wide[r : r + 1], parent)
    parent = parent.astype(jnp.int32)
    rooted = jnp.where(parent < 0, NODES - 1, parent)
    pick_ref[...] = jnp.where(row == base + rooted, 1.0, 0.0).astype(BF16)
    up = jnp.where(row == base + parent, jnp.where(parent >= 0, 1.0, 0.0), 0.0)
    reach = (jnp.where(row == lane, 1.0, 0.0) + up).astype(BF16)
    for _ in range((NODES - 1).bit_length()):
        reach = jnp.minimum(dot(reach, reach, ((1,), (0,))), 1.0).astype(BF16)
    reach_ref[...] = reach
    own = jnp.where(row % NODES == 2 * rank + lane, jnp.where(lane < 2, 1.0, 0.0), 0.0)
    visible = dot(reach, own.astype(BF16), ((0,), (0,)))
    scale = 1.0 / math.sqrt(HEAD)
    span = ck_ref.shape[1]
    slot = lax.broadcasted_iota(jnp.int32, (256, span), 1) + rank * span
    wide_lane = lax.broadcasted_iota(jnp.int32, (NODES, 128), 1)
    for r in range(q_ref.shape[0]):
        live = slot < len_ref[r]
        seen = visible[r * NODES : (r + 1) * NODES, : tk_ref.shape[1]]
        seen = jnp.concatenate([seen] * 8, axis=0) > 0.5
        stats = jnp.zeros((NODES, 128), F32)
        for k in range(KV_HEADS):
            head = slice(k * HEAD, (k + 1) * HEAD)
            query = jnp.concatenate(
                [q_ref[r, :, (k * 8 + g) * HEAD : (k * 8 + g + 1) * HEAD] for g in range(8)], axis=0
            )
            scores = dot(query, ck_ref[r, :, head], ((1,), (1,))) * scale
            tree = dot(query, tk_ref[r, :, head], ((1,), (1,))) * scale
            scores = jnp.where(live, scores, NEG_FILL)
            tree = jnp.where(seen, tree, NEG_FILL)
            top = jnp.maximum(
                jnp.max(scores, axis=1, keepdims=True), jnp.max(tree, axis=1, keepdims=True)
            )
            top = top.astype(BF16).astype(F32)
            probs = jnp.where(live, jnp.exp(scores - top), 0.0).astype(BF16)
            tree = jnp.where(seen, jnp.exp(tree - top), 0.0).astype(BF16)
            total = jnp.sum(probs.astype(F32), axis=1, keepdims=True) + jnp.sum(
                tree.astype(F32), axis=1, keepdims=True
            )
            high = total.astype(BF16).astype(F32)
            low = total - high
            value = dot(probs, cv_ref[r, :, head], ((1,), (0,))) + dot(
                tree, tv_ref[r, :, head], ((1,), (0,))
            )
            value = value.astype(BF16)
            for g in range(8):
                h = k * 8 + g
                part = slice(g * NODES, (g + 1) * NODES)
                out_ref[h // 2, r * NODES : (r + 1) * NODES, (h % 2) * HEAD : (h % 2 + 1) * HEAD] = value[part]
                for at, column in enumerate((top, high, low)):
                    stats = jnp.where(wide_lane == h * 4 + at, column[part], stats)
        stat_ref[r * NODES : (r + 1) * NODES, :] = stats
    turned = jnp.transpose(stat_ref[...])
    empty = jnp.zeros((8, 128), F32)
    blank = jnp.zeros((16, 128), BF16)
    for owner in range(N_TP):
        block = jnp.concatenate([turned[owner * 8 : (owner + 1) * 8], empty], axis=0)
        out_ref[owner, 128:144, 0:128] = block.astype(BF16)
        out_ref[owner, 128:144, 128:256] = blank


def project_kernel(parcel_ref, weight_ref, out_ref, att_ref):
    @pl.when(pl.program_id(0) == 0)
    def join():
        stats = jnp.concatenate(
            [parcel_ref[src, 128:144, 0:128].astype(F32)[0:8] for src in range(N_TP)], axis=0
        )
        total = pltpu.roll(stats, 127, 0) + pltpu.roll(stats, 126, 0)
        stats = stats.reshape(N_TP, 8, 128)
        factor = jnp.exp(stats - jnp.max(stats, axis=0, keepdims=True))
        share = factor / jnp.sum(factor * total.reshape(N_TP, 8, 128), axis=0, keepdims=True)
        share = jnp.transpose(share.reshape(128, 128))
        for side in range(2):
            cols = slice(side * HEAD, (side + 1) * HEAD)
            joined = jnp.zeros((128, HEAD), F32)
            for src in range(N_TP):
                at = src * 8 + side * 4
                joined = joined + parcel_ref[src, 0:128, cols].astype(F32) * share[:, at : at + 1]
            att_ref[:, cols] = joined.astype(BF16)

    for x in range(4):
        cols = slice(x * 512, (x + 1) * 512)
        out_ref[x, 0] = dot(att_ref[...], weight_ref[:, cols], ((1,), (0,))).astype(BF16)


def settle_kernel(rank_ref, along_ref, residual_ref, gain_ref, prev_ref, mixed_ref, near_ref, table_ref):
    mixed = residual_ref[...].astype(F32)
    total = along_ref[0].astype(F32)
    for term in range(1, 4):
        total = total + along_ref[term].astype(F32)
    mixed = mixed + total
    mixed_ref[...] = mixed
    near_ref[...] = mixed.astype(BF16)
    scaled = mixed * gain_ref[0]
    node = lax.broadcasted_iota(jnp.int32, (NODES, 1), 0)
    prev = prev_ref[...].astype(F32)
    for r in range(4):
        part = slice(r * NODES, (r + 1) * NODES)
        table_ref[part] = jnp.where(node == NODES - 1, prev[r : r + 1], scaled[part]).astype(BF16)


def predict_kernel(
    source_ref, rank_ref, len_ref, leaf_ref, far_ref, mixed_ref, gain_ref, prev_ref, reach_ref,
    pick_ref, near_ref, other_ref, own_ref, err_ref, loss_ref, scale_ref, ahead_ref,
):
    step = pl.program_id(0)

    @pl.when(step == 0)
    def start():
        square = jnp.zeros((128, 128), F32)
        for zl in range(4):
            for x in range(4):
                part = far_ref[x, zl].astype(F32)
                part = part * part
                for i in range(4):
                    square = square + part[:, i * 128 : (i + 1) * 128]
        square = jnp.sum(square, axis=1, keepdims=True)
        scale = lax.rsqrt(square / D + NORM_EPSILON)
        scale_ref[...] = jnp.broadcast_to(scale, (128, 128))
        own_ref[...] = (mixed_ref[...] * scale * gain_ref[rank_ref[0]]).astype(BF16)

    node = lax.broadcasted_iota(jnp.int32, (NODES, 1), 0)

    def multiply(weight_ref):
        total = jnp.zeros((128, 512), F32)
        for i in range(4):
            p = source_ref[step * 4 + i]
            block = far_ref[lax.rem(p, 4), p // 4].astype(F32) * scale_ref[:, 0:1] * gain_ref[p]
            prev = prev_ref[:, pl.ds(pl.multiple_of(p * 512, 512), 512)].astype(F32)
            block = jnp.concatenate(
                [
                    jnp.where(node == NODES - 1, prev[r : r + 1], block[r * NODES : (r + 1) * NODES])
                    for r in range(4)
                ],
                axis=0,
            ).astype(BF16)
            total = total + dot(block, weight_ref[i], ((1,), (0,)))
        return total

    @pl.when(step == 0)
    def first():
        ahead_ref[...] = multiply(near_ref)

    @pl.when(step == 1)
    def second():
        ahead_ref[...] += multiply(near_ref)

    @pl.when(step >= 2)
    def rest():
        ahead_ref[...] += multiply(other_ref)

    @pl.when(step == 3)
    def finish():
        row, lane = same_request()
        accepted = []
        for r in range(4):
            part = slice(r * NODES, (r + 1) * NODES)
            path = jnp.where(lane[part] == leaf_ref[r] + r * NODES, reach_ref[part].astype(F32), 0.0)
            path = jnp.sum(path, axis=1, keepdims=True)
            accepted.append((1.0 + 3.0 * path) * (0.5 + len_ref[r].astype(F32) / CACHE))
        weights = jnp.concatenate(accepted, axis=0)
        pick = pick_ref[...].astype(F32)
        predicted = dot(pick, ahead_ref[...], ((0,), (0,)), precision=lax.Precision.HIGHEST)
        error = predicted - own_ref[...].astype(F32)
        weighted = weights * error
        joined = dot(pick, weighted, ((1,), (0,)), precision=lax.Precision.HIGHEST)
        scale = jnp.where(row[:, 0:1] % NODES == NODES - 1, 1.0, scale_ref[:, 0:1])
        err_ref[...] = (joined * scale).astype(BF16)
        loss = jnp.sum(jnp.sum(weighted * error, axis=0, keepdims=True), axis=1, keepdims=True)
        loss_ref[...] = jnp.broadcast_to(loss, (8, 128))


def differentiate_kernel(source_ref, column_ref, near_ref, other_ref, loss_ref, grad_ref, pair_ref):
    for part in range(4):
        left = jnp.concatenate([column_ref[source_ref[part * 4 + i]] for i in range(4)], axis=0)
        err_ref = near_ref if part < 2 else other_ref
        right = jnp.concatenate(
            [err_ref[(part % 2) * 2 + i // 2, i % 2] for i in range(4)], axis=0
        )
        term = dot(left, right, ((0,), (0,)))
        if part == 0:
            grad_ref[...] = term
        else:
            grad_ref[...] += term
    value = grad_ref[...]
    square = jnp.sum(jnp.sum(value * value, axis=0, keepdims=True), axis=1, keepdims=True)
    lane = lax.broadcasted_iota(jnp.int32, (8, 128), 1)
    pair = jnp.where(lane == 0, square, jnp.where(lane == 1, loss_ref[...], 0.0))
    for i in range(32):
        pair_ref[i * 8 : (i + 1) * 8] = pair


def in_vmem():
    return pl.BlockSpec(memory_space=pltpu.VMEM)


def in_smem():
    return pl.BlockSpec(memory_space=pltpu.SMEM)


def attend(rank, lengths, parents, queries, cache_keys, cache_values, tree_keys, tree_values):
    return pl.pallas_call(
        attend_kernel,
        out_shape=(
            jax.ShapeDtypeStruct((N_TP, 144, 2 * HEAD), BF16),
            jax.ShapeDtypeStruct((128, 128), BF16),
            jax.ShapeDtypeStruct((128, 128), BF16),
        ),
        in_specs=[in_smem(), in_smem()] + [in_vmem()] * 6,
        out_specs=(in_vmem(), in_vmem(), in_vmem()),
        scratch_shapes=[pltpu.VMEM((128, 128), F32)],
        cost_estimate=pl.CostEstimate(
            flops=2 * 2 * 16 * 256 * 256 * 128, bytes_accessed=4 << 20, transcendentals=16 * 256 * 256
        ),
        name="attend",
    )(rank, lengths, parents, queries, cache_keys, cache_values, tree_keys, tree_values)


def project(parcel, out_weight):
    return pl.pallas_call(
        project_kernel,
        grid=(4,),
        out_shape=jax.ShapeDtypeStruct((4, 4, 128, 512), BF16),
        in_specs=[
            pl.BlockSpec((N_TP, 144, 2 * HEAD), lambda p: (0, 0, 0)),
            pl.BlockSpec((2 * HEAD, 2048), lambda p: (0, p)),
        ],
        out_specs=pl.BlockSpec((4, 1, 128, 512), lambda p: (0, p, 0, 0)),
        scratch_shapes=[pltpu.VMEM((128, 2 * HEAD), BF16)],
        cost_estimate=pl.CostEstimate(
            flops=2 * 128 * 256 * 8192, bytes_accessed=7 << 20, transcendentals=0
        ),
        name="project",
    )(parcel, out_weight)


def settle(rank, along, residual, gain, prev):
    return pl.pallas_call(
        settle_kernel,
        grid_spec=pltpu.PrefetchScalarGridSpec(
            num_scalar_prefetch=1,
            grid=(1,),
            in_specs=[
                pl.BlockSpec((4, 128, 512), lambda p, at: (0, 0, 0)),
                pl.BlockSpec((128, 512), lambda p, at: (0, 0)),
                pl.BlockSpec((1, 1, 512), lambda p, at: (at[0], 0, 0)),
                pl.BlockSpec((4, 512), lambda p, at: (0, at[0])),
            ],
            out_specs=[pl.BlockSpec((128, 512), lambda p, at: (0, 0))] * 3,
        ),
        out_shape=(
            jax.ShapeDtypeStruct((128, 512), F32),
            jax.ShapeDtypeStruct((128, 512), BF16),
            jax.ShapeDtypeStruct((128, 512), BF16),
        ),
        cost_estimate=pl.CostEstimate(
            flops=128 * 512 * 8, bytes_accessed=2 << 20, transcendentals=0
        ),
        name="settle",
    )(rank, along, residual, gain, prev)


def predict(source, rank, lengths, leaf, far, mixed, gain, prev, reach, pick, near, other):
    return pl.pallas_call(
        predict_kernel,
        grid=(4,),
        out_shape=(
            jax.ShapeDtypeStruct((128, 512), BF16),
            jax.ShapeDtypeStruct((128, 512), BF16),
            jax.ShapeDtypeStruct((8, 128), F32),
        ),
        in_specs=[in_smem()] * 4
        + [
            pl.BlockSpec((4, 4, 128, 512), lambda p: (0, 0, 0, 0)),
            pl.BlockSpec((128, 512), lambda p: (0, 0)),
            pl.BlockSpec((N_TP, 1, 512), lambda p: (0, 0, 0)),
            pl.BlockSpec((4, D), lambda p: (0, 0)),
            pl.BlockSpec((128, 128), lambda p: (0, 0)),
            pl.BlockSpec((128, 128), lambda p: (0, 0)),
            pl.BlockSpec((4, 512, 512), lambda p: (jnp.minimum(p, 1), 0, 0)),
            pl.BlockSpec((4, 512, 512), lambda p: (jnp.maximum(p - 2, 0), 0, 0)),
        ],
        out_specs=(
            pl.BlockSpec((128, 512), lambda p: (0, 0)),
            pl.BlockSpec((128, 512), lambda p: (0, 0)),
            pl.BlockSpec((8, 128), lambda p: (0, 0)),
        ),
        scratch_shapes=[pltpu.VMEM((128, 128), F32), pltpu.VMEM((128, 512), F32)],
        cost_estimate=pl.CostEstimate(
            flops=2 * 128 * 8192 * 512, bytes_accessed=13 << 20, transcendentals=0
        ),
        name="predict",
    )(source, rank, lengths, leaf, far, mixed, gain, prev, reach, pick, near, other)


def differentiate(source, columns, near_err, other_err, loss):
    return pl.pallas_call(
        differentiate_kernel,
        out_shape=(
            jax.ShapeDtypeStruct((512, 512), F32),
            jax.ShapeDtypeStruct((N_REQ * N_TP, 128), F32),
        ),
        in_specs=[in_smem()] + [in_vmem()] * 4,
        out_specs=(in_vmem(), in_vmem()),
        cost_estimate=pl.CostEstimate(
            flops=2 * 2048 * 512 * 512, bytes_accessed=5 << 20, transcendentals=0
        ),
        name="differentiate",
    )(source, columns, near_err, other_err, loss)


def body(
    queries,
    cache_keys,
    cache_values,
    tree_keys,
    tree_values,
    parents,
    lengths,
    accepted_leaf,
    residual,
    norm_gain,
    out_weight,
    prev_feature,
    draft_weight,
    first_moment,
    second_moment,
):
    requests = queries.shape[0]
    rows = requests * NODES
    tp_rank = lax.axis_index(TP)
    rank = tp_rank.reshape(1)
    block = residual.shape[2]
    gain = norm_gain.reshape(N_TP, 1, block)
    zh, y, c = lax.axis_index("zh"), lax.axis_index("y"), lax.axis_index("c")
    piece = jnp.arange(N_REQ, dtype=jnp.int32)
    source = (
        ((zh + piece % 2) % 2) * 8 + ((y + 4 - (piece // 2) % 4) % 4) * 2 + (c + piece // 8) % 2
    )
    place = (source % 4) * 4 + (lax.axis_index("zl") + 4 - source // 4) % 4

    wide_weight = turns(draft_weight, "zh", 2)
    parcel, reach, pick = attend(
        rank, lengths, parents, queries, cache_keys, cache_values, tree_keys, tree_values
    )
    parcel = exchange(parcel, TP)
    parcel, wide_weight = lax.optimization_barrier((parcel, wide_weight))
    wide_weight = turns(wide_weight, "y", 4)

    partial_value = project(parcel, out_weight)
    along_x = exchange(partial_value, "x")
    along_x = jnp.sum(along_x.astype(F32), axis=0).astype(BF16)
    along_x, wide_weight = lax.optimization_barrier((along_x, wide_weight))
    other_weight = lax.ppermute(wide_weight, "c", turn(2, 1))
    along_z = exchange(along_x, "zl")
    mixed, near, table = settle(rank, along_z, residual.reshape(rows, block), gain, prev_feature)

    swapped = lax.ppermute(
        table, REQ + TP, [(i * N_TP + j, j * N_TP + i) for i in range(16) for j in range(16)]
    )
    far = gather(near[None], "zl")
    far = spread(far, "x", 4).reshape(4, 4, rows, block)
    swapped, far = lax.optimization_barrier((swapped, far))
    columns = turns(swapped, "zl", 4)
    own_features, scaled_err, loss = predict(
        source,
        rank,
        lengths,
        accepted_leaf,
        far,
        mixed,
        gain,
        prev_feature,
        reach,
        pick,
        wide_weight.reshape(8, block, block),
        other_weight.reshape(8, block, block),
    )
    columns, scaled_err = lax.optimization_barrier((columns, scaled_err))
    columns = spread(columns, "x", 4).reshape(N_REQ, rows, block)
    near_err = turns(scaled_err, "zh", 2)
    near_err = turns(near_err, "y", 4)
    other_err = lax.ppermute(near_err, "c", turn(2, 1))
    gradient, pair = differentiate(place, columns, near_err, other_err, loss)
    pair = jnp.sum(exchange(pair, REQ + TP), axis=0)
    square_total, error_total = pair[0], pair[1]
    draft_loss = 0.5 * error_total / (rows * N_REQ * D)
    grad_norm = jnp.sqrt(square_total) + 1e-06
    clip_factor = jnp.minimum(1.0, D / grad_norm)
    clipped = gradient * clip_factor
    new_first = BETA_ONE * first_moment + (1.0 - BETA_ONE) * clipped
    new_second = BETA_TWO * second_moment + (1.0 - BETA_TWO) * clipped * clipped
    direction = new_first / CORRECT_ONE / (jnp.sqrt(new_second / CORRECT_TWO) + 1e-08)
    new_weight = (draft_weight.astype(F32) - LEARN_RATE * direction).astype(BF16)
    return (
        own_features.reshape(requests, NODES, block),
        new_weight,
        new_first,
        new_second,
        draft_loss,
    )


def solution(mesh):
    fine = Mesh(mesh.devices.reshape(2, 4, 2, 4, 4), REQ + TP)
    placed = (
        P(REQ, None, None),
        P(REQ, TP, None),
        P(REQ, TP, None),
        P(REQ, TP, None),
        P(REQ, TP, None),
        P(REQ, None),
        P(REQ),
        P(REQ),
        P(REQ, None, TP),
        P(),
        P(TP, None),
        P(REQ, None),
        P(REQ, TP),
        P(REQ, TP),
        P(REQ, TP),
    )

    return jax.shard_map(
        body,
        mesh=fine,
        in_specs=placed,
        out_specs=(P(REQ, None, TP), P(REQ, TP), P(REQ, TP), P(REQ, TP), P()),
        check_vma=False,
    )
```

```python
import math

import jax
import jax.numpy as jnp
from jax import lax
from jax.experimental import pallas as pl
from jax.experimental.pallas import tpu as pltpu
from jax.sharding import Mesh
from jax.sharding import PartitionSpec as P

KV_HEADS = 4
HEAD = 128
NODES = 32
CACHE = 4096
D = 8192
N_TP = 16
N_REQ = 16

NEG_FILL = -1e30
NORM_EPSILON = 1e-06
BETA_ONE = 0.9
BETA_TWO = 0.95
CORRECT_ONE = 1.0 - 0.9**10
CORRECT_TWO = 1.0 - 0.95**10
LEARN_RATE = 0.001


REQ = ("zh", "y", "c")
TP = ("zl", "x")
F32 = jnp.float32
BF16 = jnp.bfloat16


def exchange(value, axis):
    return lax.all_to_all(value, axis, 0, 0, tiled=True)


def spread(value, axis, count):
    wide = jnp.broadcast_to(value[None], (count, *value.shape))
    return exchange(wide.reshape(count * value.shape[0], *value.shape[1:]), axis)


def turn(count, step):
    return [(i, (i + step) % count) for i in range(count)]


def passed(value, axis, count):
    return [value] + [lax.ppermute(value, axis, turn(count, step)) for step in range(1, count)]


def turns(value, axis, count):
    return jnp.stack(passed(value, axis, count))


def dot(left, right, dims, **kwargs):
    return lax.dot_general(left, right, (dims, ((), ())), preferred_element_type=F32, **kwargs)


def same_request(width=128):
    row = lax.broadcasted_iota(jnp.int32, (128, width), 0)
    lane = lax.broadcasted_iota(jnp.int32, (128, width), 1)
    return row, lane


def attend_kernel(
    rank_ref, len_ref, par_ref, q_ref, ck_ref, cv_ref, tk_ref, tv_ref,
    out_ref, reach_ref, pick_ref, stat_ref,
):
    rank = rank_ref[0]
    row, lane = same_request()
    base = (lane // NODES) * NODES
    tile = jnp.where(
        lax.broadcasted_iota(jnp.int32, (NODES, 128), 0)
        == lax.broadcasted_iota(jnp.int32, (NODES, 128), 1) % NODES,
        1.0,
        0.0,
    )
    wide = dot(par_ref[...].astype(F32).astype(BF16), tile.astype(BF16), ((1,), (0,)))
    lane_request = lax.broadcasted_iota(jnp.int32, (1, 128), 1) // NODES
    parent = wide[0:1]
    for r in range(1, 4):
        parent = jnp.where(lane_request == r, wide[r : r + 1], parent)
    parent = parent.astype(jnp.int32)
    rooted = jnp.where(parent < 0, NODES - 1, parent)
    pick_ref[...] = jnp.where(row == base + rooted, 1.0, 0.0).astype(BF16)
    up = jnp.where(row == base + parent, jnp.where(parent >= 0, 1.0, 0.0), 0.0)
    reach = (jnp.where(row == lane, 1.0, 0.0) + up).astype(BF16)
    for _ in range((NODES - 1).bit_length()):
        reach = jnp.minimum(dot(reach, reach, ((1,), (0,))), 1.0).astype(BF16)
    reach_ref[...] = reach
    own = jnp.where(row % NODES == 2 * rank + lane, jnp.where(lane < 2, 1.0, 0.0), 0.0)
    visible = dot(reach, own.astype(BF16), ((0,), (0,)))
    scale = 1.0 / math.sqrt(HEAD)
    span = ck_ref.shape[1]
    slot = lax.broadcasted_iota(jnp.int32, (256, span), 1) + rank * span
    wide_lane = lax.broadcasted_iota(jnp.int32, (NODES, 128), 1)
    for r in range(q_ref.shape[0]):
        live = slot < len_ref[r]
        seen = visible[r * NODES : (r + 1) * NODES, : tk_ref.shape[1]]
        seen = jnp.concatenate([seen] * 8, axis=0) > 0.5
        stats = jnp.zeros((NODES, 128), F32)
        for k in range(KV_HEADS):
            head = slice(k * HEAD, (k + 1) * HEAD)
            query = jnp.concatenate(
                [q_ref[r, :, (k * 8 + g) * HEAD : (k * 8 + g + 1) * HEAD] for g in range(8)], axis=0
            )
            scores = dot(query, ck_ref[r, :, head], ((1,), (1,))) * scale
            tree = dot(query, tk_ref[r, :, head], ((1,), (1,))) * scale
            scores = jnp.where(live, scores, NEG_FILL)
            tree = jnp.where(seen, tree, NEG_FILL)
            top = jnp.maximum(
                jnp.max(scores, axis=1, keepdims=True), jnp.max(tree, axis=1, keepdims=True)
            )
            top = top.astype(BF16).astype(F32)
            probs = jnp.where(live, jnp.exp(scores - top), 0.0).astype(BF16)
            tree = jnp.where(seen, jnp.exp(tree - top), 0.0).astype(BF16)
            total = jnp.sum(probs.astype(F32), axis=1, keepdims=True) + jnp.sum(
                tree.astype(F32), axis=1, keepdims=True
            )
            high = total.astype(BF16).astype(F32)
            low = total - high
            value = dot(probs, cv_ref[r, :, head], ((1,), (0,))) + dot(
                tree, tv_ref[r, :, head], ((1,), (0,))
            )
            value = value.astype(BF16)
            for g in range(8):
                h = k * 8 + g
                part = slice(g * NODES, (g + 1) * NODES)
                out_ref[h // 2, r * NODES : (r + 1) * NODES, (h % 2) * HEAD : (h % 2 + 1) * HEAD] = value[part]
                for at, column in enumerate((top, high, low)):
                    stats = jnp.where(wide_lane == h * 4 + at, column[part], stats)
        stat_ref[r * NODES : (r + 1) * NODES, :] = stats
    turned = jnp.transpose(stat_ref[...])
    empty = jnp.zeros((8, 128), F32)
    blank = jnp.zeros((16, 128), BF16)
    for owner in range(N_TP):
        block = jnp.concatenate([turned[owner * 8 : (owner + 1) * 8], empty], axis=0)
        out_ref[owner, 128:144, 0:128] = block.astype(BF16)
        out_ref[owner, 128:144, 128:256] = blank


def project_kernel(parcel_ref, weight_ref, out_ref, att_ref):
    @pl.when(pl.program_id(0) == 0)
    def join():
        stats = jnp.concatenate(
            [parcel_ref[src, 128:144, 0:128].astype(F32)[0:8] for src in range(N_TP)], axis=0
        )
        total = pltpu.roll(stats, 127, 0) + pltpu.roll(stats, 126, 0)
        stats = stats.reshape(N_TP, 8, 128)
        factor = jnp.exp(stats - jnp.max(stats, axis=0, keepdims=True))
        share = factor / jnp.sum(factor * total.reshape(N_TP, 8, 128), axis=0, keepdims=True)
        share = jnp.transpose(share.reshape(128, 128))
        for side in range(2):
            cols = slice(side * HEAD, (side + 1) * HEAD)
            joined = jnp.zeros((128, HEAD), F32)
            for src in range(N_TP):
                at = src * 8 + side * 4
                joined = joined + parcel_ref[src, 0:128, cols].astype(F32) * share[:, at : at + 1]
            att_ref[:, cols] = joined.astype(BF16)

    for x in range(4):
        cols = slice(x * 512, (x + 1) * 512)
        out_ref[x, 0] = dot(att_ref[...], weight_ref[:, cols], ((1,), (0,))).astype(BF16)


def fold_kernel(rank_ref, along_ref, *out_refs):
    for step in range(4):
        zl = lax.rem(rank_ref[0] // 4 + step, 4)
        total = along_ref[0, zl].astype(F32)
        for x in range(1, 4):
            total = total + along_ref[x, zl].astype(F32)
        out_refs[step][...] = total.astype(BF16)


def settle_kernel(
    rank_ref, own_ref, one_ref, two_ref, three_ref, residual_ref, gain_ref, prev_ref,
    mixed_ref, near_ref, table_ref,
):
    total = own_ref[...].astype(F32) + one_ref[...].astype(F32)
    total = total + (two_ref[...].astype(F32) + three_ref[...].astype(F32))
    mixed = residual_ref[...].astype(F32) + total
    mixed_ref[...] = mixed
    near_ref[...] = mixed.astype(BF16)
    scaled = mixed * gain_ref[0]
    node = lax.broadcasted_iota(jnp.int32, (NODES, 1), 0)
    prev = prev_ref[...].astype(F32)
    for r in range(4):
        part = slice(r * NODES, (r + 1) * NODES)
        table_ref[part] = jnp.where(node == NODES - 1, prev[r : r + 1], scaled[part]).astype(BF16)


def predict_kernel(
    source_ref, rank_ref, len_ref, leaf_ref, far_ref, mixed_ref, gain_ref, prev_ref, reach_ref,
    pick_ref, *refs,
):
    weight_refs = refs[:16]
    own_ref, err_ref, loss_ref, scale_ref, ahead_ref, weight_ref, sem_ref = refs[16:]
    loads = [pltpu.make_async_copy(weight_refs[i], weight_ref.at[i], sem_ref.at[i]) for i in range(16)]
    for load in loads:
        load.start()
    square = jnp.zeros((128, 128), F32)
    for k in range(4):
        for x in range(4):
            part = far_ref[x, k].astype(F32)
            part = part * part
            for i in range(4):
                square = square + part[:, i * 128 : (i + 1) * 128]
    square = jnp.sum(square, axis=1, keepdims=True)
    scale = lax.rsqrt(square / D + NORM_EPSILON)
    scale_ref[...] = jnp.broadcast_to(scale, (128, 128))
    own_ref[...] = (mixed_ref[...] * scale * gain_ref[rank_ref[0]]).astype(BF16)

    node = lax.broadcasted_iota(jnp.int32, (NODES, 1), 0)
    for part in range(8):
        loads[part].wait()
        loads[part + 8].wait()
        total = jnp.zeros((128, 512), F32)
        for i in range(2):
            p = source_ref[part * 2 + i]
            back = lax.rem(rank_ref[0] // 4 + 4 - p // 4, 4)
            block = far_ref[lax.rem(p, 4), back].astype(F32) * scale_ref[:, 0:1] * gain_ref[p]
            prev = prev_ref[:, pl.ds(pl.multiple_of(p * 512, 512), 512)].astype(F32)
            block = jnp.concatenate(
                [
                    jnp.where(node == NODES - 1, prev[r : r + 1], block[r * NODES : (r + 1) * NODES])
                    for r in range(4)
                ],
                axis=0,
            ).astype(BF16)
            total = total + dot(block[:, :256], weight_ref[part, i], ((1,), (0,)))
            total = total + dot(block[:, 256:], weight_ref[part + 8, i], ((1,), (0,)))
        if part == 0:
            ahead_ref[...] = total
        else:
            ahead_ref[...] += total

    row, lane = same_request()
    accepted = []
    for r in range(4):
        part = slice(r * NODES, (r + 1) * NODES)
        path = jnp.where(lane[part] == leaf_ref[r] + r * NODES, reach_ref[part].astype(F32), 0.0)
        path = jnp.sum(path, axis=1, keepdims=True)
        accepted.append((1.0 + 3.0 * path) * (0.5 + len_ref[r].astype(F32) / CACHE))
    weights = jnp.concatenate(accepted, axis=0)
    pick = pick_ref[...].astype(F32)
    predicted = dot(pick, ahead_ref[...], ((0,), (0,)), precision=lax.Precision.HIGHEST)
    error = predicted - own_ref[...].astype(F32)
    weighted = weights * error
    joined = dot(pick, weighted, ((1,), (0,)), precision=lax.Precision.HIGHEST)
    scale = jnp.where(row[:, 0:1] % NODES == NODES - 1, 1.0, scale_ref[:, 0:1])
    err_ref[...] = (joined * scale).astype(BF16)
    loss = jnp.sum(jnp.sum(weighted * error, axis=0, keepdims=True), axis=1, keepdims=True)
    loss_ref[...] = jnp.broadcast_to(loss, (8, 128))


def differentiate_kernel(source_ref, column_ref, near_ref, other_ref, loss_ref, grad_ref, pair_ref):
    for part in range(4):
        left = jnp.concatenate([column_ref[source_ref[part * 4 + i]] for i in range(4)], axis=0)
        err_ref = near_ref if part < 2 else other_ref
        right = jnp.concatenate(
            [err_ref[(part % 2) * 2 + i // 2, i % 2] for i in range(4)], axis=0
        )
        term = dot(left, right, ((0,), (0,)))
        if part == 0:
            grad_ref[...] = term
        else:
            grad_ref[...] += term
    value = grad_ref[...]
    square = jnp.sum(jnp.sum(value * value, axis=0, keepdims=True), axis=1, keepdims=True)
    lane = lax.broadcasted_iota(jnp.int32, (8, 128), 1)
    pair = jnp.where(lane == 0, square, jnp.where(lane == 1, loss_ref[...], 0.0))
    for i in range(32):
        pair_ref[i * 8 : (i + 1) * 8] = pair


def in_vmem():
    return pl.BlockSpec(memory_space=pltpu.VMEM)


def in_smem():
    return pl.BlockSpec(memory_space=pltpu.SMEM)


def attend(rank, lengths, parents, queries, cache_keys, cache_values, tree_keys, tree_values):
    return pl.pallas_call(
        attend_kernel,
        out_shape=(
            jax.ShapeDtypeStruct((N_TP, 144, 2 * HEAD), BF16),
            jax.ShapeDtypeStruct((128, 128), BF16),
            jax.ShapeDtypeStruct((128, 128), BF16),
        ),
        in_specs=[in_smem(), in_smem()] + [in_vmem()] * 6,
        out_specs=(in_vmem(), in_vmem(), in_vmem()),
        scratch_shapes=[pltpu.VMEM((128, 128), F32)],
        cost_estimate=pl.CostEstimate(
            flops=2 * 2 * 16 * 256 * 256 * 128, bytes_accessed=4 << 20, transcendentals=16 * 256 * 256
        ),
        name="attend",
    )(rank, lengths, parents, queries, cache_keys, cache_values, tree_keys, tree_values)


def project(parcel, out_weight):
    return pl.pallas_call(
        project_kernel,
        grid=(4,),
        out_shape=jax.ShapeDtypeStruct((4, 4, 128, 512), BF16),
        in_specs=[
            pl.BlockSpec((N_TP, 144, 2 * HEAD), lambda p: (0, 0, 0)),
            pl.BlockSpec((2 * HEAD, 2048), lambda p: (0, p)),
        ],
        out_specs=pl.BlockSpec((4, 1, 128, 512), lambda p: (0, p, 0, 0)),
        scratch_shapes=[pltpu.VMEM((128, 2 * HEAD), BF16)],
        cost_estimate=pl.CostEstimate(
            flops=2 * 128 * 256 * 8192, bytes_accessed=7 << 20, transcendentals=0
        ),
        name="project",
    )(parcel, out_weight)


def fold(rank, along):
    return pl.pallas_call(
        fold_kernel,
        out_shape=(jax.ShapeDtypeStruct((128, 512), BF16),) * 4,
        in_specs=[in_smem(), in_vmem()],
        out_specs=(in_vmem(),) * 4,
        cost_estimate=pl.CostEstimate(
            flops=16 * 128 * 512, bytes_accessed=5 << 19, transcendentals=0
        ),
        name="fold",
    )(rank, along)


def settle(rank, terms, residual, gain, prev):
    whole = pl.BlockSpec((128, 512), lambda p, at: (0, 0))
    return pl.pallas_call(
        settle_kernel,
        grid_spec=pltpu.PrefetchScalarGridSpec(
            num_scalar_prefetch=1,
            grid=(1,),
            in_specs=[whole] * 5
            + [
                pl.BlockSpec((1, 1, 512), lambda p, at: (at[0], 0, 0)),
                pl.BlockSpec((4, 512), lambda p, at: (0, at[0])),
            ],
            out_specs=[whole] * 3,
        ),
        out_shape=(
            jax.ShapeDtypeStruct((128, 512), F32),
            jax.ShapeDtypeStruct((128, 512), BF16),
            jax.ShapeDtypeStruct((128, 512), BF16),
        ),
        cost_estimate=pl.CostEstimate(
            flops=128 * 512 * 8, bytes_accessed=2 << 20, transcendentals=0
        ),
        name="settle",
    )(rank, *terms, residual, gain, prev)


def predict(source, rank, lengths, leaf, far, mixed, gain, prev, reach, pick, all_weight):
    return pl.pallas_call(
        predict_kernel,
        out_shape=(
            jax.ShapeDtypeStruct((128, 512), BF16),
            jax.ShapeDtypeStruct((128, 512), BF16),
            jax.ShapeDtypeStruct((8, 128), F32),
        ),
        in_specs=[in_smem()] * 4
        + [in_vmem()] * 6
        + [pl.BlockSpec(memory_space=pl.ANY)] * 16,
        out_specs=(in_vmem(),) * 3,
        scratch_shapes=[
            pltpu.VMEM((128, 128), F32),
            pltpu.VMEM((128, 512), F32),
            pltpu.VMEM((16, 2, 256, 512), BF16),
            pltpu.SemaphoreType.DMA((16,)),
        ],
        compiler_params=pltpu.CompilerParams(vmem_limit_bytes=32 << 20),
        cost_estimate=pl.CostEstimate(
            flops=2 * 128 * 8192 * 512, bytes_accessed=13 << 20, transcendentals=0
        ),
        name="predict",
    )(source, rank, lengths, leaf, far, mixed, gain, prev, reach, pick, *all_weight)


def differentiate(source, columns, near_err, other_err, loss):
    return pl.pallas_call(
        differentiate_kernel,
        out_shape=(
            jax.ShapeDtypeStruct((512, 512), F32),
            jax.ShapeDtypeStruct((N_REQ * N_TP, 128), F32),
        ),
        in_specs=[in_smem()] + [in_vmem()] * 4,
        out_specs=(in_vmem(), in_vmem()),
        cost_estimate=pl.CostEstimate(
            flops=2 * 2048 * 512 * 512, bytes_accessed=5 << 20, transcendentals=0
        ),
        name="differentiate",
    )(source, columns, near_err, other_err, loss)


def body(
    queries,
    cache_keys,
    cache_values,
    tree_keys,
    tree_values,
    parents,
    lengths,
    accepted_leaf,
    residual,
    norm_gain,
    out_weight,
    prev_feature,
    draft_weight,
    first_moment,
    second_moment,
):
    requests = queries.shape[0]
    rows = requests * NODES
    tp_rank = lax.axis_index(TP)
    rank = tp_rank.reshape(1)
    block = residual.shape[2]
    gain = norm_gain.reshape(N_TP, 1, block)
    zh, y, c = lax.axis_index("zh"), lax.axis_index("y"), lax.axis_index("c")
    piece = jnp.arange(N_REQ, dtype=jnp.int32)
    source = (
        ((zh + piece % 2) % 2) * 8 + ((y + 4 - (piece // 2) % 4) % 4) * 2 + (c + piece // 8) % 2
    )
    place = (source % 4) * 4 + (lax.axis_index("zl") + 4 - source // 4) % 4

    half = draft_weight.shape[0] // 2
    upper = passed(draft_weight[:half], "zh", 2)
    parcel, reach, pick = attend(
        rank, lengths, parents, queries, cache_keys, cache_values, tree_keys, tree_values
    )
    parcel = exchange(parcel, TP)
    upper = jnp.stack(upper)
    upper = passed(upper, "y", 4)
    parcel, lower = lax.optimization_barrier((parcel, draft_weight[half:]))
    lower = passed(lower, "zh", 2)

    partial_value = project(parcel, out_weight)
    along_x = exchange(partial_value, "x")
    other_upper = [lax.ppermute(part, "c", turn(2, 1)) for part in upper]
    lower = jnp.stack(lower)
    lower = passed(lower, "y", 4)
    terms = list(fold(rank, along_x))
    terms[1:] = [lax.ppermute(terms[step], "zl", turn(4, step)) for step in (1, 2, 3)]
    mixed, near, table = settle(rank, terms, residual.reshape(rows, block), gain, prev_feature)

    far = turns(near, "zl", 4)
    far, table = lax.optimization_barrier((far, table))
    far = spread(far, "x", 4).reshape(4, 4, rows, block)
    swapped = lax.ppermute(
        table, REQ + TP, [(i * N_TP + j, j * N_TP + i) for i in range(16) for j in range(16)]
    )
    other_lower = [lax.ppermute(part, "c", turn(2, 1)) for part in lower]
    swapped, far = lax.optimization_barrier((swapped, far))
    columns = turns(swapped, "zl", 4)
    own_features, scaled_err, loss = predict(
        source,
        rank,
        lengths,
        accepted_leaf,
        far,
        mixed,
        gain,
        prev_feature,
        reach,
        pick,
        upper + other_upper + lower + other_lower,
    )
    columns, scaled_err = lax.optimization_barrier((columns, scaled_err))
    columns = spread(columns, "x", 4).reshape(N_REQ, rows, block)
    near_err = turns(scaled_err, "zh", 2)
    near_err = turns(near_err, "y", 4)
    other_err = lax.ppermute(near_err, "c", turn(2, 1))
    gradient, pair = differentiate(place, columns, near_err, other_err, loss)
    pair = jnp.sum(exchange(pair, REQ + TP), axis=0)
    square_total, error_total = pair[0], pair[1]
    draft_loss = 0.5 * error_total / (rows * N_REQ * D)
    grad_norm = jnp.sqrt(square_total) + 1e-06
    clip_factor = jnp.minimum(1.0, D / grad_norm)
    clipped = gradient * clip_factor
    new_first = BETA_ONE * first_moment + (1.0 - BETA_ONE) * clipped
    new_second = BETA_TWO * second_moment + (1.0 - BETA_TWO) * clipped * clipped
    direction = new_first / CORRECT_ONE / (jnp.sqrt(new_second / CORRECT_TWO) + 1e-08)
    new_weight = (draft_weight.astype(F32) - LEARN_RATE * direction).astype(BF16)
    return (
        own_features.reshape(requests, NODES, block),
        new_weight,
        new_first,
        new_second,
        draft_loss,
    )


def solution(mesh):
    fine = Mesh(mesh.devices.reshape(2, 4, 2, 4, 4), REQ + TP)
    placed = (
        P(REQ, None, None),
        P(REQ, TP, None),
        P(REQ, TP, None),
        P(REQ, TP, None),
        P(REQ, TP, None),
        P(REQ, None),
        P(REQ),
        P(REQ),
        P(REQ, None, TP),
        P(),
        P(TP, None),
        P(REQ, None),
        P(REQ, TP),
        P(REQ, TP),
        P(REQ, TP),
    )

    return jax.shard_map(
        body,
        mesh=fine,
        in_specs=placed,
        out_specs=(P(REQ, None, TP), P(REQ, TP), P(REQ, TP), P(REQ, TP), P()),
        check_vma=False,
    )
```

```python
import math

import jax
import jax.numpy as jnp
from jax import lax
from jax.experimental import pallas as pl
from jax.experimental.pallas import tpu as pltpu
from jax.sharding import Mesh
from jax.sharding import PartitionSpec as P

KV_HEADS = 4
HEAD = 128
NODES = 32
CACHE = 4096
D = 8192
N_TP = 16
N_REQ = 16

NEG_FILL = -1e30
NORM_EPSILON = 1e-06
BETA_ONE = 0.9
BETA_TWO = 0.95
CORRECT_ONE = 1.0 - 0.9**10
CORRECT_TWO = 1.0 - 0.95**10
LEARN_RATE = 0.001


REQ = ("zh", "y", "c")
TP = ("zl", "x")
F32 = jnp.float32
BF16 = jnp.bfloat16


def exchange(value, axis):
    return lax.all_to_all(value, axis, 0, 0, tiled=True)


def spread(value, axis, count):
    wide = jnp.broadcast_to(value[None], (count, *value.shape))
    return exchange(wide.reshape(count * value.shape[0], *value.shape[1:]), axis)


def turn(count, step):
    return [(i, (i + step) % count) for i in range(count)]


def passed(value, axis, count):
    return [value] + [lax.ppermute(value, axis, turn(count, step)) for step in range(1, count)]


def turns(value, axis, count):
    return jnp.stack(passed(value, axis, count))


def dot(left, right, dims, **kwargs):
    return lax.dot_general(left, right, (dims, ((), ())), preferred_element_type=F32, **kwargs)


def same_request(width=128):
    row = lax.broadcasted_iota(jnp.int32, (128, width), 0)
    lane = lax.broadcasted_iota(jnp.int32, (128, width), 1)
    return row, lane


def attend_kernel(
    rank_ref, len_ref, par_ref, q_ref, ck_ref, cv_ref, tk_ref, tv_ref,
    out_ref, reach_ref, pick_ref, stat_ref,
):
    rank = rank_ref[0]
    row, lane = same_request()
    base = (lane // NODES) * NODES
    tile = jnp.where(
        lax.broadcasted_iota(jnp.int32, (NODES, 128), 0)
        == lax.broadcasted_iota(jnp.int32, (NODES, 128), 1) % NODES,
        1.0,
        0.0,
    )
    wide = dot(par_ref[...].astype(F32).astype(BF16), tile.astype(BF16), ((1,), (0,)))
    lane_request = lax.broadcasted_iota(jnp.int32, (1, 128), 1) // NODES
    parent = wide[0:1]
    for r in range(1, 4):
        parent = jnp.where(lane_request == r, wide[r : r + 1], parent)
    parent = parent.astype(jnp.int32)
    rooted = jnp.where(parent < 0, NODES - 1, parent)
    pick_ref[...] = jnp.where(row == base + rooted, 1.0, 0.0).astype(BF16)
    up = jnp.where(row == base + parent, jnp.where(parent >= 0, 1.0, 0.0), 0.0)
    reach = (jnp.where(row == lane, 1.0, 0.0) + up).astype(BF16)
    for _ in range((NODES - 1).bit_length()):
        reach = jnp.minimum(dot(reach, reach, ((1,), (0,))), 1.0).astype(BF16)
    reach_ref[...] = reach
    own = jnp.where(row % NODES == 2 * rank + lane, jnp.where(lane < 2, 1.0, 0.0), 0.0)
    stat_ref[...] = dot(reach, own.astype(BF16), ((0,), (0,)))
    scale = 1.0 / math.sqrt(HEAD)
    span = ck_ref.shape[1]
    slot = lax.broadcasted_iota(jnp.int32, (256, span), 1) + rank * span
    wide_lane = lax.broadcasted_iota(jnp.int32, (NODES, 128), 1)

    def attend_one(r, carry):
        own_rows = pl.ds(pl.multiple_of(r * NODES, NODES), NODES)
        live = slot < len_ref[r]
        seen = stat_ref[own_rows, :][:, : tk_ref.shape[1]]
        seen = jnp.concatenate([seen] * 8, axis=0) > 0.5
        stats = jnp.zeros((NODES, 128), F32)
        for k in range(KV_HEADS):
            head = slice(k * HEAD, (k + 1) * HEAD)
            query = jnp.concatenate(
                [q_ref[r, :, (k * 8 + g) * HEAD : (k * 8 + g + 1) * HEAD] for g in range(8)], axis=0
            )
            scores = dot(query, ck_ref[r, :, head], ((1,), (1,))) * scale
            tree = dot(query, tk_ref[r, :, head], ((1,), (1,))) * scale
            scores = jnp.where(live, scores, NEG_FILL)
            tree = jnp.where(seen, tree, NEG_FILL)
            top = jnp.maximum(
                jnp.max(scores, axis=1, keepdims=True), jnp.max(tree, axis=1, keepdims=True)
            )
            top = top.astype(BF16).astype(F32)
            probs = jnp.where(live, jnp.exp(scores - top), 0.0).astype(BF16)
            tree = jnp.where(seen, jnp.exp(tree - top), 0.0).astype(BF16)
            total = jnp.sum(probs.astype(F32), axis=1, keepdims=True) + jnp.sum(
                tree.astype(F32), axis=1, keepdims=True
            )
            high = total.astype(BF16).astype(F32)
            low = total - high
            value = dot(probs, cv_ref[r, :, head], ((1,), (0,))) + dot(
                tree, tv_ref[r, :, head], ((1,), (0,))
            )
            value = value.astype(BF16)
            for g in range(8):
                h = k * 8 + g
                part = slice(g * NODES, (g + 1) * NODES)
                out_ref[h // 2, own_rows, (h % 2) * HEAD : (h % 2 + 1) * HEAD] = value[part]
                for at, column in enumerate((top, high, low)):
                    stats = jnp.where(wide_lane == h * 4 + at, column[part], stats)
        stat_ref[own_rows, :] = stats
        return carry

    lax.fori_loop(0, q_ref.shape[0], attend_one, 0)
    turned = jnp.transpose(stat_ref[...])
    empty = jnp.zeros((8, 128), F32)
    blank = jnp.zeros((16, 128), BF16)
    for owner in range(N_TP):
        block = jnp.concatenate([turned[owner * 8 : (owner + 1) * 8], empty], axis=0)
        out_ref[owner, 128:144, 0:128] = block.astype(BF16)
        out_ref[owner, 128:144, 128:256] = blank


def project_kernel(parcel_ref, weight_ref, out_ref, att_ref):
    @pl.when(pl.program_id(0) == 0)
    def join():
        stats = jnp.concatenate(
            [parcel_ref[src, 128:144, 0:128].astype(F32)[0:8] for src in range(N_TP)], axis=0
        )
        total = pltpu.roll(stats, 127, 0) + pltpu.roll(stats, 126, 0)
        stats = stats.reshape(N_TP, 8, 128)
        factor = jnp.exp(stats - jnp.max(stats, axis=0, keepdims=True))
        share = factor / jnp.sum(factor * total.reshape(N_TP, 8, 128), axis=0, keepdims=True)
        share = jnp.transpose(share.reshape(128, 128))
        for side in range(2):
            cols = slice(side * HEAD, (side + 1) * HEAD)
            joined = jnp.zeros((128, HEAD), F32)
            for src in range(N_TP):
                at = src * 8 + side * 4
                joined = joined + parcel_ref[src, 0:128, cols].astype(F32) * share[:, at : at + 1]
            att_ref[:, cols] = joined.astype(BF16)

    for x in range(4):
        cols = slice(x * 512, (x + 1) * 512)
        out_ref[x, 0] = dot(att_ref[...], weight_ref[:, cols], ((1,), (0,))).astype(BF16)


def fold_kernel(rank_ref, along_ref, *out_refs):
    for step in range(4):
        zl = lax.rem(rank_ref[0] // 4 + step, 4)
        total = along_ref[0, zl].astype(F32)
        for x in range(1, 4):
            total = total + along_ref[x, zl].astype(F32)
        out_refs[step][...] = total.astype(BF16)


def settle_kernel(
    rank_ref, own_ref, one_ref, two_ref, three_ref, residual_ref, gain_ref, prev_ref,
    mixed_ref, near_ref, table_ref,
):
    total = own_ref[...].astype(F32) + one_ref[...].astype(F32)
    total = total + (two_ref[...].astype(F32) + three_ref[...].astype(F32))
    mixed = residual_ref[...].astype(F32) + total
    mixed_ref[...] = mixed
    near_ref[...] = mixed.astype(BF16)
    scaled = mixed * gain_ref[0]
    node = lax.broadcasted_iota(jnp.int32, (NODES, 1), 0)
    prev = prev_ref[...].astype(F32)
    for r in range(4):
        part = slice(r * NODES, (r + 1) * NODES)
        table_ref[part] = jnp.where(node == NODES - 1, prev[r : r + 1], scaled[part]).astype(BF16)


def predict_kernel(
    source_ref, rank_ref, len_ref, leaf_ref, far_own_ref, far_rest_ref, mixed_ref, gain_ref, prev_ref, reach_ref,
    pick_ref, *refs,
):
    weight_refs = refs[:16]
    own_ref, err_ref, loss_ref, scale_ref, ahead_ref, weight_ref, sem_ref, far_ref, far_sem = refs[16:]
    own_load = pltpu.make_async_copy(far_own_ref, far_ref.at[:, 0], far_sem.at[0])
    rest_load = pltpu.make_async_copy(far_rest_ref, far_ref.at[:, 1:4], far_sem.at[1])
    own_load.start()
    rest_load.start()
    loads = [pltpu.make_async_copy(weight_refs[i], weight_ref.at[i], sem_ref.at[i]) for i in range(16)]
    for load in loads:
        load.start()
    square = jnp.zeros((128, 128), F32)
    own_load.wait()
    for k in range(4):
        if k == 1:
            rest_load.wait()
        for x in range(4):
            part = far_ref[x, k].astype(F32)
            part = part * part
            for i in range(4):
                square = square + part[:, i * 128 : (i + 1) * 128]
    square = jnp.sum(square, axis=1, keepdims=True)
    scale = lax.rsqrt(square / D + NORM_EPSILON)
    scale_ref[...] = jnp.broadcast_to(scale, (128, 128))
    own_ref[...] = (mixed_ref[...] * scale * gain_ref[rank_ref[0]]).astype(BF16)

    node = lax.broadcasted_iota(jnp.int32, (NODES, 1), 0)
    for part in range(8):
        loads[part].wait()
        loads[part + 8].wait()
        total = jnp.zeros((128, 512), F32)
        for i in range(2):
            p = source_ref[part * 2 + i]
            back = lax.rem(rank_ref[0] // 4 + 4 - p // 4, 4)
            block = far_ref[lax.rem(p, 4), back].astype(F32) * scale_ref[:, 0:1] * gain_ref[p]
            prev = prev_ref[:, pl.ds(pl.multiple_of(p * 512, 512), 512)].astype(F32)
            block = jnp.concatenate(
                [
                    jnp.where(node == NODES - 1, prev[r : r + 1], block[r * NODES : (r + 1) * NODES])
                    for r in range(4)
                ],
                axis=0,
            ).astype(BF16)
            total = total + dot(block[:, :256], weight_ref[part, i], ((1,), (0,)))
            total = total + dot(block[:, 256:], weight_ref[part + 8, i], ((1,), (0,)))
        if part == 0:
            ahead_ref[...] = total
        else:
            ahead_ref[...] += total

    row, lane = same_request()
    accepted = []
    for r in range(4):
        part = slice(r * NODES, (r + 1) * NODES)
        path = jnp.where(lane[part] == leaf_ref[r] + r * NODES, reach_ref[part].astype(F32), 0.0)
        path = jnp.sum(path, axis=1, keepdims=True)
        accepted.append((1.0 + 3.0 * path) * (0.5 + len_ref[r].astype(F32) / CACHE))
    weights = jnp.concatenate(accepted, axis=0)
    pick = pick_ref[...].astype(F32)
    predicted = dot(pick, ahead_ref[...], ((0,), (0,)), precision=lax.Precision.HIGHEST)
    error = predicted - own_ref[...].astype(F32)
    weighted = weights * error
    joined = dot(pick, weighted, ((1,), (0,)), precision=lax.Precision.HIGHEST)
    scale = jnp.where(row[:, 0:1] % NODES == NODES - 1, 1.0, scale_ref[:, 0:1])
    err_ref[...] = (joined * scale).astype(BF16)
    loss = jnp.sum(jnp.sum(weighted * error, axis=0, keepdims=True), axis=1, keepdims=True)
    loss_ref[...] = jnp.broadcast_to(loss, (8, 128))


def differentiate_kernel(place_ref, column_ref, e0_ref, e1_ref, e2_ref, e3_ref, loss_ref, grad_ref, pair_ref):
    for part, err_ref in enumerate((e0_ref, e1_ref, e2_ref, e3_ref)):
        first = (part // 2) * 8 + part % 2
        left = jnp.concatenate([column_ref[place_ref[first + 2 * i]] for i in range(4)], axis=0)
        right = jnp.concatenate([err_ref[i] for i in range(4)], axis=0)
        term = dot(left, right, ((0,), (0,)))
        if part == 0:
            grad_ref[...] = term
        else:
            grad_ref[...] += term
    value = grad_ref[...]
    square = jnp.sum(jnp.sum(value * value, axis=0, keepdims=True), axis=1, keepdims=True)
    lane = lax.broadcasted_iota(jnp.int32, (8, 128), 1)
    pair = jnp.where(lane == 0, square, jnp.where(lane == 1, loss_ref[...], 0.0))
    for i in range(32):
        pair_ref[i * 8 : (i + 1) * 8] = pair


def update_kernel(
    pair_ref, grad_ref, weight_ref, first_ref, second_ref,
    new_weight_ref, new_first_ref, new_second_ref, loss_ref,
):
    total = jnp.sum(pair_ref[...], axis=0, keepdims=True)
    norm = jnp.sqrt(total[:, 0:1]) + 1e-06
    clipped = grad_ref[...] * jnp.minimum(1.0, D / norm)
    new_first = BETA_ONE * first_ref[...] + (1.0 - BETA_ONE) * clipped
    new_second = BETA_TWO * second_ref[...] + (1.0 - BETA_TWO) * clipped * clipped
    direction = new_first / CORRECT_ONE / (jnp.sqrt(new_second / CORRECT_TWO) + 1e-08)
    new_first_ref[...] = new_first
    new_second_ref[...] = new_second
    new_weight_ref[...] = (weight_ref[...].astype(F32) - LEARN_RATE * direction).astype(BF16)
    lane = lax.broadcasted_iota(jnp.int32, (1, 128), 1)
    loss_ref[0, 0] = jnp.sum(jnp.where(lane == 1, total, 0.0)) * (0.5 / (128 * N_REQ * D))


def in_vmem():
    return pl.BlockSpec(memory_space=pltpu.VMEM)


def in_smem():
    return pl.BlockSpec(memory_space=pltpu.SMEM)


def attend(rank, lengths, parents, queries, cache_keys, cache_values, tree_keys, tree_values):
    return pl.pallas_call(
        attend_kernel,
        out_shape=(
            jax.ShapeDtypeStruct((N_TP, 144, 2 * HEAD), BF16),
            jax.ShapeDtypeStruct((128, 128), BF16),
            jax.ShapeDtypeStruct((128, 128), BF16),
        ),
        in_specs=[in_smem(), in_smem()] + [in_vmem()] * 6,
        out_specs=(in_vmem(), in_vmem(), in_vmem()),
        scratch_shapes=[pltpu.VMEM((128, 128), F32)],
        cost_estimate=pl.CostEstimate(
            flops=2 * 2 * 16 * 256 * 256 * 128, bytes_accessed=4 << 20, transcendentals=16 * 256 * 256
        ),
        name="attend",
    )(rank, lengths, parents, queries, cache_keys, cache_values, tree_keys, tree_values)


def project(parcel, out_weight):
    return pl.pallas_call(
        project_kernel,
        grid=(4,),
        out_shape=jax.ShapeDtypeStruct((4, 4, 128, 512), BF16),
        in_specs=[
            pl.BlockSpec((N_TP, 144, 2 * HEAD), lambda p: (0, 0, 0)),
            pl.BlockSpec((2 * HEAD, 2048), lambda p: (0, p)),
        ],
        out_specs=pl.BlockSpec((4, 1, 128, 512), lambda p: (0, p, 0, 0)),
        scratch_shapes=[pltpu.VMEM((128, 2 * HEAD), BF16)],
        cost_estimate=pl.CostEstimate(
            flops=2 * 128 * 256 * 8192, bytes_accessed=7 << 20, transcendentals=0
        ),
        name="project",
    )(parcel, out_weight)


def fold(rank, along):
    return pl.pallas_call(
        fold_kernel,
        out_shape=(jax.ShapeDtypeStruct((128, 512), BF16),) * 4,
        in_specs=[in_smem(), in_vmem()],
        out_specs=(in_vmem(),) * 4,
        cost_estimate=pl.CostEstimate(
            flops=16 * 128 * 512, bytes_accessed=5 << 19, transcendentals=0
        ),
        name="fold",
    )(rank, along)


def settle(rank, terms, residual, gain, prev):
    whole = pl.BlockSpec((128, 512), lambda p, at: (0, 0))
    return pl.pallas_call(
        settle_kernel,
        grid_spec=pltpu.PrefetchScalarGridSpec(
            num_scalar_prefetch=1,
            grid=(1,),
            in_specs=[whole] * 5
            + [
                pl.BlockSpec((1, 1, 512), lambda p, at: (at[0], 0, 0)),
                pl.BlockSpec((4, 512), lambda p, at: (0, at[0])),
            ],
            out_specs=[whole] * 3,
        ),
        out_shape=(
            jax.ShapeDtypeStruct((128, 512), F32),
            jax.ShapeDtypeStruct((128, 512), BF16),
            jax.ShapeDtypeStruct((128, 512), BF16),
        ),
        cost_estimate=pl.CostEstimate(
            flops=128 * 512 * 8, bytes_accessed=2 << 20, transcendentals=0
        ),
        name="settle",
    )(rank, *terms, residual, gain, prev)


def predict(source, rank, lengths, leaf, far_own, far, mixed, gain, prev, reach, pick, all_weight):
    return pl.pallas_call(
        predict_kernel,
        out_shape=(
            jax.ShapeDtypeStruct((128, 512), BF16),
            jax.ShapeDtypeStruct((128, 512), BF16),
            jax.ShapeDtypeStruct((8, 128), F32),
        ),
        in_specs=[in_smem()] * 4
        + [pl.BlockSpec(memory_space=pl.ANY)] * 2
        + [in_vmem()] * 5
        + [pl.BlockSpec(memory_space=pl.ANY)] * 16,
        out_specs=(in_vmem(),) * 3,
        scratch_shapes=[
            pltpu.VMEM((128, 128), F32),
            pltpu.VMEM((128, 512), F32),
            pltpu.VMEM((16, 2, 256, 512), BF16),
            pltpu.SemaphoreType.DMA((16,)),
            pltpu.VMEM((4, 4, 128, 512), BF16),
            pltpu.SemaphoreType.DMA((2,)),
        ],
        compiler_params=pltpu.CompilerParams(vmem_limit_bytes=32 << 20),
        cost_estimate=pl.CostEstimate(
            flops=2 * 128 * 8192 * 512, bytes_accessed=13 << 20, transcendentals=0
        ),
        name="predict",
    )(source, rank, lengths, leaf, far_own, far, mixed, gain, prev, reach, pick, *all_weight)


def differentiate(place, columns, errors, loss):
    return pl.pallas_call(
        differentiate_kernel,
        out_shape=(
            jax.ShapeDtypeStruct((512, 512), F32),
            jax.ShapeDtypeStruct((N_REQ * N_TP, 128), F32),
        ),
        in_specs=[in_smem()] + [in_vmem()] * 6,
        out_specs=(in_vmem(), in_vmem()),
        cost_estimate=pl.CostEstimate(
            flops=2 * 2048 * 512 * 512, bytes_accessed=5 << 20, transcendentals=0
        ),
        name="differentiate",
    )(place, columns, *errors, loss)


def update(pair, gradient, weight, first, second):
    part = pl.BlockSpec((128, 512), lambda p: (p, 0))
    return pl.pallas_call(
        update_kernel,
        grid=(4,),
        out_shape=(
            jax.ShapeDtypeStruct((512, 512), BF16),
            jax.ShapeDtypeStruct((512, 512), F32),
            jax.ShapeDtypeStruct((512, 512), F32),
            jax.ShapeDtypeStruct((1, 1), F32),
        ),
        in_specs=[pl.BlockSpec((N_REQ * N_TP, 128), lambda p: (0, 0))] + [part] * 4,
        out_specs=(part, part, part, in_smem()),
        cost_estimate=pl.CostEstimate(
            flops=20 * 512 * 512, bytes_accessed=6 << 20, transcendentals=512 * 512
        ),
        name="update",
    )(pair, gradient, weight, first, second)


def body(
    queries,
    cache_keys,
    cache_values,
    tree_keys,
    tree_values,
    parents,
    lengths,
    accepted_leaf,
    residual,
    norm_gain,
    out_weight,
    prev_feature,
    draft_weight,
    first_moment,
    second_moment,
):
    requests = queries.shape[0]
    rows = requests * NODES
    tp_rank = lax.axis_index(TP)
    rank = tp_rank.reshape(1)
    block = residual.shape[2]
    gain = norm_gain.reshape(N_TP, 1, block)
    zh, y, c = lax.axis_index("zh"), lax.axis_index("y"), lax.axis_index("c")
    piece = jnp.arange(N_REQ, dtype=jnp.int32)
    source = (
        ((zh + piece % 2) % 2) * 8 + ((y + 4 - (piece // 2) % 4) % 4) * 2 + (c + piece // 8) % 2
    )
    place = (source % 4) * 4 + (lax.axis_index("zl") + 4 - source // 4) % 4

    parcel, reach, pick = attend(
        rank, lengths, parents, queries, cache_keys, cache_values, tree_keys, tree_values
    )
    parcel = exchange(parcel, TP)
    half = draft_weight.shape[0] // 2
    parcel, upper, lower = lax.optimization_barrier(
        (parcel, draft_weight[:half], draft_weight[half:])
    )
    upper = passed(upper, "zh", 2)
    lower = passed(lower, "zh", 2)
    upper = jnp.stack(upper)
    upper = passed(upper, "y", 4)

    partial_value = project(parcel, out_weight)
    along_x = exchange(partial_value, "x")
    other_upper = [lax.ppermute(part, "c", turn(2, 1)) for part in upper]
    lower = jnp.stack(lower)
    lower = passed(lower, "y", 4)
    terms = list(fold(rank, along_x))
    terms[1:] = [lax.ppermute(terms[step], "zl", turn(4, step)) for step in (1, 2, 3)]
    mixed, near, table = settle(rank, terms, residual.reshape(rows, block), gain, prev_feature)

    far = passed(near, "zl", 4)[1:]
    far_own = spread(near[None], "x", 4)
    far = jnp.stack(far)
    far = spread(far, "x", 4).reshape(4, 3, rows, block)
    swapped = lax.ppermute(
        table, REQ + TP, [(i * N_TP + j, j * N_TP + i) for i in range(16) for j in range(16)]
    )
    other_lower = [lax.ppermute(part, "c", turn(2, 1)) for part in lower]
    columns = turns(swapped, "zl", 4)
    own_features, scaled_err, loss = predict(
        source,
        rank,
        lengths,
        accepted_leaf,
        far_own,
        far,
        mixed,
        gain,
        prev_feature,
        reach,
        pick,
        upper + other_upper + lower + other_lower,
    )
    columns, scaled_err = lax.optimization_barrier((columns, scaled_err))
    columns = spread(columns, "x", 4).reshape(N_REQ, rows, block)
    far_err = lax.ppermute(scaled_err, "zh", turn(2, 1))
    err = passed(scaled_err, "y", 4)
    far_err = passed(far_err, "y", 4)
    err, far_err = jnp.stack(err), jnp.stack(far_err)
    errors = [err, far_err] + [lax.ppermute(part, "c", turn(2, 1)) for part in (err, far_err)]
    gradient, pair = differentiate(place, columns, errors, loss)
    pair = exchange(pair, REQ + TP)
    new_weight, new_first, new_second, draft_loss = update(
        pair, gradient, draft_weight, first_moment, second_moment
    )
    return (
        own_features.reshape(requests, NODES, block),
        new_weight,
        new_first,
        new_second,
        draft_loss.reshape(()),
    )


def solution(mesh):
    fine = Mesh(mesh.devices.reshape(2, 4, 2, 4, 4), REQ + TP)
    placed = (
        P(REQ, None, None),
        P(REQ, TP, None),
        P(REQ, TP, None),
        P(REQ, TP, None),
        P(REQ, TP, None),
        P(REQ, None),
        P(REQ),
        P(REQ),
        P(REQ, None, TP),
        P(),
        P(TP, None),
        P(REQ, None),
        P(REQ, TP),
        P(REQ, TP),
        P(REQ, TP),
    )

    return jax.shard_map(
        body,
        mesh=fine,
        in_specs=placed,
        out_specs=(P(REQ, None, TP), P(REQ, TP), P(REQ, TP), P(REQ, TP), P()),
        check_vma=False,
    )
```

```python
import math

import jax
import jax.numpy as jnp
from jax import lax
from jax.experimental import pallas as pl
from jax.experimental.pallas import tpu as pltpu
from jax.sharding import Mesh
from jax.sharding import PartitionSpec as P

HEADS = 32
KV_HEADS = 4
HEAD = 128
NODES = 32
CACHE = 4096
D = 8192
N_TP = 16
N_REQ = 16

NEG_FILL = -1e30
NORM_EPSILON = 1e-06
BETA_ONE = 0.9
BETA_TWO = 0.95
CORRECT_ONE = 1.0 - 0.9**10
CORRECT_TWO = 1.0 - 0.95**10
LEARN_RATE = 0.001


REQ = ("zh", "y", "c")
TP = ("zl", "x")
F32 = jnp.float32
BF16 = jnp.bfloat16


def exchange(value, axis):
    return lax.all_to_all(value, axis, 0, 0, tiled=True)


def spread(value, axis, count):
    wide = jnp.broadcast_to(value[None], (count, *value.shape))
    return exchange(wide.reshape(count * value.shape[0], *value.shape[1:]), axis)


def turn(count, step):
    return [(i, (i + step) % count) for i in range(count)]


def passed(value, axis, count):
    return [value] + [lax.ppermute(value, axis, turn(count, step)) for step in range(1, count)]


def turns(value, axis, count):
    return jnp.stack(passed(value, axis, count))


def dot(left, right, dims, **kwargs):
    return lax.dot_general(left, right, (dims, ((), ())), preferred_element_type=F32, **kwargs)


def same_request(width=128):
    row = lax.broadcasted_iota(jnp.int32, (128, width), 0)
    lane = lax.broadcasted_iota(jnp.int32, (128, width), 1)
    return row, lane


def attend_kernel(
    rank_ref, len_ref, par_ref, q_ref, ck_ref, cv_ref, tk_ref, tv_ref,
    out_ref, reach_ref, pick_ref, stat_ref,
):
    r = pl.program_id(0)
    rank = rank_ref[0]

    @pl.when(r == 0)
    def trees():
        row, lane = same_request()
        base = (lane // NODES) * NODES
        tile = jnp.where(
            lax.broadcasted_iota(jnp.int32, (NODES, 128), 0)
            == lax.broadcasted_iota(jnp.int32, (NODES, 128), 1) % NODES,
            1.0,
            0.0,
        )
        wide = dot(par_ref[...].astype(F32).astype(BF16), tile.astype(BF16), ((1,), (0,)))
        lane_request = lax.broadcasted_iota(jnp.int32, (1, 128), 1) // NODES
        parent = wide[0:1]
        for r in range(1, 4):
            parent = jnp.where(lane_request == r, wide[r : r + 1], parent)
        parent = parent.astype(jnp.int32)
        rooted = jnp.where(parent < 0, NODES - 1, parent)
        pick_ref[...] = jnp.where(row == base + rooted, 1.0, 0.0).astype(BF16)
        up = jnp.where(row == base + parent, jnp.where(parent >= 0, 1.0, 0.0), 0.0)
        reach = (jnp.where(row == lane, 1.0, 0.0) + up).astype(BF16)
        for _ in range((NODES - 1).bit_length()):
            reach = jnp.minimum(dot(reach, reach, ((1,), (0,))), 1.0).astype(BF16)
        reach_ref[...] = reach
        own = jnp.where(row % NODES == 2 * rank + lane, jnp.where(lane < 2, 1.0, 0.0), 0.0)
        stat_ref[...] = dot(reach, own.astype(BF16), ((0,), (0,)))

    scale = 1.0 / math.sqrt(HEAD)
    span = ck_ref.shape[1]
    slot = lax.broadcasted_iota(jnp.int32, (256, span), 1) + rank * span
    wide_lane = lax.broadcasted_iota(jnp.int32, (NODES, 128), 1)

    own_rows = pl.ds(pl.multiple_of(r * NODES, NODES), NODES)
    live = slot < len_ref[r]
    seen = stat_ref[own_rows, :][:, : tk_ref.shape[1]]
    seen = jnp.concatenate([seen] * 8, axis=0) > 0.5
    stats = jnp.zeros((NODES, 128), F32)
    for k in range(KV_HEADS):
        head = slice(k * HEAD, (k + 1) * HEAD)
        query = jnp.concatenate(
            [q_ref[0, :, (k * 8 + g) * HEAD : (k * 8 + g + 1) * HEAD] for g in range(8)], axis=0
        )
        scores = dot(query, ck_ref[0, :, head], ((1,), (1,))) * scale
        tree = dot(query, tk_ref[0, :, head], ((1,), (1,))) * scale
        scores = jnp.where(live, scores, NEG_FILL)
        tree = jnp.where(seen, tree, NEG_FILL)
        top = jnp.maximum(
            jnp.max(scores, axis=1, keepdims=True), jnp.max(tree, axis=1, keepdims=True)
        )
        top = jnp.maximum(top, 0.5 * NEG_FILL).astype(BF16).astype(F32)
        probs = jnp.exp(scores - top).astype(BF16)
        tree = jnp.exp(tree - top).astype(BF16)
        total = jnp.sum(probs.astype(F32), axis=1, keepdims=True) + jnp.sum(
            tree.astype(F32), axis=1, keepdims=True
        )
        high = total.astype(BF16).astype(F32)
        low = total - high
        value = dot(probs, cv_ref[0, :, head], ((1,), (0,))) + dot(
            tree, tv_ref[0, :, head], ((1,), (0,))
        )
        value = value.astype(BF16)
        for g in range(8):
            h = k * 8 + g
            part = slice(g * NODES, (g + 1) * NODES)
            out_ref[h // 2, own_rows, (h % 2) * HEAD : (h % 2 + 1) * HEAD] = value[part]
            for at, column in enumerate((top, high, low)):
                stats = jnp.where(wide_lane == h * 4 + at, column[part], stats)
    stat_ref[own_rows, :] = stats

    @pl.when(r == 3)
    def statistics():
        turned = jnp.transpose(stat_ref[...])
        empty = jnp.zeros((8, 128), F32)
        blank = jnp.zeros((16, 128), BF16)
        for owner in range(N_TP):
            block = jnp.concatenate([turned[owner * 8 : (owner + 1) * 8], empty], axis=0)
            out_ref[owner, 128:144, 0:128] = block.astype(BF16)
            out_ref[owner, 128:144, 128:256] = blank


def project_kernel(parcel_ref, weight_ref, out_ref, att_ref):
    @pl.when(pl.program_id(0) == 0)
    def join():
        stats = jnp.concatenate(
            [parcel_ref[src, 128:144, 0:128].astype(F32)[0:8] for src in range(N_TP)], axis=0
        )
        total = pltpu.roll(stats, 127, 0) + pltpu.roll(stats, 126, 0)
        stats = stats.reshape(N_TP, 8, 128)
        factor = jnp.exp(stats - jnp.max(stats, axis=0, keepdims=True))
        share = factor / jnp.sum(factor * total.reshape(N_TP, 8, 128), axis=0, keepdims=True)
        share = jnp.transpose(share.reshape(128, 128))
        for side in range(2):
            cols = slice(side * HEAD, (side + 1) * HEAD)
            joined = jnp.zeros((128, HEAD), F32)
            for src in range(N_TP):
                at = src * 8 + side * 4
                joined = joined + parcel_ref[src, 0:128, cols].astype(F32) * share[:, at : at + 1]
            att_ref[:, cols] = joined.astype(BF16)

    for x in range(4):
        cols = slice(x * 512, (x + 1) * 512)
        out_ref[x, 0] = dot(att_ref[...], weight_ref[:, cols], ((1,), (0,))).astype(BF16)


def fold_kernel(rank_ref, along_ref, *out_refs):
    for step in range(4):
        zl = lax.rem(rank_ref[0] // 4 + step, 4)
        total = along_ref[0, zl].astype(F32)
        for x in range(1, 4):
            total = total + along_ref[x, zl].astype(F32)
        out_refs[step][...] = total.astype(BF16)


def settle_kernel(
    rank_ref, own_ref, one_ref, two_ref, three_ref, residual_ref, gain_ref, prev_ref,
    mixed_ref, near_ref, table_ref,
):
    total = own_ref[...].astype(F32) + one_ref[...].astype(F32)
    total = total + (two_ref[...].astype(F32) + three_ref[...].astype(F32))
    mixed = residual_ref[...].astype(F32) + total
    mixed_ref[...] = mixed
    near_ref[...] = mixed.astype(BF16)
    scaled = mixed * gain_ref[0]
    node = lax.broadcasted_iota(jnp.int32, (NODES, 1), 0)
    prev = prev_ref[...].astype(F32)
    for r in range(4):
        part = slice(r * NODES, (r + 1) * NODES)
        table_ref[part] = jnp.where(node == NODES - 1, prev[r : r + 1], scaled[part]).astype(BF16)


def predict_kernel(
    source_ref, rank_ref, len_ref, leaf_ref, far_own_ref, far_rest_ref, mixed_ref, gain_ref, prev_ref, reach_ref,
    pick_ref, *refs,
):
    weight_refs = refs[:16]
    own_ref, err_ref, loss_ref, scale_ref, ahead_ref, weight_ref, sem_ref, far_ref, far_sem = refs[16:]
    own_load = pltpu.make_async_copy(far_own_ref, far_ref.at[:, 0], far_sem.at[0])
    rest_load = pltpu.make_async_copy(far_rest_ref, far_ref.at[:, 1:4], far_sem.at[1])
    own_load.start()
    rest_load.start()
    loads = [pltpu.make_async_copy(weight_refs[i], weight_ref.at[i], sem_ref.at[i]) for i in range(16)]
    for load in loads:
        load.start()
    square = jnp.zeros((128, 128), F32)
    own_load.wait()
    for k in range(4):
        if k == 1:
            rest_load.wait()
        for x in range(4):
            part = far_ref[x, k].astype(F32)
            part = part * part
            for i in range(4):
                square = square + part[:, i * 128 : (i + 1) * 128]
    square = jnp.sum(square, axis=1, keepdims=True)
    scale = lax.rsqrt(square / D + NORM_EPSILON)
    scale_ref[...] = jnp.broadcast_to(scale, (128, 128))
    own_ref[...] = (mixed_ref[...] * scale * gain_ref[rank_ref[0]]).astype(BF16)

    node = lax.broadcasted_iota(jnp.int32, (NODES, 1), 0)
    for part in range(8):
        loads[part].wait()
        loads[part + 8].wait()
        total = jnp.zeros((128, 512), F32)
        for i in range(2):
            p = source_ref[part * 2 + i]
            back = lax.rem(rank_ref[0] // 4 + 4 - p // 4, 4)
            block = far_ref[lax.rem(p, 4), back].astype(F32) * scale_ref[:, 0:1] * gain_ref[p]
            prev = prev_ref[:, pl.ds(pl.multiple_of(p * 512, 512), 512)].astype(F32)
            block = jnp.concatenate(
                [
                    jnp.where(node == NODES - 1, prev[r : r + 1], block[r * NODES : (r + 1) * NODES])
                    for r in range(4)
                ],
                axis=0,
            ).astype(BF16)
            total = total + dot(block[:, :256], weight_ref[part, i], ((1,), (0,)))
            total = total + dot(block[:, 256:], weight_ref[part + 8, i], ((1,), (0,)))
        if part == 0:
            ahead_ref[...] = total
        else:
            ahead_ref[...] += total

    row, lane = same_request()
    accepted = []
    for r in range(4):
        part = slice(r * NODES, (r + 1) * NODES)
        path = jnp.where(lane[part] == leaf_ref[r] + r * NODES, reach_ref[part].astype(F32), 0.0)
        path = jnp.sum(path, axis=1, keepdims=True)
        accepted.append((1.0 + 3.0 * path) * (0.5 + len_ref[r].astype(F32) / CACHE))
    weights = jnp.concatenate(accepted, axis=0)
    pick = pick_ref[...].astype(F32)
    predicted = dot(pick, ahead_ref[...], ((0,), (0,)), precision=lax.Precision.HIGHEST)
    error = predicted - own_ref[...].astype(F32)
    weighted = weights * error
    joined = dot(pick, weighted, ((1,), (0,)), precision=lax.Precision.HIGHEST)
    scale = jnp.where(row[:, 0:1] % NODES == NODES - 1, 1.0, scale_ref[:, 0:1])
    err_ref[...] = (joined * scale).astype(BF16)
    loss = jnp.sum(jnp.sum(weighted * error, axis=0, keepdims=True), axis=1, keepdims=True)
    loss_ref[...] = jnp.broadcast_to(loss, (8, 128))


def differentiate_kernel(place_ref, column_ref, e0_ref, e1_ref, e2_ref, e3_ref, loss_ref, grad_ref, pair_ref):
    for part, err_ref in enumerate((e0_ref, e1_ref, e2_ref, e3_ref)):
        first = (part // 2) * 8 + part % 2
        left = jnp.concatenate([column_ref[place_ref[first + 2 * i]] for i in range(4)], axis=0)
        right = jnp.concatenate([err_ref[i] for i in range(4)], axis=0)
        term = dot(left, right, ((0,), (0,)))
        if part == 0:
            grad_ref[...] = term
        else:
            grad_ref[...] += term
    value = grad_ref[...]
    square = jnp.sum(jnp.sum(value * value, axis=0, keepdims=True), axis=1, keepdims=True)
    lane = lax.broadcasted_iota(jnp.int32, (8, 128), 1)
    pair = jnp.where(lane == 0, square, jnp.where(lane == 1, loss_ref[...], 0.0))
    for i in range(32):
        pair_ref[i * 8 : (i + 1) * 8] = pair


def update_kernel(
    pair_ref, grad_ref, weight_ref, first_ref, second_ref,
    new_weight_ref, new_first_ref, new_second_ref, loss_ref,
):
    total = jnp.sum(pair_ref[...], axis=0, keepdims=True)
    norm = jnp.sqrt(total[:, 0:1]) + 1e-06
    clipped = grad_ref[...] * jnp.minimum(1.0, D / norm)
    new_first = BETA_ONE * first_ref[...] + (1.0 - BETA_ONE) * clipped
    new_second = BETA_TWO * second_ref[...] + (1.0 - BETA_TWO) * clipped * clipped
    direction = new_first / CORRECT_ONE / (jnp.sqrt(new_second / CORRECT_TWO) + 1e-08)
    new_first_ref[...] = new_first
    new_second_ref[...] = new_second
    new_weight_ref[...] = (weight_ref[...].astype(F32) - LEARN_RATE * direction).astype(BF16)
    lane = lax.broadcasted_iota(jnp.int32, (1, 128), 1)
    loss_ref[0, 0] = jnp.sum(jnp.where(lane == 1, total, 0.0)) * (0.5 / (128 * N_REQ * D))


def in_vmem():
    return pl.BlockSpec(memory_space=pltpu.VMEM)


def in_smem():
    return pl.BlockSpec(memory_space=pltpu.SMEM)


def attend(rank, lengths, parents, queries, cache_keys, cache_values, tree_keys, tree_values):
    return pl.pallas_call(
        attend_kernel,
        out_shape=(
            jax.ShapeDtypeStruct((N_TP, 144, 2 * HEAD), BF16),
            jax.ShapeDtypeStruct((128, 128), BF16),
            jax.ShapeDtypeStruct((128, 128), BF16),
        ),
        grid=(4,),
        in_specs=[
            in_smem(),
            in_smem(),
            pl.BlockSpec((4, NODES), lambda r: (0, 0)),
            pl.BlockSpec((1, NODES, HEADS * HEAD), lambda r: (r, 0, 0)),
        ]
        + [pl.BlockSpec((1, 256, KV_HEADS * HEAD), lambda r: (r, 0, 0))] * 2
        + [pl.BlockSpec((1, 2, KV_HEADS * HEAD), lambda r: (r, 0, 0))] * 2,
        out_specs=(
            pl.BlockSpec((N_TP, 144, 2 * HEAD), lambda r: (0, 0, 0)),
            pl.BlockSpec((128, 128), lambda r: (0, 0)),
            pl.BlockSpec((128, 128), lambda r: (0, 0)),
        ),
        scratch_shapes=[pltpu.VMEM((128, 128), F32)],
        cost_estimate=pl.CostEstimate(
            flops=2 * 2 * 16 * 256 * 256 * 128, bytes_accessed=4 << 20, transcendentals=16 * 256 * 256
        ),
        name="attend",
    )(rank, lengths, parents, queries, cache_keys, cache_values, tree_keys, tree_values)


def project(parcel, out_weight):
    return pl.pallas_call(
        project_kernel,
        grid=(4,),
        out_shape=jax.ShapeDtypeStruct((4, 4, 128, 512), BF16),
        in_specs=[
            pl.BlockSpec((N_TP, 144, 2 * HEAD), lambda p: (0, 0, 0)),
            pl.BlockSpec((2 * HEAD, 2048), lambda p: (0, p)),
        ],
        out_specs=pl.BlockSpec((4, 1, 128, 512), lambda p: (0, p, 0, 0)),
        scratch_shapes=[pltpu.VMEM((128, 2 * HEAD), BF16)],
        cost_estimate=pl.CostEstimate(
            flops=2 * 128 * 256 * 8192, bytes_accessed=7 << 20, transcendentals=0
        ),
        name="project",
    )(parcel, out_weight)


def fold(rank, along):
    return pl.pallas_call(
        fold_kernel,
        out_shape=(jax.ShapeDtypeStruct((128, 512), BF16),) * 4,
        in_specs=[in_smem(), in_vmem()],
        out_specs=(in_vmem(),) * 4,
        cost_estimate=pl.CostEstimate(
            flops=16 * 128 * 512, bytes_accessed=5 << 19, transcendentals=0
        ),
        name="fold",
    )(rank, along)


def settle(rank, terms, residual, gain, prev):
    whole = pl.BlockSpec((128, 512), lambda p, at: (0, 0))
    return pl.pallas_call(
        settle_kernel,
        grid_spec=pltpu.PrefetchScalarGridSpec(
            num_scalar_prefetch=1,
            grid=(1,),
            in_specs=[whole] * 5
            + [
                pl.BlockSpec((1, 1, 512), lambda p, at: (at[0], 0, 0)),
                pl.BlockSpec((4, 512), lambda p, at: (0, at[0])),
            ],
            out_specs=[whole] * 3,
        ),
        out_shape=(
            jax.ShapeDtypeStruct((128, 512), F32),
            jax.ShapeDtypeStruct((128, 512), BF16),
            jax.ShapeDtypeStruct((128, 512), BF16),
        ),
        cost_estimate=pl.CostEstimate(
            flops=128 * 512 * 8, bytes_accessed=2 << 20, transcendentals=0
        ),
        name="settle",
    )(rank, *terms, residual, gain, prev)


def predict(source, rank, lengths, leaf, far_own, far, mixed, gain, prev, reach, pick, all_weight):
    return pl.pallas_call(
        predict_kernel,
        out_shape=(
            jax.ShapeDtypeStruct((128, 512), BF16),
            jax.ShapeDtypeStruct((128, 512), BF16),
            jax.ShapeDtypeStruct((8, 128), F32),
        ),
        in_specs=[in_smem()] * 4
        + [pl.BlockSpec(memory_space=pl.ANY)] * 2
        + [in_vmem()] * 5
        + [pl.BlockSpec(memory_space=pl.ANY)] * 16,
        out_specs=(in_vmem(),) * 3,
        scratch_shapes=[
            pltpu.VMEM((128, 128), F32),
            pltpu.VMEM((128, 512), F32),
            pltpu.VMEM((16, 2, 256, 512), BF16),
            pltpu.SemaphoreType.DMA((16,)),
            pltpu.VMEM((4, 4, 128, 512), BF16),
            pltpu.SemaphoreType.DMA((2,)),
        ],
        compiler_params=pltpu.CompilerParams(vmem_limit_bytes=32 << 20),
        cost_estimate=pl.CostEstimate(
            flops=2 * 128 * 8192 * 512, bytes_accessed=13 << 20, transcendentals=0
        ),
        name="predict",
    )(source, rank, lengths, leaf, far_own, far, mixed, gain, prev, reach, pick, *all_weight)


def differentiate(place, columns, errors, loss):
    return pl.pallas_call(
        differentiate_kernel,
        out_shape=(
            jax.ShapeDtypeStruct((512, 512), F32),
            jax.ShapeDtypeStruct((N_REQ * N_TP, 128), F32),
        ),
        in_specs=[in_smem()] + [in_vmem()] * 6,
        out_specs=(in_vmem(), in_vmem()),
        cost_estimate=pl.CostEstimate(
            flops=2 * 2048 * 512 * 512, bytes_accessed=5 << 20, transcendentals=0
        ),
        name="differentiate",
    )(place, columns, *errors, loss)


def update(pair, gradient, weight, first, second):
    part = pl.BlockSpec((128, 512), lambda p: (p, 0))
    return pl.pallas_call(
        update_kernel,
        grid=(4,),
        out_shape=(
            jax.ShapeDtypeStruct((512, 512), BF16),
            jax.ShapeDtypeStruct((512, 512), F32),
            jax.ShapeDtypeStruct((512, 512), F32),
            jax.ShapeDtypeStruct((1, 1), F32),
        ),
        in_specs=[pl.BlockSpec((N_REQ * N_TP, 128), lambda p: (0, 0))] + [part] * 4,
        out_specs=(part, part, part, in_smem()),
        cost_estimate=pl.CostEstimate(
            flops=20 * 512 * 512, bytes_accessed=6 << 20, transcendentals=512 * 512
        ),
        name="update",
    )(pair, gradient, weight, first, second)


def body(
    queries,
    cache_keys,
    cache_values,
    tree_keys,
    tree_values,
    parents,
    lengths,
    accepted_leaf,
    residual,
    norm_gain,
    out_weight,
    prev_feature,
    draft_weight,
    first_moment,
    second_moment,
):
    requests = queries.shape[0]
    rows = requests * NODES
    tp_rank = lax.axis_index(TP)
    rank = tp_rank.reshape(1)
    block = residual.shape[2]
    gain = norm_gain.reshape(N_TP, 1, block)
    zh, y, c = lax.axis_index("zh"), lax.axis_index("y"), lax.axis_index("c")
    piece = jnp.arange(N_REQ, dtype=jnp.int32)
    source = (
        ((zh + piece % 2) % 2) * 8 + ((y + 4 - (piece // 2) % 4) % 4) * 2 + (c + piece // 8) % 2
    )
    place = (source % 4) * 4 + (lax.axis_index("zl") + 4 - source // 4) % 4

    parcel, reach, pick = attend(
        rank, lengths, parents, queries, cache_keys, cache_values, tree_keys, tree_values
    )
    parcel = exchange(parcel, TP)
    half = draft_weight.shape[0] // 2
    parcel, upper, lower = lax.optimization_barrier(
        (parcel, draft_weight[:half], draft_weight[half:])
    )
    upper = passed(upper, "zh", 2)
    lower = passed(lower, "zh", 2)
    upper = jnp.stack(upper)
    upper = passed(upper, "y", 4)

    partial_value = project(parcel, out_weight)
    along_x = exchange(partial_value, "x")
    other_upper = [lax.ppermute(part, "c", turn(2, 1)) for part in upper]
    lower = jnp.stack(lower)
    lower = passed(lower, "y", 4)
    terms = list(fold(rank, along_x))
    terms[1:] = [lax.ppermute(terms[step], "zl", turn(4, step)) for step in (1, 2, 3)]
    mixed, near, table = settle(rank, terms, residual.reshape(rows, block), gain, prev_feature)

    far = passed(near, "zl", 4)[1:]
    far_own = spread(near[None], "x", 4)
    far = jnp.stack(far)
    far = spread(far, "x", 4).reshape(4, 3, rows, block)
    swapped = lax.ppermute(
        table, REQ + TP, [(i * N_TP + j, j * N_TP + i) for i in range(16) for j in range(16)]
    )
    other_lower = [lax.ppermute(part, "c", turn(2, 1)) for part in lower]
    columns = turns(swapped, "zl", 4)
    columns = spread(columns, "x", 4).reshape(N_REQ, rows, block)
    own_features, scaled_err, loss = predict(
        source,
        rank,
        lengths,
        accepted_leaf,
        far_own,
        far,
        mixed,
        gain,
        prev_feature,
        reach,
        pick,
        upper + other_upper + lower + other_lower,
    )
    far_err = lax.ppermute(scaled_err, "zh", turn(2, 1))
    err = passed(scaled_err, "y", 4)
    far_err = passed(far_err, "y", 4)
    err, far_err = jnp.stack(err), jnp.stack(far_err)
    errors = [err, far_err] + [lax.ppermute(part, "c", turn(2, 1)) for part in (err, far_err)]
    gradient, pair = differentiate(place, columns, errors, loss)
    pair = exchange(pair, REQ + TP)
    new_weight, new_first, new_second, draft_loss = update(
        pair, gradient, draft_weight, first_moment, second_moment
    )
    return (
        own_features.reshape(requests, NODES, block),
        new_weight,
        new_first,
        new_second,
        draft_loss.reshape(()),
    )


def solution(mesh):
    fine = Mesh(mesh.devices.reshape(2, 4, 2, 4, 4), REQ + TP)
    placed = (
        P(REQ, None, None),
        P(REQ, TP, None),
        P(REQ, TP, None),
        P(REQ, TP, None),
        P(REQ, TP, None),
        P(REQ, None),
        P(REQ),
        P(REQ),
        P(REQ, None, TP),
        P(),
        P(TP, None),
        P(REQ, None),
        P(REQ, TP),
        P(REQ, TP),
        P(REQ, TP),
    )

    return jax.shard_map(
        body,
        mesh=fine,
        in_specs=placed,
        out_specs=(P(REQ, None, TP), P(REQ, TP), P(REQ, TP), P(REQ, TP), P()),
        check_vma=False,
    )
```

```python
import math

import jax
import jax.numpy as jnp
from jax import lax
from jax.experimental import pallas as pl
from jax.experimental.pallas import tpu as pltpu
from jax.sharding import Mesh
from jax.sharding import PartitionSpec as P

HEADS = 32
KV_HEADS = 4
HEAD = 128
NODES = 32
CACHE = 4096
D = 8192
N_TP = 16
N_REQ = 16

NEG_FILL = -1e30
NORM_EPSILON = 1e-06
BETA_ONE = 0.9
BETA_TWO = 0.95
CORRECT_ONE = 1.0 - 0.9**10
CORRECT_TWO = 1.0 - 0.95**10
LEARN_RATE = 0.001


REQ = ("zh", "y", "c")
TP = ("zl", "x")
F32 = jnp.float32
BF16 = jnp.bfloat16


def exchange(value, axis):
    return lax.all_to_all(value, axis, 0, 0, tiled=True)


def spread(value, axis, count):
    wide = jnp.broadcast_to(value[None], (count, *value.shape))
    return exchange(wide.reshape(count * value.shape[0], *value.shape[1:]), axis)


def turn(count, step):
    return [(i, (i + step) % count) for i in range(count)]


def passed(value, axis, count):
    return [value] + [lax.ppermute(value, axis, turn(count, step)) for step in range(1, count)]


def dot(left, right, dims, **kwargs):
    return lax.dot_general(left, right, (dims, ((), ())), preferred_element_type=F32, **kwargs)


def same_request(width=128):
    row = lax.broadcasted_iota(jnp.int32, (128, width), 0)
    lane = lax.broadcasted_iota(jnp.int32, (128, width), 1)
    return row, lane


def attend_kernel(
    rank_ref, len_ref, par_ref, q_ref, ck_ref, cv_ref, tk_ref, tv_ref,
    out_ref, reach_ref, pick_ref, stat_ref,
):
    r = pl.program_id(0)
    rank = rank_ref[0]

    @pl.when(r == 0)
    def trees():
        row, lane = same_request()
        base = (lane // NODES) * NODES
        tile = jnp.where(
            lax.broadcasted_iota(jnp.int32, (NODES, 128), 0)
            == lax.broadcasted_iota(jnp.int32, (NODES, 128), 1) % NODES,
            1.0,
            0.0,
        )
        wide = dot(par_ref[...].astype(F32).astype(BF16), tile.astype(BF16), ((1,), (0,)))
        lane_request = lax.broadcasted_iota(jnp.int32, (1, 128), 1) // NODES
        parent = wide[0:1]
        for r in range(1, 4):
            parent = jnp.where(lane_request == r, wide[r : r + 1], parent)
        parent = parent.astype(jnp.int32)
        rooted = jnp.where(parent < 0, NODES - 1, parent)
        pick_ref[...] = jnp.where(row == base + rooted, 1.0, 0.0).astype(BF16)
        up = jnp.where(row == base + parent, jnp.where(parent >= 0, 1.0, 0.0), 0.0)
        reach = (jnp.where(row == lane, 1.0, 0.0) + up).astype(BF16)
        for _ in range((NODES - 1).bit_length()):
            reach = jnp.minimum(dot(reach, reach, ((1,), (0,))), 1.0).astype(BF16)
        reach_ref[...] = reach
        own = jnp.where(row % NODES == 2 * rank + lane, jnp.where(lane < 2, 1.0, 0.0), 0.0)
        stat_ref[...] = dot(reach, own.astype(BF16), ((0,), (0,)))

    scale = 1.0 / math.sqrt(HEAD)
    span = ck_ref.shape[1]
    slot = lax.broadcasted_iota(jnp.int32, (256, span), 1) + rank * span
    wide_lane = lax.broadcasted_iota(jnp.int32, (NODES, 128), 1)

    own_rows = pl.ds(pl.multiple_of(r * NODES, NODES), NODES)
    live = slot < len_ref[r]
    seen = stat_ref[own_rows, :][:, : tk_ref.shape[1]]
    seen = jnp.concatenate([seen] * 8, axis=0) > 0.5
    stats = jnp.zeros((NODES, 128), F32)
    for k in range(KV_HEADS):
        head = slice(k * HEAD, (k + 1) * HEAD)
        query = jnp.concatenate(
            [q_ref[0, :, (k * 8 + g) * HEAD : (k * 8 + g + 1) * HEAD] for g in range(8)], axis=0
        )
        scores = dot(query, ck_ref[0, :, head], ((1,), (1,))) * scale
        tree = dot(query, tk_ref[0, :, head], ((1,), (1,))) * scale
        scores = jnp.where(live, scores, NEG_FILL)
        tree = jnp.where(seen, tree, NEG_FILL)
        top = jnp.maximum(
            jnp.max(scores, axis=1, keepdims=True), jnp.max(tree, axis=1, keepdims=True)
        )
        top = jnp.maximum(top, 0.5 * NEG_FILL).astype(BF16).astype(F32)
        probs = jnp.exp(scores - top).astype(BF16)
        tree = jnp.exp(tree - top).astype(BF16)
        total = jnp.sum(probs.astype(F32), axis=1, keepdims=True) + jnp.sum(
            tree.astype(F32), axis=1, keepdims=True
        )
        high = total.astype(BF16).astype(F32)
        low = total - high
        value = dot(probs, cv_ref[0, :, head], ((1,), (0,))) + dot(
            tree, tv_ref[0, :, head], ((1,), (0,))
        )
        value = value.astype(BF16)
        for g in range(8):
            h = k * 8 + g
            part = slice(g * NODES, (g + 1) * NODES)
            out_ref[h // 2, own_rows, (h % 2) * HEAD : (h % 2 + 1) * HEAD] = value[part]
            for at, column in enumerate((top, high, low)):
                stats = jnp.where(wide_lane == h * 4 + at, column[part], stats)
    stat_ref[own_rows, :] = stats

    @pl.when(r == 3)
    def statistics():
        turned = jnp.transpose(stat_ref[...])
        empty = jnp.zeros((8, 128), F32)
        blank = jnp.zeros((16, 128), BF16)
        for owner in range(N_TP):
            block = jnp.concatenate([turned[owner * 8 : (owner + 1) * 8], empty], axis=0)
            out_ref[owner, 128:144, 0:128] = block.astype(BF16)
            out_ref[owner, 128:144, 128:256] = blank


def project_kernel(from_ref, weight_ref, out_ref, att_ref, parcel_ref, sem_ref):
    @pl.when(pl.program_id(0) == 0)
    def join():
        load = pltpu.make_async_copy(from_ref, parcel_ref, sem_ref.at[0])
        load.start()
        load.wait()
        stats = jnp.concatenate(
            [parcel_ref[src, 128:144, 0:128].astype(F32)[0:8] for src in range(N_TP)], axis=0
        )
        total = pltpu.roll(stats, 127, 0) + pltpu.roll(stats, 126, 0)
        stats = stats.reshape(N_TP, 8, 128)
        factor = jnp.exp(stats - jnp.max(stats, axis=0, keepdims=True))
        share = factor / jnp.sum(factor * total.reshape(N_TP, 8, 128), axis=0, keepdims=True)
        share = jnp.transpose(share.reshape(128, 128))
        for side in range(2):
            cols = slice(side * HEAD, (side + 1) * HEAD)
            joined = jnp.zeros((128, HEAD), F32)
            for src in range(N_TP):
                at = src * 8 + side * 4
                joined = joined + parcel_ref[src, 0:128, cols].astype(F32) * share[:, at : at + 1]
            att_ref[:, cols] = joined.astype(BF16)

    for x in range(4):
        cols = slice(x * 512, (x + 1) * 512)
        out_ref[x, 0] = dot(att_ref[...], weight_ref[:, cols], ((1,), (0,))).astype(BF16)


def fold_kernel(rank_ref, from_ref, *refs):
    out_refs, (along_ref, sem_ref) = refs[:4], refs[4:]
    loads = [pltpu.make_async_copy(from_ref.at[x], along_ref.at[x], sem_ref.at[x]) for x in range(4)]
    for load in loads:
        load.start()
    for load in loads:
        load.wait()
    for step in range(4):
        zl = lax.rem(rank_ref[0] // 4 + step, 4)
        total = along_ref[0, zl].astype(F32)
        for x in range(1, 4):
            total = total + along_ref[x, zl].astype(F32)
        out_refs[step][...] = total.astype(BF16)


def settle_kernel(
    rank_ref, own_ref, one_ref, two_ref, three_ref, residual_ref, gain_ref, prev_ref,
    mixed_ref, near_ref, table_ref,
):
    total = own_ref[...].astype(F32) + one_ref[...].astype(F32)
    total = total + (two_ref[...].astype(F32) + three_ref[...].astype(F32))
    mixed = residual_ref[...].astype(F32) + total
    mixed_ref[...] = mixed
    near_ref[...] = mixed.astype(BF16)
    scaled = mixed * gain_ref[0]
    node = lax.broadcasted_iota(jnp.int32, (NODES, 1), 0)
    prev = prev_ref[...].astype(F32)
    for r in range(4):
        part = slice(r * NODES, (r + 1) * NODES)
        table_ref[part] = jnp.where(node == NODES - 1, prev[r : r + 1], scaled[part]).astype(BF16)


def predict_kernel(
    source_ref, rank_ref, len_ref, leaf_ref, far_own_ref, far_rest_ref, mixed_ref, gain_ref, prev_ref, reach_ref,
    pick_ref, *refs,
):
    weight_refs = refs[:16]
    own_ref, err_ref, loss_ref, scale_ref, ahead_ref, weight_ref, sem_ref, far_ref, far_sem = refs[16:]
    own_load = pltpu.make_async_copy(far_own_ref, far_ref.at[:, 0], far_sem.at[0])
    rest_load = pltpu.make_async_copy(far_rest_ref, far_ref.at[:, 1:4], far_sem.at[1])
    own_load.start()
    rest_load.start()
    loads = [pltpu.make_async_copy(weight_refs[i], weight_ref.at[i], sem_ref.at[i]) for i in range(16)]
    for load in loads:
        load.start()
    square = jnp.zeros((128, 128), F32)
    own_load.wait()
    for k in range(4):
        if k == 1:
            rest_load.wait()
        for x in range(4):
            part = far_ref[x, k].astype(F32)
            part = part * part
            for i in range(4):
                square = square + part[:, i * 128 : (i + 1) * 128]
    square = jnp.sum(square, axis=1, keepdims=True)
    scale = lax.rsqrt(square / D + NORM_EPSILON)
    scale_ref[...] = jnp.broadcast_to(scale, (128, 128))
    own_ref[...] = (mixed_ref[...] * scale * gain_ref[rank_ref[0]]).astype(BF16)

    node = lax.broadcasted_iota(jnp.int32, (NODES, 1), 0)
    for part in range(8):
        loads[part].wait()
        loads[part + 8].wait()
        total = jnp.zeros((128, 512), F32)
        for i in range(2):
            p = source_ref[part * 2 + i]
            back = lax.rem(rank_ref[0] // 4 + 4 - p // 4, 4)
            block = far_ref[lax.rem(p, 4), back].astype(F32) * scale_ref[:, 0:1] * gain_ref[p]
            prev = prev_ref[:, pl.ds(pl.multiple_of(p * 512, 512), 512)].astype(F32)
            block = jnp.concatenate(
                [
                    jnp.where(node == NODES - 1, prev[r : r + 1], block[r * NODES : (r + 1) * NODES])
                    for r in range(4)
                ],
                axis=0,
            ).astype(BF16)
            total = total + dot(block[:, :256], weight_ref[part, i], ((1,), (0,)))
            total = total + dot(block[:, 256:], weight_ref[part + 8, i], ((1,), (0,)))
        if part == 0:
            ahead_ref[...] = total
        else:
            ahead_ref[...] += total

    row, lane = same_request()
    accepted = []
    for r in range(4):
        part = slice(r * NODES, (r + 1) * NODES)
        path = jnp.where(lane[part] == leaf_ref[r] + r * NODES, reach_ref[part].astype(F32), 0.0)
        path = jnp.sum(path, axis=1, keepdims=True)
        accepted.append((1.0 + 3.0 * path) * (0.5 + len_ref[r].astype(F32) / CACHE))
    weights = jnp.concatenate(accepted, axis=0)
    pick = pick_ref[...].astype(F32)
    predicted = dot(pick, ahead_ref[...], ((0,), (0,)), precision=lax.Precision.HIGHEST)
    error = predicted - own_ref[...].astype(F32)
    weighted = weights * error
    joined = dot(pick, weighted, ((1,), (0,)), precision=lax.Precision.HIGHEST)
    scale = jnp.where(row[:, 0:1] % NODES == NODES - 1, 1.0, scale_ref[:, 0:1])
    err_ref[...] = (joined * scale).astype(BF16)
    loss = jnp.sum(jnp.sum(weighted * error, axis=0, keepdims=True), axis=1, keepdims=True)
    loss_ref[...] = jnp.broadcast_to(loss, (8, 128))


def differentiate_kernel(place_ref, *refs):
    loss_ref, grad_ref, pair_ref, column_ref, sem_ref = refs[8:]
    column_loads = [
        pltpu.make_async_copy(refs[i], column_ref.at[pl.ds(4 * i, 4)], sem_ref.at[i]) for i in range(4)
    ]
    for load in column_loads:
        load.start()
    for load in column_loads:
        load.wait()
    for part in range(4):
        first = (part // 2) * 8 + part % 2
        left = jnp.concatenate([column_ref[place_ref[first + 2 * i]] for i in range(4)], axis=0)
        right = jnp.concatenate([refs[4 + part][i] for i in range(4)], axis=0)
        term = dot(left, right, ((0,), (0,)))
        if part == 0:
            grad_ref[...] = term
        else:
            grad_ref[...] += term
    value = grad_ref[...]
    square = jnp.sum(jnp.sum(value * value, axis=0, keepdims=True), axis=1, keepdims=True)
    lane = lax.broadcasted_iota(jnp.int32, (8, 128), 1)
    pair = jnp.where(lane == 0, square, jnp.where(lane == 1, loss_ref[...], 0.0))
    for i in range(32):
        pair_ref[i * 8 : (i + 1) * 8] = pair


def update_kernel(
    pair_ref, grad_ref, weight_ref, first_ref, second_ref,
    new_weight_ref, new_first_ref, new_second_ref, loss_ref,
):
    total = jnp.sum(pair_ref[...], axis=0, keepdims=True)
    norm = jnp.sqrt(total[:, 0:1]) + 1e-06
    clipped = grad_ref[...] * jnp.minimum(1.0, D / norm)
    new_first = BETA_ONE * first_ref[...] + (1.0 - BETA_ONE) * clipped
    new_second = BETA_TWO * second_ref[...] + (1.0 - BETA_TWO) * clipped * clipped
    direction = new_first / CORRECT_ONE / (jnp.sqrt(new_second / CORRECT_TWO) + 1e-08)
    new_first_ref[...] = new_first
    new_second_ref[...] = new_second
    new_weight_ref[...] = (weight_ref[...].astype(F32) - LEARN_RATE * direction).astype(BF16)
    lane = lax.broadcasted_iota(jnp.int32, (1, 128), 1)
    loss_ref[0, 0] = jnp.sum(jnp.where(lane == 1, total, 0.0)) * (0.5 / (128 * N_REQ * D))


def in_vmem():
    return pl.BlockSpec(memory_space=pltpu.VMEM)


def in_smem():
    return pl.BlockSpec(memory_space=pltpu.SMEM)


def attend(rank, lengths, parents, queries, cache_keys, cache_values, tree_keys, tree_values):
    return pl.pallas_call(
        attend_kernel,
        out_shape=(
            jax.ShapeDtypeStruct((N_TP, 144, 2 * HEAD), BF16),
            jax.ShapeDtypeStruct((128, 128), BF16),
            jax.ShapeDtypeStruct((128, 128), BF16),
        ),
        grid=(4,),
        in_specs=[
            in_smem(),
            in_smem(),
            pl.BlockSpec((4, NODES), lambda r: (0, 0)),
            pl.BlockSpec((1, NODES, HEADS * HEAD), lambda r: (r, 0, 0)),
        ]
        + [pl.BlockSpec((1, 256, KV_HEADS * HEAD), lambda r: (r, 0, 0))] * 2
        + [pl.BlockSpec((1, 2, KV_HEADS * HEAD), lambda r: (r, 0, 0))] * 2,
        out_specs=(
            pl.BlockSpec((N_TP, 144, 2 * HEAD), lambda r: (0, 0, 0)),
            pl.BlockSpec((128, 128), lambda r: (0, 0)),
            pl.BlockSpec((128, 128), lambda r: (0, 0)),
        ),
        scratch_shapes=[pltpu.VMEM((128, 128), F32)],
        cost_estimate=pl.CostEstimate(
            flops=2 * 2 * 16 * 256 * 256 * 128, bytes_accessed=4 << 20, transcendentals=16 * 256 * 256
        ),
        name="attend",
    )(rank, lengths, parents, queries, cache_keys, cache_values, tree_keys, tree_values)


def project(parcel, out_weight):
    return pl.pallas_call(
        project_kernel,
        grid=(4,),
        out_shape=jax.ShapeDtypeStruct((4, 4, 128, 512), BF16),
        in_specs=[
            pl.BlockSpec(memory_space=pl.ANY),
            pl.BlockSpec((2 * HEAD, 2048), lambda p: (0, p)),
        ],
        out_specs=pl.BlockSpec((4, 1, 128, 512), lambda p: (0, p, 0, 0)),
        scratch_shapes=[
            pltpu.VMEM((128, 2 * HEAD), BF16),
            pltpu.VMEM((N_TP, 144, 2 * HEAD), BF16),
            pltpu.SemaphoreType.DMA((1,)),
        ],
        cost_estimate=pl.CostEstimate(
            flops=2 * 128 * 256 * 8192, bytes_accessed=7 << 20, transcendentals=0
        ),
        name="project",
    )(parcel, out_weight)


def fold(rank, along):
    return pl.pallas_call(
        fold_kernel,
        out_shape=(jax.ShapeDtypeStruct((128, 512), BF16),) * 4,
        in_specs=[in_smem(), pl.BlockSpec(memory_space=pl.ANY)],
        out_specs=(in_vmem(),) * 4,
        scratch_shapes=[pltpu.VMEM((4, 4, 128, 512), BF16), pltpu.SemaphoreType.DMA((4,))],
        cost_estimate=pl.CostEstimate(
            flops=16 * 128 * 512, bytes_accessed=5 << 19, transcendentals=0
        ),
        name="fold",
    )(rank, along)


def settle(rank, terms, residual, gain, prev):
    whole = pl.BlockSpec((128, 512), lambda p, at: (0, 0))
    return pl.pallas_call(
        settle_kernel,
        grid_spec=pltpu.PrefetchScalarGridSpec(
            num_scalar_prefetch=1,
            grid=(1,),
            in_specs=[whole] * 5
            + [
                pl.BlockSpec((1, 1, 512), lambda p, at: (at[0], 0, 0)),
                pl.BlockSpec((4, 512), lambda p, at: (0, at[0])),
            ],
            out_specs=[whole] * 3,
        ),
        out_shape=(
            jax.ShapeDtypeStruct((128, 512), F32),
            jax.ShapeDtypeStruct((128, 512), BF16),
            jax.ShapeDtypeStruct((128, 512), BF16),
        ),
        cost_estimate=pl.CostEstimate(
            flops=128 * 512 * 8, bytes_accessed=2 << 20, transcendentals=0
        ),
        name="settle",
    )(rank, *terms, residual, gain, prev)


def predict(source, rank, lengths, leaf, far_own, far, mixed, gain, prev, reach, pick, all_weight):
    return pl.pallas_call(
        predict_kernel,
        out_shape=(
            jax.ShapeDtypeStruct((128, 512), BF16),
            jax.ShapeDtypeStruct((128, 512), BF16),
            jax.ShapeDtypeStruct((8, 128), F32),
        ),
        in_specs=[in_smem()] * 4
        + [pl.BlockSpec(memory_space=pl.ANY)] * 2
        + [in_vmem()] * 5
        + [pl.BlockSpec(memory_space=pl.ANY)] * 16,
        out_specs=(in_vmem(),) * 3,
        scratch_shapes=[
            pltpu.VMEM((128, 128), F32),
            pltpu.VMEM((128, 512), F32),
            pltpu.VMEM((16, 2, 256, 512), BF16),
            pltpu.SemaphoreType.DMA((16,)),
            pltpu.VMEM((4, 4, 128, 512), BF16),
            pltpu.SemaphoreType.DMA((2,)),
        ],
        compiler_params=pltpu.CompilerParams(vmem_limit_bytes=32 << 20),
        cost_estimate=pl.CostEstimate(
            flops=2 * 128 * 8192 * 512, bytes_accessed=13 << 20, transcendentals=0
        ),
        name="predict",
    )(source, rank, lengths, leaf, far_own, far, mixed, gain, prev, reach, pick, *all_weight)


def differentiate(place, columns, errors, loss):
    return pl.pallas_call(
        differentiate_kernel,
        out_shape=(
            jax.ShapeDtypeStruct((512, 512), F32),
            jax.ShapeDtypeStruct((N_REQ * N_TP, 128), F32),
        ),
        in_specs=[in_smem()] + [pl.BlockSpec(memory_space=pl.ANY)] * 4 + [in_vmem()] * 5,
        out_specs=(in_vmem(), in_vmem()),
        scratch_shapes=[
            pltpu.VMEM((16, 128, 512), BF16),
            pltpu.SemaphoreType.DMA((4,)),
        ],
        cost_estimate=pl.CostEstimate(
            flops=2 * 2048 * 512 * 512, bytes_accessed=5 << 20, transcendentals=0
        ),
        name="differentiate",
    )(place, *columns, *errors, loss)


def update(pair, gradient, weight, first, second):
    part = pl.BlockSpec((128, 512), lambda p: (p, 0))
    return pl.pallas_call(
        update_kernel,
        grid=(4,),
        out_shape=(
            jax.ShapeDtypeStruct((512, 512), BF16),
            jax.ShapeDtypeStruct((512, 512), F32),
            jax.ShapeDtypeStruct((512, 512), F32),
            jax.ShapeDtypeStruct((1, 1), F32),
        ),
        in_specs=[pl.BlockSpec((N_REQ * N_TP, 128), lambda p: (0, 0))] + [part] * 4,
        out_specs=(part, part, part, in_smem()),
        cost_estimate=pl.CostEstimate(
            flops=20 * 512 * 512, bytes_accessed=6 << 20, transcendentals=512 * 512
        ),
        name="update",
    )(pair, gradient, weight, first, second)


def body(
    queries,
    cache_keys,
    cache_values,
    tree_keys,
    tree_values,
    parents,
    lengths,
    accepted_leaf,
    residual,
    norm_gain,
    out_weight,
    prev_feature,
    draft_weight,
    first_moment,
    second_moment,
):
    requests = queries.shape[0]
    rows = requests * NODES
    tp_rank = lax.axis_index(TP)
    rank = tp_rank.reshape(1)
    block = residual.shape[2]
    gain = norm_gain.reshape(N_TP, 1, block)
    zh, y, c = lax.axis_index("zh"), lax.axis_index("y"), lax.axis_index("c")
    piece = jnp.arange(N_REQ, dtype=jnp.int32)
    source = (
        ((zh + piece % 2) % 2) * 8 + ((y + 4 - (piece // 2) % 4) % 4) * 2 + (c + piece // 8) % 2
    )
    place = ((lax.axis_index("x") + 4 - source % 4) % 4) * 4 + (
        lax.axis_index("zl") + 4 - source // 4
    ) % 4

    parcel, reach, pick = attend(
        rank, lengths, parents, queries, cache_keys, cache_values, tree_keys, tree_values
    )
    parcel = exchange(parcel, TP)
    half = draft_weight.shape[0] // 2
    parcel, upper, lower = lax.optimization_barrier(
        (parcel, draft_weight[:half], draft_weight[half:])
    )
    upper = passed(upper, "zh", 2)
    lower = passed(lower, "zh", 2)
    upper = jnp.stack(upper)
    upper = passed(upper, "y", 4)

    partial_value = project(parcel, out_weight)
    along_x = exchange(partial_value, "x")
    other_upper = [lax.ppermute(part, "c", turn(2, 1)) for part in upper]
    lower = jnp.stack(lower)
    lower = passed(lower, "y", 4)
    terms = list(fold(rank, along_x))
    terms[1:] = [lax.ppermute(terms[step], "zl", turn(4, step)) for step in (1, 2, 3)]
    mixed, near, table = settle(rank, terms, residual.reshape(rows, block), gain, prev_feature)

    far = passed(near, "zl", 4)[1:]
    far_own = spread(near[None], "x", 4)
    far = jnp.stack(far)
    far = spread(far, "x", 4).reshape(4, 3, rows, block)
    swapped = lax.ppermute(
        table, REQ + TP, [(i * N_TP + j, j * N_TP + i) for i in range(16) for j in range(16)]
    )
    other_lower = [lax.ppermute(part, "c", turn(2, 1)) for part in lower]
    columns = passed(swapped, "zl", 4)
    columns = jnp.stack(columns)
    columns = passed(columns, "x", 4)
    own_features, scaled_err, loss = predict(
        source,
        rank,
        lengths,
        accepted_leaf,
        far_own,
        far,
        mixed,
        gain,
        prev_feature,
        reach,
        pick,
        upper + other_upper + lower + other_lower,
    )
    far_err = lax.ppermute(scaled_err, "zh", turn(2, 1))
    err = passed(scaled_err, "y", 4)
    far_err = passed(far_err, "y", 4)
    err, far_err = jnp.stack(err), jnp.stack(far_err)
    errors = [err, far_err] + [lax.ppermute(part, "c", turn(2, 1)) for part in (err, far_err)]
    gradient, pair = differentiate(place, columns, errors, loss)
    pair = exchange(pair, REQ + TP)
    new_weight, new_first, new_second, draft_loss = update(
        pair, gradient, draft_weight, first_moment, second_moment
    )
    return (
        own_features.reshape(requests, NODES, block),
        new_weight,
        new_first,
        new_second,
        draft_loss.reshape(()),
    )


def solution(mesh):
    fine = Mesh(mesh.devices.reshape(2, 4, 2, 4, 4), REQ + TP)
    placed = (
        P(REQ, None, None),
        P(REQ, TP, None),
        P(REQ, TP, None),
        P(REQ, TP, None),
        P(REQ, TP, None),
        P(REQ, None),
        P(REQ),
        P(REQ),
        P(REQ, None, TP),
        P(),
        P(TP, None),
        P(REQ, None),
        P(REQ, TP),
        P(REQ, TP),
        P(REQ, TP),
    )

    return jax.shard_map(
        body,
        mesh=fine,
        in_specs=placed,
        out_specs=(P(REQ, None, TP), P(REQ, TP), P(REQ, TP), P(REQ, TP), P()),
        check_vma=False,
    )
```

```python
import math

import jax
import jax.numpy as jnp
from jax import lax
from jax.experimental import pallas as pl
from jax.experimental.pallas import tpu as pltpu
from jax.sharding import Mesh
from jax.sharding import PartitionSpec as P

HEADS = 32
KV_HEADS = 4
HEAD = 128
NODES = 32
CACHE = 4096
D = 8192
N_TP = 16
N_REQ = 16

NEG_FILL = -1e30
NORM_EPSILON = 1e-06
BETA_ONE = 0.9
BETA_TWO = 0.95
CORRECT_ONE = 1.0 - 0.9**10
CORRECT_TWO = 1.0 - 0.95**10
LEARN_RATE = 0.001


REQ = ("zh", "y", "c")
TP = ("zl", "x")
F32 = jnp.float32
BF16 = jnp.bfloat16


def exchange(value, axis):
    return lax.all_to_all(value, axis, 0, 0, tiled=True)


def turn(count, step):
    return [(i, (i + step) % count) for i in range(count)]


def passed(value, axis, count):
    return [value] + [lax.ppermute(value, axis, turn(count, step)) for step in range(1, count)]


def dot(left, right, dims, **kwargs):
    return lax.dot_general(left, right, (dims, ((), ())), preferred_element_type=F32, **kwargs)


def same_request(width=128):
    row = lax.broadcasted_iota(jnp.int32, (128, width), 0)
    lane = lax.broadcasted_iota(jnp.int32, (128, width), 1)
    return row, lane


def attend_kernel(
    rank_ref, len_ref, par_ref, q_ref, ck_ref, cv_ref, tk_ref, tv_ref,
    out_ref, maps_ref, stat_ref,
):
    r = pl.program_id(0)
    rank = rank_ref[0]

    @pl.when(r == 0)
    def trees():
        row, lane = same_request()
        base = (lane // NODES) * NODES
        tile = jnp.where(
            lax.broadcasted_iota(jnp.int32, (NODES, 128), 0)
            == lax.broadcasted_iota(jnp.int32, (NODES, 128), 1) % NODES,
            1.0,
            0.0,
        )
        wide = dot(par_ref[...].astype(F32).astype(BF16), tile.astype(BF16), ((1,), (0,)))
        lane_request = lax.broadcasted_iota(jnp.int32, (1, 128), 1) // NODES
        parent = wide[0:1]
        for r in range(1, 4):
            parent = jnp.where(lane_request == r, wide[r : r + 1], parent)
        parent = parent.astype(jnp.int32)
        rooted = jnp.where(parent < 0, NODES - 1, parent)
        maps_ref[128:256] = jnp.where(row == base + rooted, 1.0, 0.0).astype(BF16)
        up = jnp.where(row == base + parent, jnp.where(parent >= 0, 1.0, 0.0), 0.0)
        reach = (jnp.where(row == lane, 1.0, 0.0) + up).astype(BF16)
        for _ in range((NODES - 1).bit_length()):
            reach = jnp.minimum(dot(reach, reach, ((1,), (0,))), 1.0).astype(BF16)
        maps_ref[0:128] = reach
        own = jnp.where(row % NODES == 2 * rank + lane, jnp.where(lane < 2, 1.0, 0.0), 0.0)
        stat_ref[...] = dot(reach, own.astype(BF16), ((0,), (0,)))

    scale = 1.0 / math.sqrt(HEAD)
    span = ck_ref.shape[1]
    slot = lax.broadcasted_iota(jnp.int32, (256, span), 1) + rank * span
    wide_lane = lax.broadcasted_iota(jnp.int32, (NODES, 128), 1)

    own_rows = pl.ds(pl.multiple_of(r * NODES, NODES), NODES)
    live = slot < len_ref[r]
    seen = stat_ref[own_rows, :][:, : tk_ref.shape[1]]
    seen = jnp.concatenate([seen] * 8, axis=0) > 0.5
    stats = jnp.zeros((NODES, 128), F32)
    for k in range(KV_HEADS):
        head = slice(k * HEAD, (k + 1) * HEAD)
        query = jnp.concatenate(
            [q_ref[0, :, (k * 8 + g) * HEAD : (k * 8 + g + 1) * HEAD] for g in range(8)], axis=0
        )
        scores = dot(query, ck_ref[0, :, head], ((1,), (1,))) * scale
        tree = dot(query, tk_ref[0, :, head], ((1,), (1,))) * scale
        scores = jnp.where(live, scores, NEG_FILL)
        tree = jnp.where(seen, tree, NEG_FILL)
        top = jnp.maximum(
            jnp.max(scores, axis=1, keepdims=True), jnp.max(tree, axis=1, keepdims=True)
        )
        top = jnp.maximum(top, 0.5 * NEG_FILL).astype(BF16).astype(F32)
        probs = jnp.exp(scores - top).astype(BF16)
        tree = jnp.exp(tree - top).astype(BF16)
        total = jnp.sum(probs.astype(F32), axis=1, keepdims=True) + jnp.sum(
            tree.astype(F32), axis=1, keepdims=True
        )
        high = total.astype(BF16).astype(F32)
        low = total - high
        value = dot(probs, cv_ref[0, :, head], ((1,), (0,))) + dot(
            tree, tv_ref[0, :, head], ((1,), (0,))
        )
        value = value.astype(BF16)
        for g in range(8):
            h = k * 8 + g
            part = slice(g * NODES, (g + 1) * NODES)
            out_ref[h // 2, own_rows, (h % 2) * HEAD : (h % 2 + 1) * HEAD] = value[part]
            for at, column in enumerate((top, high, low)):
                stats = jnp.where(wide_lane == h * 4 + at, column[part], stats)
    stat_ref[own_rows, :] = stats

    @pl.when(r == 3)
    def statistics():
        turned = jnp.transpose(stat_ref[...])
        empty = jnp.zeros((8, 128), F32)
        blank = jnp.zeros((16, 128), BF16)
        for owner in range(N_TP):
            block = jnp.concatenate([turned[owner * 8 : (owner + 1) * 8], empty], axis=0)
            out_ref[owner, 128:144, 0:128] = block.astype(BF16)
            out_ref[owner, 128:144, 128:256] = blank


def project_kernel(parcel_ref, weight_ref, out_ref, att_ref):
    @pl.when(pl.program_id(0) == 0)
    def join():
        stats = jnp.concatenate(
            [parcel_ref[src, 128:144, 0:128].astype(F32)[0:8] for src in range(N_TP)], axis=0
        )
        total = pltpu.roll(stats, 127, 0) + pltpu.roll(stats, 126, 0)
        stats = stats.reshape(N_TP, 8, 128)
        factor = jnp.exp(stats - jnp.max(stats, axis=0, keepdims=True))
        share = factor / jnp.sum(factor * total.reshape(N_TP, 8, 128), axis=0, keepdims=True)
        share = jnp.transpose(share.reshape(128, 128))
        for side in range(2):
            cols = slice(side * HEAD, (side + 1) * HEAD)
            joined = jnp.zeros((128, HEAD), F32)
            for src in range(N_TP):
                at = src * 8 + side * 4
                joined = joined + parcel_ref[src, 0:128, cols].astype(F32) * share[:, at : at + 1]
            att_ref[:, cols] = joined.astype(BF16)

    for x in range(4):
        cols = slice(x * 512, (x + 1) * 512)
        out_ref[x, 0] = dot(att_ref[...], weight_ref[:, cols], ((1,), (0,))).astype(BF16)


def fold_kernel(rank_ref, along_ref, *out_refs):
    for step in range(4):
        zl = lax.rem(rank_ref[0] // 4 + step, 4)
        total = along_ref[0, zl].astype(F32)
        for x in range(1, 4):
            total = total + along_ref[x, zl].astype(F32)
        out_refs[step][...] = total.astype(BF16)


def settle_kernel(
    rank_ref, own_ref, one_ref, two_ref, three_ref, residual_ref, gain_ref, prev_ref,
    mixed_ref, near_ref, wide_ref, table_ref,
):
    total = own_ref[...].astype(F32) + one_ref[...].astype(F32)
    total = total + (two_ref[...].astype(F32) + three_ref[...].astype(F32))
    mixed = residual_ref[...].astype(F32) + total
    mixed_ref[...] = mixed
    near = mixed.astype(BF16)
    near_ref[...] = near
    for x in range(4):
        wide_ref[x] = near
    scaled = mixed * gain_ref[0]
    node = lax.broadcasted_iota(jnp.int32, (NODES, 1), 0)
    prev = prev_ref[...].astype(F32)
    for r in range(4):
        part = slice(r * NODES, (r + 1) * NODES)
        table_ref[part] = jnp.where(node == NODES - 1, prev[r : r + 1], scaled[part]).astype(BF16)


def predict_kernel(
    source_ref, rank_ref, len_ref, leaf_ref, far_own_ref, far_rest_ref, mixed_ref, gain_ref, prev_ref, maps_ref,
    *refs,
):
    weight_refs = refs[:16]
    own_ref, err_ref, loss_ref, scale_ref, ahead_ref, weight_ref, sem_ref, far_ref, far_sem = refs[16:]
    own_load = pltpu.make_async_copy(far_own_ref, far_ref.at[:, 0], far_sem.at[0])
    rest_load = pltpu.make_async_copy(far_rest_ref, far_ref.at[:, 1:4], far_sem.at[1])
    own_load.start()
    rest_load.start()
    loads = [pltpu.make_async_copy(weight_refs[i], weight_ref.at[i], sem_ref.at[i]) for i in range(16)]
    for load in loads:
        load.start()
    square = jnp.zeros((128, 128), F32)
    own_load.wait()
    for k in range(4):
        if k == 1:
            rest_load.wait()
        for x in range(4):
            part = far_ref[x, k].astype(F32)
            part = part * part
            for i in range(4):
                square = square + part[:, i * 128 : (i + 1) * 128]
    square = jnp.sum(square, axis=1, keepdims=True)
    scale = lax.rsqrt(square / D + NORM_EPSILON)
    scale_ref[...] = jnp.broadcast_to(scale, (128, 128))
    own_ref[...] = (mixed_ref[...] * scale * gain_ref[rank_ref[0]]).astype(BF16)

    node = lax.broadcasted_iota(jnp.int32, (NODES, 1), 0)
    for part in range(8):
        loads[part].wait()
        loads[part + 8].wait()
        total = jnp.zeros((128, 512), F32)
        for i in range(2):
            p = source_ref[part * 2 + i]
            back = lax.rem(rank_ref[0] // 4 + 4 - p // 4, 4)
            block = far_ref[lax.rem(p, 4), back].astype(F32) * scale_ref[:, 0:1] * gain_ref[p]
            prev = prev_ref[:, pl.ds(pl.multiple_of(p * 512, 512), 512)].astype(F32)
            block = jnp.concatenate(
                [
                    jnp.where(node == NODES - 1, prev[r : r + 1], block[r * NODES : (r + 1) * NODES])
                    for r in range(4)
                ],
                axis=0,
            ).astype(BF16)
            total = total + dot(block[:, :256], weight_ref[part, i], ((1,), (0,)))
            total = total + dot(block[:, 256:], weight_ref[part + 8, i], ((1,), (0,)))
        if part == 0:
            ahead_ref[...] = total
        else:
            ahead_ref[...] += total

    row, lane = same_request()
    accepted = []
    for r in range(4):
        part = slice(r * NODES, (r + 1) * NODES)
        path = jnp.where(lane[part] == leaf_ref[r] + r * NODES, maps_ref[part].astype(F32), 0.0)
        path = jnp.sum(path, axis=1, keepdims=True)
        accepted.append((1.0 + 3.0 * path) * (0.5 + len_ref[r].astype(F32) / CACHE))
    weights = jnp.concatenate(accepted, axis=0)
    pick = maps_ref[128:256].astype(F32)
    predicted = dot(pick, ahead_ref[...], ((0,), (0,)), precision=lax.Precision.HIGHEST)
    error = predicted - own_ref[...].astype(F32)
    weighted = weights * error
    joined = dot(pick, weighted, ((1,), (0,)), precision=lax.Precision.HIGHEST)
    scale = jnp.where(row[:, 0:1] % NODES == NODES - 1, 1.0, scale_ref[:, 0:1])
    err_ref[...] = (joined * scale).astype(BF16)
    loss = jnp.sum(jnp.sum(weighted * error, axis=0, keepdims=True), axis=1, keepdims=True)
    loss_ref[...] = jnp.broadcast_to(loss, (8, 128))


def differentiate_kernel(place_ref, column_ref, e0_ref, e1_ref, e2_ref, e3_ref, loss_ref, grad_ref, pair_ref):
    for part, err_ref in enumerate((e0_ref, e1_ref, e2_ref, e3_ref)):
        first = (part // 2) * 8 + part % 2
        left = jnp.concatenate([column_ref[place_ref[first + 2 * i]] for i in range(4)], axis=0)
        right = jnp.concatenate([err_ref[i] for i in range(4)], axis=0)
        term = dot(left, right, ((0,), (0,)))
        if part == 0:
            grad_ref[...] = term
        else:
            grad_ref[...] += term
    value = grad_ref[...]
    square = jnp.sum(jnp.sum(value * value, axis=0, keepdims=True), axis=1, keepdims=True)
    lane = lax.broadcasted_iota(jnp.int32, (8, 128), 1)
    pair = jnp.where(lane == 0, square, jnp.where(lane == 1, loss_ref[...], 0.0))
    for i in range(32):
        pair_ref[i * 8 : (i + 1) * 8] = pair


def update_kernel(
    pair_ref, grad_ref, weight_ref, first_ref, second_ref,
    new_weight_ref, new_first_ref, new_second_ref, loss_ref,
):
    total = jnp.sum(pair_ref[...], axis=0, keepdims=True)
    norm = jnp.sqrt(total[:, 0:1]) + 1e-06
    clipped = grad_ref[...] * jnp.minimum(1.0, D / norm)
    new_first = BETA_ONE * first_ref[...] + (1.0 - BETA_ONE) * clipped
    new_second = BETA_TWO * second_ref[...] + (1.0 - BETA_TWO) * clipped * clipped
    direction = new_first / CORRECT_ONE / (jnp.sqrt(new_second / CORRECT_TWO) + 1e-08)
    new_first_ref[...] = new_first
    new_second_ref[...] = new_second
    new_weight_ref[...] = (weight_ref[...].astype(F32) - LEARN_RATE * direction).astype(BF16)
    lane = lax.broadcasted_iota(jnp.int32, (1, 128), 1)
    loss_ref[0, 0] = jnp.sum(jnp.where(lane == 1, total, 0.0)) * (0.5 / (128 * N_REQ * D))


def in_vmem():
    return pl.BlockSpec(memory_space=pltpu.VMEM)


def in_smem():
    return pl.BlockSpec(memory_space=pltpu.SMEM)


def attend(rank, lengths, parents, queries, cache_keys, cache_values, tree_keys, tree_values):
    return pl.pallas_call(
        attend_kernel,
        out_shape=(
            jax.ShapeDtypeStruct((N_TP, 144, 2 * HEAD), BF16),
            jax.ShapeDtypeStruct((256, 128), BF16),
        ),
        grid=(4,),
        in_specs=[
            in_smem(),
            in_smem(),
            pl.BlockSpec((4, NODES), lambda r: (0, 0)),
            pl.BlockSpec((1, NODES, HEADS * HEAD), lambda r: (r, 0, 0)),
        ]
        + [pl.BlockSpec((1, 256, KV_HEADS * HEAD), lambda r: (r, 0, 0))] * 2
        + [pl.BlockSpec((1, 2, KV_HEADS * HEAD), lambda r: (r, 0, 0))] * 2,
        out_specs=(
            pl.BlockSpec((N_TP, 144, 2 * HEAD), lambda r: (0, 0, 0)),
            pl.BlockSpec((256, 128), lambda r: (0, 0)),
        ),
        scratch_shapes=[pltpu.VMEM((128, 128), F32)],
        cost_estimate=pl.CostEstimate(
            flops=2 * 2 * 16 * 256 * 256 * 128, bytes_accessed=4 << 20, transcendentals=16 * 256 * 256
        ),
        name="attend",
    )(rank, lengths, parents, queries, cache_keys, cache_values, tree_keys, tree_values)


def project(parcel, out_weight):
    return pl.pallas_call(
        project_kernel,
        grid=(4,),
        out_shape=jax.ShapeDtypeStruct((4, 4, 128, 512), BF16),
        in_specs=[
            pl.BlockSpec((N_TP, 144, 2 * HEAD), lambda p: (0, 0, 0)),
            pl.BlockSpec((2 * HEAD, 2048), lambda p: (0, p)),
        ],
        out_specs=pl.BlockSpec((4, 1, 128, 512), lambda p: (0, p, 0, 0)),
        scratch_shapes=[pltpu.VMEM((128, 2 * HEAD), BF16)],
        cost_estimate=pl.CostEstimate(
            flops=2 * 128 * 256 * 8192, bytes_accessed=7 << 20, transcendentals=0
        ),
        name="project",
    )(parcel, out_weight)


def fold(rank, along):
    return pl.pallas_call(
        fold_kernel,
        out_shape=(jax.ShapeDtypeStruct((128, 512), BF16),) * 4,
        in_specs=[in_smem(), in_vmem()],
        out_specs=(in_vmem(),) * 4,
        cost_estimate=pl.CostEstimate(
            flops=16 * 128 * 512, bytes_accessed=5 << 19, transcendentals=0
        ),
        name="fold",
    )(rank, along)


def settle(rank, terms, residual, gain, prev):
    whole = pl.BlockSpec((128, 512), lambda p, at: (0, 0))
    return pl.pallas_call(
        settle_kernel,
        grid_spec=pltpu.PrefetchScalarGridSpec(
            num_scalar_prefetch=1,
            grid=(1,),
            in_specs=[whole] * 5
            + [
                pl.BlockSpec((1, 1, 512), lambda p, at: (at[0], 0, 0)),
                pl.BlockSpec((4, 512), lambda p, at: (0, at[0])),
            ],
            out_specs=[
                whole,
                whole,
                pl.BlockSpec((4, 128, 512), lambda p, at: (0, 0, 0)),
                whole,
            ],
        ),
        out_shape=(
            jax.ShapeDtypeStruct((128, 512), F32),
            jax.ShapeDtypeStruct((128, 512), BF16),
            jax.ShapeDtypeStruct((4, 128, 512), BF16),
            jax.ShapeDtypeStruct((128, 512), BF16),
        ),
        cost_estimate=pl.CostEstimate(
            flops=128 * 512 * 8, bytes_accessed=2 << 20, transcendentals=0
        ),
        name="settle",
    )(rank, *terms, residual, gain, prev)


def predict(source, rank, lengths, leaf, far_own, far, mixed, gain, prev, maps, all_weight):
    return pl.pallas_call(
        predict_kernel,
        out_shape=(
            jax.ShapeDtypeStruct((128, 512), BF16),
            jax.ShapeDtypeStruct((128, 512), BF16),
            jax.ShapeDtypeStruct((8, 128), F32),
        ),
        in_specs=[in_smem()] * 4
        + [pl.BlockSpec(memory_space=pl.ANY)] * 2
        + [in_vmem()] * 4
        + [pl.BlockSpec(memory_space=pl.ANY)] * 16,
        out_specs=(in_vmem(),) * 3,
        scratch_shapes=[
            pltpu.VMEM((128, 128), F32),
            pltpu.VMEM((128, 512), F32),
            pltpu.VMEM((16, 2, 256, 512), BF16),
            pltpu.SemaphoreType.DMA((16,)),
            pltpu.VMEM((4, 4, 128, 512), BF16),
            pltpu.SemaphoreType.DMA((2,)),
        ],
        compiler_params=pltpu.CompilerParams(vmem_limit_bytes=32 << 20),
        cost_estimate=pl.CostEstimate(
            flops=2 * 128 * 8192 * 512, bytes_accessed=13 << 20, transcendentals=0
        ),
        name="predict",
    )(source, rank, lengths, leaf, far_own, far, mixed, gain, prev, maps, *all_weight)


def differentiate(place, columns, errors, loss):
    return pl.pallas_call(
        differentiate_kernel,
        out_shape=(
            jax.ShapeDtypeStruct((512, 512), F32),
            jax.ShapeDtypeStruct((N_REQ * N_TP, 128), F32),
        ),
        in_specs=[in_smem()] + [in_vmem()] * 6,
        out_specs=(in_vmem(), in_vmem()),
        cost_estimate=pl.CostEstimate(
            flops=2 * 2048 * 512 * 512, bytes_accessed=5 << 20, transcendentals=0
        ),
        name="differentiate",
    )(place, columns, *errors, loss)


def update(pair, gradient, weight, first, second):
    part = pl.BlockSpec((128, 512), lambda p: (p, 0))
    return pl.pallas_call(
        update_kernel,
        grid=(4,),
        out_shape=(
            jax.ShapeDtypeStruct((512, 512), BF16),
            jax.ShapeDtypeStruct((512, 512), F32),
            jax.ShapeDtypeStruct((512, 512), F32),
            jax.ShapeDtypeStruct((1, 1), F32),
        ),
        in_specs=[pl.BlockSpec((N_REQ * N_TP, 128), lambda p: (0, 0))] + [part] * 4,
        out_specs=(part, part, part, in_smem()),
        cost_estimate=pl.CostEstimate(
            flops=20 * 512 * 512, bytes_accessed=6 << 20, transcendentals=512 * 512
        ),
        name="update",
    )(pair, gradient, weight, first, second)


def body(
    queries,
    cache_keys,
    cache_values,
    tree_keys,
    tree_values,
    parents,
    lengths,
    accepted_leaf,
    residual,
    norm_gain,
    out_weight,
    prev_feature,
    draft_weight,
    first_moment,
    second_moment,
):
    requests = queries.shape[0]
    rows = requests * NODES
    tp_rank = lax.axis_index(TP)
    rank = tp_rank.reshape(1)
    block = residual.shape[2]
    gain = norm_gain.reshape(N_TP, 1, block)
    zh, y, c = lax.axis_index("zh"), lax.axis_index("y"), lax.axis_index("c")
    piece = jnp.arange(N_REQ, dtype=jnp.int32)
    source = (
        ((zh + piece % 2) % 2) * 8 + ((y + 4 - (piece // 2) % 4) % 4) * 2 + (c + piece // 8) % 2
    )
    place = (source % 4) * 4 + (lax.axis_index("zl") + 4 - source // 4) % 4

    parcel, maps = attend(
        rank, lengths, parents, queries, cache_keys, cache_values, tree_keys, tree_values
    )
    parcel = exchange(parcel, TP)
    half = draft_weight.shape[0] // 2
    parcel, upper, lower = lax.optimization_barrier(
        (parcel, draft_weight[:half], draft_weight[half:])
    )
    upper = passed(upper, "zh", 2)
    lower = passed(lower, "zh", 2)
    upper = jnp.stack(upper)
    upper = passed(upper, "y", 4)

    partial_value = project(parcel, out_weight)
    along_x = exchange(partial_value, "x")
    other_upper = [lax.ppermute(part, "c", turn(2, 1)) for part in upper]
    lower = jnp.stack(lower)
    lower = passed(lower, "y", 4)
    terms = list(fold(rank, along_x))
    terms[1:] = [lax.ppermute(terms[step], "zl", turn(4, step)) for step in (1, 2, 3)]
    mixed, near, wide, table = settle(rank, terms, residual.reshape(rows, block), gain, prev_feature)

    far = passed(near, "zl", 4)[1:]
    far_own = exchange(wide, "x")
    far = jnp.stack(far)
    far = jnp.broadcast_to(far[None], (4, 3, rows, block)).reshape(12, rows, block)
    far = exchange(far, "x").reshape(4, 3, rows, block)
    swapped = lax.ppermute(
        table, REQ + TP, [(i * N_TP + j, j * N_TP + i) for i in range(16) for j in range(16)]
    )
    other_lower = [lax.ppermute(part, "c", turn(2, 1)) for part in lower]
    columns = passed(swapped, "zl", 4)
    columns = jnp.stack(columns)
    columns = jnp.broadcast_to(columns[None], (4, 4, rows, block)).reshape(16, rows, block)
    columns = exchange(columns, "x")
    own_features, scaled_err, loss = predict(
        source,
        rank,
        lengths,
        accepted_leaf,
        far_own,
        far,
        mixed,
        gain,
        prev_feature,
        maps,
        upper + other_upper + lower + other_lower,
    )
    far_err = lax.ppermute(scaled_err, "zh", turn(2, 1))
    err = passed(scaled_err, "y", 4)
    far_err = passed(far_err, "y", 4)
    err, far_err = jnp.stack(err), jnp.stack(far_err)
    errors = [err, far_err] + [lax.ppermute(part, "c", turn(2, 1)) for part in (err, far_err)]
    gradient, pair = differentiate(place, columns, errors, loss)
    pair = exchange(pair, REQ + TP)
    new_weight, new_first, new_second, draft_loss = update(
        pair, gradient, draft_weight, first_moment, second_moment
    )
    return (
        own_features.reshape(requests, NODES, block),
        new_weight,
        new_first,
        new_second,
        draft_loss.reshape(()),
    )


def solution(mesh):
    fine = Mesh(mesh.devices.reshape(2, 4, 2, 4, 4), REQ + TP)
    placed = (
        P(REQ, None, None),
        P(REQ, TP, None),
        P(REQ, TP, None),
        P(REQ, TP, None),
        P(REQ, TP, None),
        P(REQ, None),
        P(REQ),
        P(REQ),
        P(REQ, None, TP),
        P(),
        P(TP, None),
        P(REQ, None),
        P(REQ, TP),
        P(REQ, TP),
        P(REQ, TP),
    )

    return jax.shard_map(
        body,
        mesh=fine,
        in_specs=placed,
        out_specs=(P(REQ, None, TP), P(REQ, TP), P(REQ, TP), P(REQ, TP), P()),
        check_vma=False,
    )
```

```python
import math

import jax
import jax.numpy as jnp
from jax import lax
from jax.experimental import pallas as pl
from jax.experimental.pallas import tpu as pltpu
from jax.sharding import Mesh
from jax.sharding import PartitionSpec as P

HEADS = 32
KV_HEADS = 4
HEAD = 128
NODES = 32
CACHE = 4096
D = 8192
N_TP = 16
N_REQ = 16

NEG_FILL = -1e30
NORM_EPSILON = 1e-06
BETA_ONE = 0.9
BETA_TWO = 0.95
CORRECT_ONE = 1.0 - 0.9**10
CORRECT_TWO = 1.0 - 0.95**10
LEARN_RATE = 0.001


REQ = ("zh", "y", "c")
TP = ("zl", "x")
F32 = jnp.float32
BF16 = jnp.bfloat16


def exchange(value, axis):
    return lax.all_to_all(value, axis, 0, 0, tiled=True)


def turn(count, step):
    return [(i, (i + step) % count) for i in range(count)]


def passed(value, axis, count):
    return [value] + [lax.ppermute(value, axis, turn(count, step)) for step in range(1, count)]


def dot(left, right, dims, **kwargs):
    return lax.dot_general(left, right, (dims, ((), ())), preferred_element_type=F32, **kwargs)


def same_request(width=128):
    row = lax.broadcasted_iota(jnp.int32, (128, width), 0)
    lane = lax.broadcasted_iota(jnp.int32, (128, width), 1)
    return row, lane


def attend_kernel(
    rank_ref, len_ref, par_ref, q_ref, ck_ref, cv_ref, tk_ref, tv_ref,
    out_ref, maps_ref, stat_ref,
):
    r = pl.program_id(0)
    rank = rank_ref[0]

    @pl.when(r == 0)
    def trees():
        row, lane = same_request()
        base = (lane // NODES) * NODES
        tile = jnp.where(
            lax.broadcasted_iota(jnp.int32, (NODES, 128), 0)
            == lax.broadcasted_iota(jnp.int32, (NODES, 128), 1) % NODES,
            1.0,
            0.0,
        )
        wide = dot(par_ref[...].astype(F32).astype(BF16), tile.astype(BF16), ((1,), (0,)))
        lane_request = lax.broadcasted_iota(jnp.int32, (1, 128), 1) // NODES
        parent = wide[0:1]
        for r in range(1, 4):
            parent = jnp.where(lane_request == r, wide[r : r + 1], parent)
        parent = parent.astype(jnp.int32)
        rooted = jnp.where(parent < 0, NODES - 1, parent)
        maps_ref[128:256] = jnp.where(row == base + rooted, 1.0, 0.0).astype(BF16)
        up = jnp.where(row == base + parent, jnp.where(parent >= 0, 1.0, 0.0), 0.0)
        reach = (jnp.where(row == lane, 1.0, 0.0) + up).astype(BF16)
        for _ in range((NODES - 1).bit_length()):
            reach = jnp.minimum(dot(reach, reach, ((1,), (0,))), 1.0).astype(BF16)
        maps_ref[0:128] = reach
        own = jnp.where(row % NODES == 2 * rank + lane, jnp.where(lane < 2, 1.0, 0.0), 0.0)
        stat_ref[...] = dot(reach, own.astype(BF16), ((0,), (0,)))

    scale = 1.0 / math.sqrt(HEAD)
    span = ck_ref.shape[1]
    slot = lax.broadcasted_iota(jnp.int32, (256, span), 1) + rank * span
    wide_lane = lax.broadcasted_iota(jnp.int32, (NODES, 128), 1)

    own_rows = pl.ds(pl.multiple_of(r * NODES, NODES), NODES)
    live = slot < len_ref[r]
    seen = stat_ref[own_rows, :][:, : tk_ref.shape[1]]
    seen = jnp.concatenate([seen] * 8, axis=0) > 0.5
    stats = jnp.zeros((NODES, 128), F32)
    for k in range(KV_HEADS):
        head = slice(k * HEAD, (k + 1) * HEAD)
        query = jnp.concatenate(
            [q_ref[0, :, (k * 8 + g) * HEAD : (k * 8 + g + 1) * HEAD] for g in range(8)], axis=0
        )
        scores = dot(query, ck_ref[0, :, head], ((1,), (1,))) * scale
        tree = dot(query, tk_ref[0, :, head], ((1,), (1,))) * scale
        scores = jnp.where(live, scores, NEG_FILL)
        tree = jnp.where(seen, tree, NEG_FILL)
        top = jnp.maximum(
            jnp.max(scores, axis=1, keepdims=True), jnp.max(tree, axis=1, keepdims=True)
        )
        top = jnp.maximum(top, 0.5 * NEG_FILL).astype(BF16).astype(F32)
        probs = jnp.exp(scores - top).astype(BF16)
        tree = jnp.exp(tree - top).astype(BF16)
        total = jnp.sum(probs.astype(F32), axis=1, keepdims=True) + jnp.sum(
            tree.astype(F32), axis=1, keepdims=True
        )
        high = total.astype(BF16).astype(F32)
        low = total - high
        value = dot(probs, cv_ref[0, :, head], ((1,), (0,))) + dot(
            tree, tv_ref[0, :, head], ((1,), (0,))
        )
        value = value.astype(BF16)
        for g in range(8):
            h = k * 8 + g
            part = slice(g * NODES, (g + 1) * NODES)
            out_ref[h // 2, own_rows, (h % 2) * HEAD : (h % 2 + 1) * HEAD] = value[part]
            for at, column in enumerate((top, high, low)):
                stats = jnp.where(wide_lane == h * 4 + at, column[part], stats)
    stat_ref[own_rows, :] = stats

    @pl.when(r == 3)
    def statistics():
        turned = jnp.transpose(stat_ref[...])
        empty = jnp.zeros((8, 128), F32)
        blank = jnp.zeros((16, 128), BF16)
        for owner in range(N_TP):
            block = jnp.concatenate([turned[owner * 8 : (owner + 1) * 8], empty], axis=0)
            out_ref[owner, 128:144, 0:128] = block.astype(BF16)
            out_ref[owner, 128:144, 128:256] = blank


def project_kernel(parcel_ref, weight_ref, out_ref, att_ref):
    @pl.when(pl.program_id(0) == 0)
    def join():
        stats = jnp.concatenate(
            [parcel_ref[src, 128:144, 0:128].astype(F32)[0:8] for src in range(N_TP)], axis=0
        )
        total = pltpu.roll(stats, 127, 0) + pltpu.roll(stats, 126, 0)
        stats = stats.reshape(N_TP, 8, 128)
        factor = jnp.exp(stats - jnp.max(stats, axis=0, keepdims=True))
        share = factor / jnp.sum(factor * total.reshape(N_TP, 8, 128), axis=0, keepdims=True)
        share = jnp.transpose(share.reshape(128, 128))
        for side in range(2):
            cols = slice(side * HEAD, (side + 1) * HEAD)
            joined = jnp.zeros((128, HEAD), F32)
            for src in range(N_TP):
                at = src * 8 + side * 4
                joined = joined + parcel_ref[src, 0:128, cols].astype(F32) * share[:, at : at + 1]
            att_ref[:, cols] = joined.astype(BF16)

    for x in range(4):
        cols = slice(x * 512, (x + 1) * 512)
        out_ref[x, 0] = dot(att_ref[...], weight_ref[:, cols], ((1,), (0,))).astype(BF16)


def fold_kernel(rank_ref, along_ref, *out_refs):
    for step in range(4):
        zl = lax.rem(rank_ref[0] // 4 + step, 4)
        total = along_ref[0, zl].astype(F32)
        for x in range(1, 4):
            total = total + along_ref[x, zl].astype(F32)
        out_refs[step][...] = total.astype(BF16)


def settle_kernel(
    rank_ref, own_ref, one_ref, two_ref, three_ref, residual_ref, gain_ref, prev_ref,
    mixed_ref, near_ref, wide_ref, table_ref,
):
    total = own_ref[...].astype(F32) + one_ref[...].astype(F32)
    total = total + (two_ref[...].astype(F32) + three_ref[...].astype(F32))
    mixed = residual_ref[...].astype(F32) + total
    mixed_ref[...] = mixed
    near = mixed.astype(BF16)
    near_ref[...] = near
    for x in range(4):
        wide_ref[x] = near
    scaled = mixed * gain_ref[0]
    node = lax.broadcasted_iota(jnp.int32, (NODES, 1), 0)
    prev = prev_ref[...].astype(F32)
    for r in range(4):
        part = slice(r * NODES, (r + 1) * NODES)
        table_ref[part] = jnp.where(node == NODES - 1, prev[r : r + 1], scaled[part]).astype(BF16)


def predict_kernel(
    source_ref, rank_ref, len_ref, leaf_ref, far_own_ref, far_rest_ref, mixed_ref, gain_ref, prev_ref, maps_from_ref,
    *refs,
):
    weight_refs = refs[:16]
    own_ref, err_ref, loss_ref, scale_ref, ahead_ref, weight_ref, sem_ref, far_ref, far_sem = refs[16:25]
    maps_ref = refs[25]
    maps_load = pltpu.make_async_copy(maps_from_ref, maps_ref, far_sem.at[2])
    own_load = pltpu.make_async_copy(far_own_ref, far_ref.at[:, 0], far_sem.at[0])
    rest_load = pltpu.make_async_copy(far_rest_ref, far_ref.at[:, 1:4], far_sem.at[1])
    own_load.start()
    rest_load.start()
    maps_load.start()
    loads = [pltpu.make_async_copy(weight_refs[i], weight_ref.at[i], sem_ref.at[i]) for i in range(16)]
    for load in loads:
        load.start()
    square = jnp.zeros((128, 128), F32)
    own_load.wait()
    maps_load.wait()
    for k in range(4):
        if k == 1:
            rest_load.wait()
        for x in range(4):
            part = far_ref[x, k].astype(F32)
            part = part * part
            for i in range(4):
                square = square + part[:, i * 128 : (i + 1) * 128]
    square = jnp.sum(square, axis=1, keepdims=True)
    scale = lax.rsqrt(square / D + NORM_EPSILON)
    scale_ref[...] = jnp.broadcast_to(scale, (128, 128))
    own_ref[...] = (mixed_ref[...] * scale * gain_ref[rank_ref[0]]).astype(BF16)

    node = lax.broadcasted_iota(jnp.int32, (NODES, 1), 0)
    for part in range(8):
        loads[part].wait()
        loads[part + 8].wait()
        total = jnp.zeros((128, 512), F32)
        for i in range(2):
            p = source_ref[part * 2 + i]
            back = lax.rem(rank_ref[0] // 4 + 4 - p // 4, 4)
            block = far_ref[lax.rem(p, 4), back].astype(F32) * scale_ref[:, 0:1] * gain_ref[p]
            prev = prev_ref[:, pl.ds(pl.multiple_of(p * 512, 512), 512)].astype(F32)
            block = jnp.concatenate(
                [
                    jnp.where(node == NODES - 1, prev[r : r + 1], block[r * NODES : (r + 1) * NODES])
                    for r in range(4)
                ],
                axis=0,
            ).astype(BF16)
            total = total + dot(block[:, :256], weight_ref[part, i], ((1,), (0,)))
            total = total + dot(block[:, 256:], weight_ref[part + 8, i], ((1,), (0,)))
        if part == 0:
            ahead_ref[...] = total
        else:
            ahead_ref[...] += total

    row, lane = same_request()
    accepted = []
    for r in range(4):
        part = slice(r * NODES, (r + 1) * NODES)
        path = jnp.where(lane[part] == leaf_ref[r] + r * NODES, maps_ref[part].astype(F32), 0.0)
        path = jnp.sum(path, axis=1, keepdims=True)
        accepted.append((1.0 + 3.0 * path) * (0.5 + len_ref[r].astype(F32) / CACHE))
    weights = jnp.concatenate(accepted, axis=0)
    pick = maps_ref[128:256].astype(F32)
    predicted = dot(pick, ahead_ref[...], ((0,), (0,)), precision=lax.Precision.HIGHEST)
    error = predicted - own_ref[...].astype(F32)
    weighted = weights * error
    joined = dot(pick, weighted, ((1,), (0,)), precision=lax.Precision.HIGHEST)
    scale = jnp.where(row[:, 0:1] % NODES == NODES - 1, 1.0, scale_ref[:, 0:1])
    err_ref[...] = (joined * scale).astype(BF16)
    loss = jnp.sum(jnp.sum(weighted * error, axis=0, keepdims=True), axis=1, keepdims=True)
    loss_ref[...] = jnp.broadcast_to(loss, (8, 128))


def differentiate_kernel(place_ref, column_ref, e0_ref, e1_ref, e2_ref, e3_ref, loss_ref, grad_ref, pair_ref):
    for part, err_ref in enumerate((e0_ref, e1_ref, e2_ref, e3_ref)):
        first = (part // 2) * 8 + part % 2
        left = jnp.concatenate([column_ref[place_ref[first + 2 * i]] for i in range(4)], axis=0)
        right = jnp.concatenate([err_ref[i] for i in range(4)], axis=0)
        term = dot(left, right, ((0,), (0,)))
        if part == 0:
            grad_ref[...] = term
        else:
            grad_ref[...] += term
    value = grad_ref[...]
    square = jnp.sum(jnp.sum(value * value, axis=0, keepdims=True), axis=1, keepdims=True)
    lane = lax.broadcasted_iota(jnp.int32, (8, 128), 1)
    pair = jnp.where(lane == 0, square, jnp.where(lane == 1, loss_ref[...], 0.0))
    for i in range(32):
        pair_ref[i * 8 : (i + 1) * 8] = pair


def update_kernel(
    pair_ref, grad_ref, weight_ref, first_ref, second_ref,
    new_weight_ref, new_first_ref, new_second_ref, loss_ref,
):
    total = jnp.sum(pair_ref[...], axis=0, keepdims=True)
    norm = jnp.sqrt(total[:, 0:1]) + 1e-06
    clipped = grad_ref[...] * jnp.minimum(1.0, D / norm)
    new_first = BETA_ONE * first_ref[...] + (1.0 - BETA_ONE) * clipped
    new_second = BETA_TWO * second_ref[...] + (1.0 - BETA_TWO) * clipped * clipped
    direction = new_first / CORRECT_ONE / (jnp.sqrt(new_second / CORRECT_TWO) + 1e-08)
    new_first_ref[...] = new_first
    new_second_ref[...] = new_second
    new_weight_ref[...] = (weight_ref[...].astype(F32) - LEARN_RATE * direction).astype(BF16)
    lane = lax.broadcasted_iota(jnp.int32, (1, 128), 1)
    loss_ref[0, 0] = jnp.sum(jnp.where(lane == 1, total, 0.0)) * (0.5 / (128 * N_REQ * D))


def in_vmem():
    return pl.BlockSpec(memory_space=pltpu.VMEM)


def in_smem():
    return pl.BlockSpec(memory_space=pltpu.SMEM)


def attend(rank, lengths, parents, queries, cache_keys, cache_values, tree_keys, tree_values):
    return pl.pallas_call(
        attend_kernel,
        out_shape=(
            jax.ShapeDtypeStruct((N_TP, 144, 2 * HEAD), BF16),
            jax.ShapeDtypeStruct((256, 128), BF16),
        ),
        grid=(4,),
        in_specs=[
            in_smem(),
            in_smem(),
            pl.BlockSpec((4, NODES), lambda r: (0, 0)),
            pl.BlockSpec((1, NODES, HEADS * HEAD), lambda r: (r, 0, 0)),
        ]
        + [pl.BlockSpec((1, 256, KV_HEADS * HEAD), lambda r: (r, 0, 0))] * 2
        + [pl.BlockSpec((1, 2, KV_HEADS * HEAD), lambda r: (r, 0, 0))] * 2,
        out_specs=(
            pl.BlockSpec((N_TP, 144, 2 * HEAD), lambda r: (0, 0, 0)),
            pl.BlockSpec((256, 128), lambda r: (0, 0)),
        ),
        scratch_shapes=[pltpu.VMEM((128, 128), F32)],
        cost_estimate=pl.CostEstimate(
            flops=2 * 2 * 16 * 256 * 256 * 128, bytes_accessed=4 << 20, transcendentals=16 * 256 * 256
        ),
        name="attend",
    )(rank, lengths, parents, queries, cache_keys, cache_values, tree_keys, tree_values)


def project(parcel, out_weight):
    return pl.pallas_call(
        project_kernel,
        grid=(4,),
        out_shape=jax.ShapeDtypeStruct((4, 4, 128, 512), BF16),
        in_specs=[
            pl.BlockSpec((N_TP, 144, 2 * HEAD), lambda p: (0, 0, 0)),
            pl.BlockSpec((2 * HEAD, 2048), lambda p: (0, p)),
        ],
        out_specs=pl.BlockSpec((4, 1, 128, 512), lambda p: (0, p, 0, 0)),
        scratch_shapes=[pltpu.VMEM((128, 2 * HEAD), BF16)],
        cost_estimate=pl.CostEstimate(
            flops=2 * 128 * 256 * 8192, bytes_accessed=7 << 20, transcendentals=0
        ),
        name="project",
    )(parcel, out_weight)


def fold(rank, along):
    return pl.pallas_call(
        fold_kernel,
        out_shape=(jax.ShapeDtypeStruct((128, 512), BF16),) * 4,
        in_specs=[in_smem(), in_vmem()],
        out_specs=(in_vmem(),) * 4,
        cost_estimate=pl.CostEstimate(
            flops=16 * 128 * 512, bytes_accessed=5 << 19, transcendentals=0
        ),
        name="fold",
    )(rank, along)


def settle(rank, terms, residual, gain, prev):
    whole = pl.BlockSpec((128, 512), lambda p, at: (0, 0))
    return pl.pallas_call(
        settle_kernel,
        grid_spec=pltpu.PrefetchScalarGridSpec(
            num_scalar_prefetch=1,
            grid=(1,),
            in_specs=[whole] * 5
            + [
                pl.BlockSpec((1, 1, 512), lambda p, at: (at[0], 0, 0)),
                pl.BlockSpec((4, 512), lambda p, at: (0, at[0])),
            ],
            out_specs=[
                whole,
                whole,
                pl.BlockSpec((4, 128, 512), lambda p, at: (0, 0, 0)),
                whole,
            ],
        ),
        out_shape=(
            jax.ShapeDtypeStruct((128, 512), F32),
            jax.ShapeDtypeStruct((128, 512), BF16),
            jax.ShapeDtypeStruct((4, 128, 512), BF16),
            jax.ShapeDtypeStruct((128, 512), BF16),
        ),
        cost_estimate=pl.CostEstimate(
            flops=128 * 512 * 8, bytes_accessed=2 << 20, transcendentals=0
        ),
        name="settle",
    )(rank, *terms, residual, gain, prev)


def predict(source, rank, lengths, leaf, far_own, far, mixed, gain, prev, maps, all_weight):
    return pl.pallas_call(
        predict_kernel,
        out_shape=(
            jax.ShapeDtypeStruct((128, 512), BF16),
            jax.ShapeDtypeStruct((128, 512), BF16),
            jax.ShapeDtypeStruct((8, 128), F32),
        ),
        in_specs=[in_smem()] * 4
        + [pl.BlockSpec(memory_space=pl.ANY)] * 2
        + [in_vmem()] * 3
        + [pl.BlockSpec(memory_space=pl.ANY)] * 17,
        out_specs=(in_vmem(),) * 3,
        scratch_shapes=[
            pltpu.VMEM((128, 128), F32),
            pltpu.VMEM((128, 512), F32),
            pltpu.VMEM((16, 2, 256, 512), BF16),
            pltpu.SemaphoreType.DMA((16,)),
            pltpu.VMEM((4, 4, 128, 512), BF16),
            pltpu.SemaphoreType.DMA((3,)),
            pltpu.VMEM((256, 128), BF16),
        ],
        compiler_params=pltpu.CompilerParams(vmem_limit_bytes=32 << 20),
        cost_estimate=pl.CostEstimate(
            flops=2 * 128 * 8192 * 512, bytes_accessed=13 << 20, transcendentals=0
        ),
        name="predict",
    )(source, rank, lengths, leaf, far_own, far, mixed, gain, prev, maps, *all_weight)


def differentiate(place, columns, errors, loss):
    return pl.pallas_call(
        differentiate_kernel,
        out_shape=(
            jax.ShapeDtypeStruct((512, 512), F32),
            jax.ShapeDtypeStruct((N_REQ * N_TP, 128), F32),
        ),
        in_specs=[in_smem()] + [in_vmem()] * 6,
        out_specs=(in_vmem(), in_vmem()),
        cost_estimate=pl.CostEstimate(
            flops=2 * 2048 * 512 * 512, bytes_accessed=5 << 20, transcendentals=0
        ),
        name="differentiate",
    )(place, columns, *errors, loss)


def update(pair, gradient, weight, first, second):
    part = pl.BlockSpec((128, 512), lambda p: (p, 0))
    return pl.pallas_call(
        update_kernel,
        grid=(4,),
        out_shape=(
            jax.ShapeDtypeStruct((512, 512), BF16),
            jax.ShapeDtypeStruct((512, 512), F32),
            jax.ShapeDtypeStruct((512, 512), F32),
            jax.ShapeDtypeStruct((1, 1), F32),
        ),
        in_specs=[pl.BlockSpec((N_REQ * N_TP, 128), lambda p: (0, 0))] + [part] * 4,
        out_specs=(part, part, part, in_smem()),
        cost_estimate=pl.CostEstimate(
            flops=20 * 512 * 512, bytes_accessed=6 << 20, transcendentals=512 * 512
        ),
        name="update",
    )(pair, gradient, weight, first, second)


def body(
    queries,
    cache_keys,
    cache_values,
    tree_keys,
    tree_values,
    parents,
    lengths,
    accepted_leaf,
    residual,
    norm_gain,
    out_weight,
    prev_feature,
    draft_weight,
    first_moment,
    second_moment,
):
    requests = queries.shape[0]
    rows = requests * NODES
    tp_rank = lax.axis_index(TP)
    rank = tp_rank.reshape(1)
    block = residual.shape[2]
    gain = norm_gain.reshape(N_TP, 1, block)
    zh, y, c = lax.axis_index("zh"), lax.axis_index("y"), lax.axis_index("c")
    piece = jnp.arange(N_REQ, dtype=jnp.int32)
    source = (
        ((zh + piece % 2) % 2) * 8 + ((y + 4 - (piece // 2) % 4) % 4) * 2 + (c + piece // 8) % 2
    )
    place = (source % 4) * 4 + (lax.axis_index("zl") + 4 - source // 4) % 4

    parcel, maps = attend(
        rank, lengths, parents, queries, cache_keys, cache_values, tree_keys, tree_values
    )
    parcel = exchange(parcel, TP)
    half = draft_weight.shape[0] // 2
    parcel, upper, lower = lax.optimization_barrier(
        (parcel, draft_weight[:half], draft_weight[half:])
    )
    upper = passed(upper, "zh", 2)
    lower = passed(lower, "zh", 2)
    upper = jnp.stack(upper)
    upper = passed(upper, "y", 4)

    partial_value = project(parcel, out_weight)
    along_x = exchange(partial_value, "x")
    other_upper = [lax.ppermute(part, "c", turn(2, 1)) for part in upper]
    lower = jnp.stack(lower)
    lower = passed(lower, "y", 4)
    terms = list(fold(rank, along_x))
    terms[1:] = [lax.ppermute(terms[step], "zl", turn(4, step)) for step in (1, 2, 3)]
    mixed, near, wide, table = settle(rank, terms, residual.reshape(rows, block), gain, prev_feature)

    far = passed(near, "zl", 4)[1:]
    far_own = exchange(wide, "x")
    far = jnp.stack(far)
    far = jnp.broadcast_to(far[None], (4, 3, rows, block)).reshape(12, rows, block)
    far = exchange(far, "x").reshape(4, 3, rows, block)
    swapped = lax.ppermute(
        table, REQ + TP, [(i * N_TP + j, j * N_TP + i) for i in range(16) for j in range(16)]
    )
    other_lower = [lax.ppermute(part, "c", turn(2, 1)) for part in lower]
    columns = passed(swapped, "zl", 4)
    columns = jnp.stack(columns)
    columns = jnp.broadcast_to(columns[None], (4, 4, rows, block)).reshape(16, rows, block)
    columns = exchange(columns, "x")
    own_features, scaled_err, loss = predict(
        source,
        rank,
        lengths,
        accepted_leaf,
        far_own,
        far,
        mixed,
        gain,
        prev_feature,
        maps,
        upper + other_upper + lower + other_lower,
    )
    far_err = lax.ppermute(scaled_err, "zh", turn(2, 1))
    err = passed(scaled_err, "y", 4)
    far_err = passed(far_err, "y", 4)
    err, far_err = jnp.stack(err), jnp.stack(far_err)
    errors = [err, far_err] + [lax.ppermute(part, "c", turn(2, 1)) for part in (err, far_err)]
    gradient, pair = differentiate(place, columns, errors, loss)
    pair = exchange(pair, REQ + TP)
    new_weight, new_first, new_second, draft_loss = update(
        pair, gradient, draft_weight, first_moment, second_moment
    )
    return (
        own_features.reshape(requests, NODES, block),
        new_weight,
        new_first,
        new_second,
        draft_loss.reshape(()),
    )


def solution(mesh):
    fine = Mesh(mesh.devices.reshape(2, 4, 2, 4, 4), REQ + TP)
    placed = (
        P(REQ, None, None),
        P(REQ, TP, None),
        P(REQ, TP, None),
        P(REQ, TP, None),
        P(REQ, TP, None),
        P(REQ, None),
        P(REQ),
        P(REQ),
        P(REQ, None, TP),
        P(),
        P(TP, None),
        P(REQ, None),
        P(REQ, TP),
        P(REQ, TP),
        P(REQ, TP),
    )

    return jax.shard_map(
        body,
        mesh=fine,
        in_specs=placed,
        out_specs=(P(REQ, None, TP), P(REQ, TP), P(REQ, TP), P(REQ, TP), P()),
        check_vma=False,
    )
```
